32 devices in a mesh: lon: 8 (over z, y), lat: 4 (over x, core).
Axes of the slice: x: 2, y: 2, z: 4, core: 2. Of those that a mesh axis runs over, the one named last changes fastest.
Arguments:
- velocity: bfloat16 [3, 75, 128, 2048], P(None, None, 'lat', 'lon'), may hold values from -1.5 to 1.5
- offsets: float32 [3, 4, 6144], P(None, 'lat', 'lon'), may hold values from 0 to 1
- cells: int32 [3, 4, 6144], P(None, 'lat', 'lon'), may hold values from 0 to 255, as said below
- counts: int32 [4, 8], P('lat', 'lon'), may hold values from 192 to 576, as said below
- moves: int32 [4, 6144], P('lat', 'lon'), may hold values from 0 to 4, as said below
Outputs:
- new_offsets: float32 [3, 4, 6144], P(None, 'lat', 'lon')
- new_cells: int32 [3, 4, 6144], P(None, 'lat', 'lon')
- new_counts: int32 [4, 8], P('lat', 'lon')
The draws below stay inside these ranges and needn't reach their ends.
Inputs may be any that keep to these rules, and one draw needn't show every extreme that they name: `cells`: values from 0 to 255, 31 and 73 for i, j, k. A valid slot with move 1 has i = 255, move 2 i = 0, move 3 j = 31, move 4 j = 0. `counts`: between 192 and 576; the upper bound is reached by some tile in every draw. `moves`: invalid slots have 0. In each tile at most 48 valid particles have each nonzero move, and in every draw some tile has exactly 48 for each move. Tiles of row 0 have no move 4.
All inputs are finite; a program needn't handle non-finite values.
Results may differ from the reference program's by a relative error of at most 0.00093.
Values may be sent and summed in bfloat16 or wider, within the bound.
No kernel may reach another device: no remote copies, remote signals or barrier semaphores. Data moves between devices by JAX's collectives and lax.ppermute only.
A program may use at most 64 MiB of HBM per device.

```python
import jax
import jax.numpy as jnp
from jax import lax

KZ = 75
CX = 256
CY = 32
P_SIZE = 768
NX = 2048
NY = 128
N_LON = 8
N_LAT = 4


def particle_plan(key):
    tiles = N_LAT * N_LON
    limit = P_SIZE // 16
    live = jax.random.randint(jax.random.fold_in(key, 101), (tiles,), 4 * limit, P_SIZE - 4 * limit + 1)
    live = live.at[jax.random.randint(jax.random.fold_in(key, 102), (), 0, tiles)].set(P_SIZE - 4 * limit)
    movers = jax.random.randint(jax.random.fold_in(key, 103), (tiles, 4), 0, limit + 1)
    lat_of = jnp.arange(tiles, dtype=jnp.int32) // N_LON
    movers = movers.at[:, 3].set(jnp.where(lat_of == 0, 0, movers[:, 3]))
    for code in range(3):
        chosen = jax.random.randint(jax.random.fold_in(key, 110 + code), (), 0, tiles)
        movers = movers.at[chosen, code].set(limit)
    southern = N_LON + jax.random.randint(jax.random.fold_in(key, 114), (), 0, tiles - N_LON)
    movers = movers.at[southern, 3].set(limit)
    tile_keys = jax.random.split(jax.random.fold_in(key, 104), tiles)
    order = jax.vmap(lambda single: jax.random.permutation(single, P_SIZE))(tile_keys).astype(jnp.int32)
    slot = jnp.arange(P_SIZE, dtype=jnp.int32)
    valid = slot[None, :] < live[:, None]

    def ranking(pair):
        keys, alive = pair
        return jnp.sum((alive[None, :] & (keys[None, :] < keys[:, None])).astype(jnp.int32), axis=1)
    rank = lax.map(ranking, (order, valid))
    bounds = jnp.cumsum(movers, axis=1)
    motion = jnp.where(rank < bounds[:, 0:1], 1, jnp.where(rank < bounds[:, 1:2], 2, jnp.where(rank < bounds[:, 2:3], 3, jnp.where(rank < bounds[:, 3:4], 4, 0))))
    motion = jnp.where(valid, motion, 0).astype(jnp.int32)
    col_i = jax.random.randint(jax.random.fold_in(key, 105), (tiles, P_SIZE), 0, CX)
    row_j = jax.random.randint(jax.random.fold_in(key, 106), (tiles, P_SIZE), 0, CY)
    lev_k = jax.random.randint(jax.random.fold_in(key, 107), (tiles, P_SIZE), 0, KZ - 1)
    col_i = jnp.where(motion == 1, CX - 1, jnp.where(motion == 2, 0, col_i))
    row_j = jnp.where(motion == 3, CY - 1, jnp.where(motion == 4, 0, row_j))
    cellpos = jnp.stack([col_i, row_j, lev_k]).astype(jnp.int32).reshape(3, N_LAT, N_LON * P_SIZE)
    return (live.astype(jnp.int32).reshape(N_LAT, N_LON), motion.reshape(N_LAT, N_LON * P_SIZE), cellpos)


def draw_cells(key, part):
    return particle_plan(key)[2]


def draw_counts(key, part):
    return particle_plan(key)[0]


def draw_moves(key, part):
    return particle_plan(key)[1]


def steps_of(own_key, dims, pieces, least, top_value):
    gain, own = 1.0, jax.random.fold_in(own_key, 6)
    for dim, shards_of in pieces:
        steps = jnp.exp(jax.random.uniform(jax.random.fold_in(own, dim), (shards_of,), jnp.float32, least / len(pieces), top_value / len(pieces)))
        gain = gain * jnp.repeat(steps, dims[dim] // shards_of).reshape([-1 if axis == dim else 1 for axis in range(len(dims))])
    return gain


def scatter_about(stream_key, shape, spread, most, pieces=(), kind=jnp.bfloat16):
    array = jax.random.normal(stream_key, shape, jnp.float32) * spread
    if len(pieces) > 0:
        array = steps_of(stream_key, shape, pieces, -0.22, 0.18) * array
    return jnp.clip(array, min=-most, max=most).astype(kind)


def setup_inputs(seed: int = 0) -> dict:
    streams_of = jax.random.split(jax.random.key(seed), 6)
    velocity = scatter_about(streams_of[0], (3, KZ, NY, NX), 0.3, 1.5, ((2, 4), (3, 8)))
    offsets = jnp.clip(1.0 * jax.random.uniform(streams_of[1], (3, N_LAT, N_LON * P_SIZE), jnp.float32) ** steps_of(streams_of[1], (3, N_LAT, N_LON * P_SIZE), ((1, 4), (2, 8)), -0.2, 0.2), 0.0, 1.0)
    cells = draw_cells(jax.random.fold_in(streams_of[5], 71), 0)
    counts = draw_counts(jax.random.fold_in(streams_of[5], 71), 0)
    moves = draw_moves(jax.random.fold_in(streams_of[5], 71), 0)
    return dict(velocity=velocity, offsets=offsets, cells=cells, counts=counts, moves=moves)


def fetch(velocity, level, row, column):
    inside = velocity[:, level, jnp.minimum(row, NY - 1), column % NX].astype(jnp.float32)
    mirrored = -velocity[:, level, NY - 1, (NX - column) % NX].astype(jnp.float32)
    return jnp.where(row == NY, mirrored, inside)


def rounded(value):
    half = lax.optimization_barrier(value.astype(jnp.bfloat16))
    return half.astype(jnp.float32)


def sample(velocity, position, grow, gcol, level):
    a, b, c = position[0], position[1], position[2]
    weights = [rounded((1.0 - b) * (1.0 - c)), rounded(b * (1.0 - c)), rounded((1.0 - b) * c), rounded(b * c)]
    corners = [(0, 0), (0, 1), (1, 0), (1, 1)]
    sums = []
    for shift in range(2):
        total = jnp.zeros((3,) + a.shape, jnp.float32)
        for weight, (dk, dj) in zip(weights, corners):
            total = total + weight * fetch(velocity, level + dk, grow + dj, gcol + shift)
        sums.append(total)
    return (1.0 - a) * sums[0] + a * sums[1]


def reference(velocity, offsets, cells, counts, moves):
    tiles = N_LAT * N_LON
    position = offsets.reshape(3, N_LAT, N_LON, P_SIZE)
    cellpos = cells.reshape(3, N_LAT, N_LON, P_SIZE)
    motion = moves.reshape(N_LAT, N_LON, P_SIZE)
    lat_id = jnp.arange(N_LAT, dtype=jnp.int32)[:, None, None]
    lon_id = jnp.arange(N_LON, dtype=jnp.int32)[None, :, None]
    gcol = lon_id * CX + cellpos[0]
    grow = lat_id * CY + cellpos[1]
    level = cellpos[2]
    first = sample(velocity, position, grow, gcol, level)
    middle = position + 0.5 * first
    moved = position + sample(velocity, middle, grow, gcol, level)
    na, nb, nc = moved[0], moved[1], moved[2]
    top = lat_id == N_LAT - 1
    slot = jnp.arange(P_SIZE, dtype=jnp.int32)[None, None, :]
    valid = slot < counts[:, :, None]
    fold = (motion == 3) & top
    new_a = jnp.where(motion == 1, na - 1.0, jnp.where(motion == 2, na + 1.0, jnp.where(fold, 1.0 - na, na)))
    new_b = jnp.where(motion == 3, jnp.where(top, 2.0 - nb, nb - 1.0), jnp.where(motion == 4, nb + 1.0, nb))
    new_i = jnp.where(motion == 1, 0, jnp.where(motion == 2, CX - 1, jnp.where(fold, CX - 1 - cellpos[0], cellpos[0])))
    new_j = jnp.where(motion == 3, jnp.where(top, CY - 1, 0), jnp.where(motion == 4, CY - 1, cellpos[1]))
    rank = jnp.zeros((N_LAT, N_LON, P_SIZE), jnp.int32)
    tallies = []
    for code in range(5):
        chosen = (valid & (motion == code)).astype(jnp.int32)
        rank = rank + jnp.where(motion == code, jnp.cumsum(chosen, axis=2) - chosen, 0)
        tallies.append(jnp.sum(chosen, axis=2))
    zero_row = jnp.zeros((1, N_LON), jnp.int32)
    top_rows = (jnp.arange(N_LAT, dtype=jnp.int32) == N_LAT - 1)[:, None]
    groups = jnp.stack([
        tallies[0],
        jnp.roll(tallies[1], 1, axis=1),
        jnp.roll(tallies[2], -1, axis=1),
        jnp.concatenate([zero_row, tallies[3][:-1]], axis=0),
        jnp.concatenate([tallies[4][1:], zero_row], axis=0),
        jnp.where(top_rows, tallies[3][:, ::-1], 0),
    ], axis=-1)
    bases = jnp.cumsum(groups, axis=-1) - groups
    new_counts = jnp.sum(groups, axis=-1).astype(jnp.int32)
    group = jnp.where(motion == 0, 0, jnp.where(motion == 1, 1, jnp.where(motion == 2, 2, jnp.where(motion == 4, 4, jnp.where(top, 5, 3)))))
    dest_lat = lat_id + jnp.where((motion == 3) & (~top), 1, 0) - jnp.where(motion == 4, 1, 0)
    dest_lon = (lon_id + jnp.where(motion == 1, 1, 0) - jnp.where(motion == 2, 1, 0)) % N_LON
    dest_lon = jnp.where(fold, N_LON - 1 - lon_id, dest_lon)
    dest_lat = jnp.clip(dest_lat, 0, N_LAT - 1).astype(jnp.int32)
    dest_lon = dest_lon.astype(jnp.int32)
    place = bases[dest_lat, dest_lon, group] + rank
    target = jnp.where(valid, (dest_lat * N_LON + dest_lon) * P_SIZE + place, tiles * P_SIZE).reshape(-1)
    floats = jnp.stack([new_a, new_b, nc]).reshape(3, -1)
    ints = jnp.stack([new_i, new_j, level]).astype(jnp.int32).reshape(3, -1)
    out_float = jnp.zeros((3, tiles * P_SIZE + 1), jnp.float32).at[:, target].set(floats)
    out_int = jnp.zeros((3, tiles * P_SIZE + 1), jnp.int32).at[:, target].set(ints)
    new_offsets = out_float[:, :tiles * P_SIZE].reshape(3, N_LAT, N_LON * P_SIZE)
    new_cells = out_int[:, :tiles * P_SIZE].reshape(3, N_LAT, N_LON * P_SIZE)
    return new_offsets, new_cells, new_counts
```

```python
import functools

import jax
import jax.numpy as jnp
from jax import lax
from jax.experimental import pallas as pl
from jax.experimental.pallas import tpu as pltpu
from jax.sharding import PartitionSpec as P

CAP = 48
LANES = 128
HALF = 64
REC = 16
F32, BF16, I32 = jnp.float32, jnp.bfloat16, jnp.int32
VMEM = pl.BlockSpec(memory_space=pltpu.VMEM)
SMEM = pl.BlockSpec(memory_space=pltpu.SMEM)
ANY = pl.BlockSpec(memory_space=pl.ANY)
BIG = pltpu.CompilerParams(vmem_limit_bytes=56 << 20)


def up8(n):
    return (n + 7) // 8 * 8


def iota(shape, dim):
    return lax.broadcasted_iota(I32, shape, dim)


def nt(a, b):
    return lax.dot_general(a, b, (((1,), (1,)), ((), ())), preferred_element_type=F32)


def pieces(value):
    high = value.astype(BF16).astype(F32)
    rest = value - high
    middle = rest.astype(BF16).astype(F32)
    return [high, middle, rest - middle]


def decode(x):
    return [x[0:1] + x[1:2] + x[2:3], x[3:4] + x[4:5] + x[5:6], x[6:7] + x[7:8] + x[8:9]]


def pack_kernel(
    vel, off, cel, counts, moves, q1, q2, lonrec, stay, number, low, high, strips, recs, sems
):
    depth, rows = vel.shape[1], vel.shape[2]
    tiles = vel.shape[3] // LANES
    slots = off.shape[2]
    stride = 3 * depth + 8
    stride += 1 - stride % 2
    planes = up8(3 * depth)
    copies = []
    for comp in range(3):
        copies.append(
            pltpu.make_async_copy(vel.at[comp, :, pl.ds(0, 8), :], low.at[comp], sems.at[0, comp])
        )
        copies.append(
            pltpu.make_async_copy(
                vel.at[comp, :, pl.ds(rows - 8, 8), :], high.at[comp], sems.at[1, comp]
            )
        )
    for copy in copies:
        copy.start()
    live = counts[0, 0]
    rows_of = []
    for d in range(3):
        rows_of += pieces(off[d])
    for d in range(3):
        rows_of.append(cel[d].astype(F32))
    rows_of.append(jnp.ones((1, slots), F32))
    for n, row in enumerate(rows_of):
        recs[n : n + 1, :] = row
    recs[len(rows_of) :, :] = jnp.zeros((REC - len(rows_of), slots), F32)
    record = recs[...].astype(BF16)
    chosen = (moves[...] == iota((8, slots), 0)) & (iota((8, slots), 1) < live)
    ones = chosen.astype(F32)
    scan_of = jnp.where(
        (iota((LANES, 2 * LANES), 0) < iota((LANES, 2 * LANES), 1))
        | (iota((LANES, 2 * LANES), 1) >= LANES),
        1.0,
        0.0,
    ).astype(BF16)
    carry = jnp.zeros((8, LANES), F32)
    ranks = []
    for block in range(slots // LANES):
        piece = ones[:, block * LANES : (block + 1) * LANES].astype(BF16)
        scanned = jnp.dot(piece, scan_of, preferred_element_type=F32)
        ranks.append(scanned[:, :LANES] + carry)
        carry = carry + scanned[:, LANES:]
    rank = jnp.where(chosen, jnp.concatenate(ranks, axis=1), -1.0).astype(I32)
    target = iota((HALF, slots), 0)
    placing = [
        jnp.where(rank[g : g + 1] == target, 1.0, 0.0).astype(BF16) for g in range(1, 5)
    ]
    lonrec[...] = nt(record, jnp.concatenate(placing[:2], axis=0)).astype(BF16)
    latrec = nt(record, jnp.concatenate(placing[2:], axis=0)).astype(BF16)
    target = iota((LANES, slots), 0)
    for block in range(slots // LANES):
        where = jnp.where(rank[0:1] - block * LANES == target, 1.0, 0.0).astype(BF16)
        out = nt(record, where)
        lanes = slice(block * LANES, (block + 1) * LANES)
        for d, row in enumerate(decode(out)):
            stay[d : d + 1, lanes] = row
        stay[3:6, lanes] = out[9:12]
        stay[6:8, lanes] = out[12:14]
    number[0] = jnp.max(carry[0:1, :]).astype(I32)
    for copy in copies:
        copy.wait()
    for comp in range(3):

        def spread(k, _):
            for source, buffer in enumerate((low, high)):
                value = buffer[comp, k].astype(F32)
                for tile in range(tiles):
                    first = (source * tiles + tile) * 8 * stride + 3 * k + comp
                    strips[pl.ds(first, 8, stride=stride), :] = value[
                        :, tile * LANES : (tile + 1) * LANES
                    ]
            return 0

        lax.fori_loop(0, depth, spread, 0, unroll=5)
    odd = lax.rem(lax.axis_index("lat"), 2)
    for n, out in enumerate((q1, q2)):
        upper = odd if n == 0 else 1 - odd
        for tile in range(tiles):
            last = ((tiles + tile) * 8 + 7) * stride
            for line in range(2):
                first = jnp.where(upper == 1, (tile * 8 + line) * stride, last)
                at = (line * tiles + tile) * planes
                out[at : at + planes, :] = strips[pl.ds(first, planes), :].astype(BF16)
        out[2 * tiles * planes :, :] = latrec


def column_kernel(vel, first, last, vbuf, sel, lines, left, right, sems):
    depth, rows, cols = vel.shape[1:]
    planes = up8(3 * depth)
    for comp in range(3):
        pltpu.make_async_copy(vel.at[comp], vbuf.at[comp, pl.ds(0, depth)], sems.at[comp]).start()
    r, c = iota((REC, cols), 0), iota((REC, cols), 1)
    pick = ((r == c) & (r < 2)) | ((r == 2) & (c == cols - 1))
    select = jnp.where(pick, 1.0, 0.0).astype(BF16)
    per = LANES // rows
    chunks = vbuf.shape[1] // per
    deep = up8(chunks)
    lane = iota((deep, LANES), 1)
    for comp in range(3):
        pltpu.make_async_copy(vel.at[comp], vbuf.at[comp, pl.ds(0, depth)], sems.at[comp]).wait()
        got = nt(select, vbuf[comp].reshape(vbuf.shape[1] * rows, cols))
        for n in range(3):
            for q in range(chunks):
                lines[n * deep + q : n * deep + q + 1, :] = got[
                    n : n + 1, q * LANES : (q + 1) * LANES
                ]
        for m in range(per):
            zero = lines[0:deep, :]
            one = lines[deep : 2 * deep, :]
            end = lines[2 * deep : 3 * deep, :]
            zero = pltpu.roll(zero, (LANES - rows * m) % LANES, 1)
            one = pltpu.roll(one, (LANES + HALF - rows * m) % LANES, 1)
            end = pltpu.roll(end, (LANES - rows * m) % LANES, 1)
            both = jnp.where(lane < HALF, zero, one)
            for q in range(0, deep, 8):
                at = pl.ds(3 * (per * q + m) + comp, 8, stride=3 * per)
                left[at, :] = both[q : q + 8]
                right[at, :] = end[q : q + 8]
    first[...] = left[0:planes, :]
    last[...] = right[0:planes, :]


def gather_kernel(
    vel, stay, number, got, listed, found, vbuf, table, idxv, idxs, seams, sems, isem
):
    depth, rows, cols = vel.shape[1:]
    slots = stay.shape[1]
    tiles = cols // LANES
    stride = 3 * depth + 8
    stride += 1 - stride % 2
    for comp in range(3):
        pltpu.make_async_copy(vel.at[comp], vbuf.at[comp], sems.at[comp]).start()
    i, j, k = (stay[n : n + 1, :].astype(I32) for n in (3, 4, 5))
    slot = iota((1, slots), 1)
    e = jnp.minimum(i + 1, cols - 1)
    idxv[0:1, :] = ((i // LANES) * rows + j) * stride + 3 * k
    idxv[1:2, :] = (slot - i) & (LANES - 1)
    odd_one = (((i & (LANES - 1)) == LANES - 1) | (j == rows - 1)) & (slot < number[0])
    idxv[2:3, :] = odd_one.astype(I32)
    idxv[3:4, :] = ((e // LANES) * rows + j) * stride + 3 * k
    idxv[4:5, :] = (slot - e) & (LANES - 1)
    idxv[5:6, :] = ((i == cols - 1) | (j == rows - 1)).astype(I32)
    copy = pltpu.make_async_copy(idxv, idxs, isem)
    copy.start()
    for comp in range(3):
        pltpu.make_async_copy(vel.at[comp], vbuf.at[comp], sems.at[comp]).wait()

        def fill(k, _):
            value = vbuf[comp, k].astype(F32)
            for tile in range(tiles):
                for r in range(0, rows, 8):
                    at = pl.ds((tile * rows + r) * stride + 3 * k + comp, 8, stride=stride)
                    table[at, :] = value[r : r + 8, tile * LANES : (tile + 1) * LANES]
            return 0

        lax.fori_loop(0, depth, fill, 0, unroll=5)
    copy.wait()
    lane = iota((8, LANES), 1)
    count = number[0]

    def block_of(b, found_before):
        def eight(g, carry):
            *acc, n = carry
            for u in range(8):
                p = g * 8 + u
                s = b * LANES + p
                row = idxs[0, s]
                shift = idxs[1, s]
                low = pltpu.roll(table[pl.ds(row, 8), :], shift, 1)
                high = pltpu.roll(table[pl.ds(row + stride, 8), :], shift, 1)
                here = lane == p
                beside = lane == ((p + 1) & (LANES - 1))
                acc = [
                    jnp.where(here, low, acc[0]),
                    jnp.where(beside, low, acc[1]),
                    jnp.where(here, high, acc[2]),
                    jnp.where(beside, high, acc[3]),
                ]
                seams[n] = s
                n = n + idxs[2, s]
            return (*acc, n)

        groups = jnp.minimum((count - b * LANES + 7) // 8, LANES // 8)
        zero = jnp.zeros((8, LANES), F32)
        *acc, n = lax.fori_loop(0, groups, eight, (zero, zero, zero, zero, found_before))
        got[0, b] = acc[0]
        got[1, b] = pltpu.roll(acc[1], LANES - 1, 1)
        got[2, b] = acc[2]
        got[3, b] = pltpu.roll(acc[3], LANES - 1, 1)
        return n

    total = lax.fori_loop(0, (count + LANES - 1) // LANES, block_of, I32(0))

    def fix(n, edges):
        s = seams[n]
        row = idxs[3, s]
        shift = idxs[4, s]
        mask = lane == (s & (LANES - 1))
        for q, place in ((1, row), (3, row + stride)):
            value = pltpu.roll(table[pl.ds(place, 8), :], shift, 1)
            pltpu.store(got.at[q, s // LANES], value, mask=mask)
        listed[edges] = s
        return edges + idxs[5, s]

    found[0] = lax.fori_loop(0, total, fix, I32(0))


def side_kernel(first, last, lonrec, q1r, q2r, p1, p2):
    planes = first.shape[0]
    even_lat = lax.rem(lax.axis_index("lat"), 2) == 0
    odd_lon = lax.rem(lax.axis_index("lon"), 2)
    lane = iota((planes, LANES), 1)

    def strip(north, n):
        a = q1r[n * planes : (n + 1) * planes, :].astype(F32)
        b = q2r[n * planes : (n + 1) * planes, :].astype(F32)
        return jnp.where(even_lat == north, a, b)

    north0, north1, second0 = strip(True, 0), strip(True, 1), strip(True, 2)
    south0 = strip(False, 0)
    west = first[...]
    west = jnp.where(lane == 32, pltpu.roll(north0, 32, 1), west)
    west = jnp.where(lane == 33, pltpu.roll(second0, 33, 1), west)
    west = jnp.where(lane == 34, pltpu.roll(south0, 34, 1), west)
    west = jnp.where(lane == 35, pltpu.roll(north1, 36, 1), west)
    west = jnp.where(lane == 96, pltpu.roll(north0, 95, 1), west).astype(BF16)
    east = last[...]
    east = jnp.where(lane == 32, pltpu.roll(north1, 33, 1), east)
    east = jnp.where((lane == 33) | (lane == 34), pltpu.roll(north0, 33, 1), east).astype(BF16)
    p1[0:planes, :] = jnp.where(odd_lon == 1, west, east)
    p2[0:planes, :] = jnp.where(odd_lon == 1, east, west)
    p1[planes:, :] = lonrec[...]
    p2[planes:, :] = lonrec[...]


def final_kernel(
    rows, cols, lat_size,
    stay, number, got, listed, found, first, last, q1, q2, q1r, q2r, p1r, p2r,
    new_off, new_cel, new_count, table, values_of, recs, idxv, idxs, isem,
):
    planes = first.shape[0]
    slots = stay.shape[1]
    values_of[...] = got[...]
    lat = lax.axis_index("lat")
    even_lat = lax.rem(lat, 2) == 0
    even_lon = lax.rem(lax.axis_index("lon"), 2) == 0
    top = lat == lat_size - 1
    both = 4 * planes

    def pick(flag, a, b, at, size):
        x = a[at : at + size, :].astype(F32)
        y = b[at : at + size, :].astype(F32)
        return jnp.where(flag, x, y)

    def put(n, value):
        table[n * planes : (n + 1) * planes, :] = value

    for t in range(2):
        at = t * planes
        put(t, pick(even_lat, q2, q1, at, planes))
        put(2 + t, pick(even_lat, q1, q2, at, planes))
        put(4 + t, pick(even_lat, q1r, q2r, at, planes))
        put(6 + t, pick(even_lat, q1r, q2r, at + 2 * planes, planes))
        put(8 + t, pick(even_lat, q2r, q1r, at, planes))
    put(10, first[...])
    put(11, last[...])
    put(12, pick(even_lon, p1r, p2r, 0, planes))
    put(13, pick(even_lon, p2r, p1r, 0, planes))
    lane = iota((8, LANES), 1)
    inside = iota((REC, LANES), 1) < HALF
    wrec = pick(even_lon, p2r, p1r, planes, REC)
    erec = pltpu.roll(pick(even_lon, p1r, p2r, planes, REC), HALF, 1)
    srec = pick(even_lat, q2r, q1r, both, REC)
    nrec = pick(even_lat, q1r, q2r, both, REC)
    nrec = jnp.where(top, nrec, pltpu.roll(nrec, HALF, 1))
    base = number[0]
    slot = iota((1, slots), 1)
    own = slot < base
    for n in range(8):
        recs[n : n + 1, :] = jnp.where(own, stay[n : n + 1, :], 0.0)
    group = jnp.zeros((1, slots), I32)
    stay_count = base
    for g, raw in enumerate((wrec, erec, srec, nrec)):
        raw = jnp.where(inside, raw, 0.0)
        count = jnp.sum(raw[12:13]).astype(I32)
        moved = pltpu.roll(raw, base & (LANES - 1), 1)
        values = decode(moved) + [moved[9:10], moved[10:11], moved[11:12]]
        mine = (slot >= base) & (slot < base + count)
        for b in range(slots // LANES):
            at = slice(b * LANES, (b + 1) * LANES)
            for n, row in enumerate(values):
                recs[n : n + 1, at] = jnp.where(mine[:, at], row, recs[n : n + 1, at])
        group = jnp.where(mine, g + 1, group)
        base = base + count
    fold = (group == 4) & top
    new_count[0, 0] = base
    i, j, k = (recs[n : n + 1, :].astype(I32) for n in (3, 4, 5))
    y0 = jnp.where(group == 3, -1, jnp.where((group == 4), rows, j))
    x0 = jnp.where(group == 1, -1, jnp.where(group == 2, cols, i))
    signs = []
    for n, (dj, di) in enumerate(((0, 0), (0, 1), (1, 0), (1, 1))):
        y = y0 + dj
        x = x0 + di

        def flat(strip, at):
            return strip * (planes * LANES) + at

        def row_at(strip, at):
            return flat(strip + at // LANES, at & (LANES - 1))

        inner = jnp.where(
            x < 0,
            flat(13, y),
            jnp.where(
                x == cols,
                flat(12, y),
                jnp.where(
                    x > cols,
                    flat(12, HALF + y),
                    jnp.where(
                        x == cols - 1,
                        flat(11, y),
                        jnp.where(x == 0, flat(10, y), row_at(jnp.where(y == 0, 0, 2), x)),
                    ),
                ),
            ),
        )
        north = jnp.where(
            x < 0,
            flat(13, 32),
            jnp.where(x == cols, flat(12, 32), jnp.where(x > cols, flat(12, 96), row_at(4, x))),
        )
        u = cols - x
        folded = jnp.where(
            u < 0,
            flat(12, 35),
            jnp.where(u == cols, flat(13, 33), jnp.where(u > cols, flat(13, 34), row_at(4, u))),
        )
        second = jnp.where(x == cols, flat(12, 33), row_at(6, x))
        south = jnp.where(x == cols, flat(12, 34), row_at(8, x))
        where = jnp.where(
            y < 0,
            south,
            jnp.where(y > rows, second, jnp.where(y == rows, jnp.where(top, folded, north), inner)),
        )
        if dj == 0:
            across = jnp.where(x == cols, flat(13, 33), row_at(4, x))
            signs.append(jnp.ones((1, slots), F32))
        else:
            across = jnp.where(u == cols, flat(12, rows - 1), row_at(2, u))
            signs.append(jnp.where(fold | (top & (y == rows)), -1.0, 1.0))
        where = jnp.where(fold, across, where)
        idxv[n : n + 1, :] = where + 3 * LANES * k
    copy = pltpu.make_async_copy(idxv, idxs, isem)
    copy.start()
    copy.wait()

    def patch(s):
        mask = lane == (s & (LANES - 1))
        values = []
        for q in range(4):
            e = idxs[q, s]
            values.append(pltpu.roll(table[pl.ds(e // LANES, 8), :], (s - e) & (LANES - 1), 1))
        for q in range(4):
            pltpu.store(values_of.at[q, s // LANES], values[q], mask=mask)

    def patch_listed(n, _):
        patch(listed[n])
        return 0

    lax.fori_loop(0, found[0], patch_listed, 0)

    def patch_arrived(n, _):
        patch(n)
        return 0

    lax.fori_loop(stay_count, base, patch_arrived, 0)
    below = iota((8, LANES), 0) < 3
    for b in range(slots // LANES):
        at = slice(b * LANES, (b + 1) * LANES)
        corner = [values_of[n, b] * signs[n][:, at] for n in range(4)]
        position = recs[0:3, at]

        def rounded(value):
            return value.astype(BF16).astype(F32)

        def sample(pos):
            pa, pb, pc = pos[0:1], pos[1:2], pos[2:3]
            near = jnp.where(below, rounded((1.0 - pb) * (1.0 - pc)), rounded((1.0 - pb) * pc))
            far = jnp.where(below, rounded(pb * (1.0 - pc)), rounded(pb * pc))
            left = near * corner[0] + far * corner[2]
            right = near * corner[1] + far * corner[3]
            mixed = (1.0 - pa) * left + pa * right
            return mixed[0:3] + mixed[3:6]

        middle = position + 0.5 * sample(position)
        moved = position + sample(middle)
        na, nb, nc = moved[0:1], moved[1:2], moved[2:3]
        g = group[:, at]
        f = fold[:, at]
        filled = slot[:, at] < base
        na = jnp.where(g == 1, na - 1.0, jnp.where(g == 2, na + 1.0, jnp.where(f, 1.0 - na, na)))
        north_b = jnp.where(f, 2.0 - nb, nb + 1.0)
        nb = jnp.where(g == 3, nb - 1.0, jnp.where(g == 4, north_b, nb))
        new_off[0, :, at] = jnp.where(filled, na, 0.0)
        new_off[1, :, at] = jnp.where(filled, nb, 0.0)
        new_off[2, :, at] = jnp.where(filled, nc, 0.0)
        ci, cj = i[:, at], j[:, at]
        ci = jnp.where(
            g == 1, 0, jnp.where(g == 2, cols - 1, jnp.where(f, cols - 1 - ci, ci))
        )
        cj = jnp.where(g == 3, 0, jnp.where(g == 4, rows - 1, cj))
        new_cel[0, :, at] = jnp.where(filled, ci, 0)
        new_cel[1, :, at] = jnp.where(filled, cj, 0)
        new_cel[2, :, at] = jnp.where(filled, k[:, at], 0)


def route(lon_size, lat_size, partner):
    pairs = []
    for p in range(lon_size):
        for r in range(lat_size):
            other = partner(p, r)
            if other is not None:
                pairs.append((p * lat_size + r, other[0] * lat_size + other[1]))
    return pairs


def shards(velocity, offsets, cells, counts, moves):
    depth, rows, cols = velocity.shape[1:]
    slots = offsets.shape[2]
    lon_size, lat_size = lax.axis_size("lon"), lax.axis_size("lat")
    axes = ("lon", "lat")
    planes = up8(3 * depth)
    stride = 3 * depth + 8
    stride += 1 - stride % 2
    tiles = cols // LANES
    high = 2 * tiles * planes + REC

    def send(x, partner):
        return lax.ppermute(x, axes, route(lon_size, lat_size, partner))

    def array(shape, dtype):
        return jax.ShapeDtypeStruct(shape, dtype)

    q1, q2, lonrec, stay, number = pl.pallas_call(
        pack_kernel,
        out_shape=(
            array((high, LANES), BF16),
            array((high, LANES), BF16),
            array((REC, LANES), BF16),
            array((8, slots), F32),
            array((1,), I32),
        ),
        in_specs=[ANY, VMEM, VMEM, SMEM, VMEM],
        out_specs=(VMEM, VMEM, VMEM, VMEM, SMEM),
        scratch_shapes=[
            pltpu.VMEM((3, depth, 8, cols), BF16),
            pltpu.VMEM((3, depth, 8, cols), BF16),
            pltpu.VMEM((2 * tiles * 8 * stride, LANES), F32),
            pltpu.VMEM((REC, slots), F32),
            pltpu.SemaphoreType.DMA((2, 3)),
        ],
        compiler_params=BIG,
        name="pack",
    )(velocity, offsets, cells, counts, moves)

    q1r = send(q1, lambda p, r: (p, r ^ 1))

    def second(p, r):
        if r == lat_size - 1:
            return (lon_size - 1 - p, r)
        return None if r == 0 else (p, ((r + 1) ^ 1) - 1)

    q2r = send(q2, second)
    per = LANES // rows
    padded = (depth + per - 1) // per * per
    chunks = padded // per
    tall = 3 * (per * (up8(chunks) - 1) + per - 1) + 3
    first, last = pl.pallas_call(
        column_kernel,
        out_shape=(array((planes, LANES), F32), array((planes, LANES), F32)),
        in_specs=[ANY],
        out_specs=(VMEM, VMEM),
        scratch_shapes=[
            pltpu.VMEM((3, padded, rows, cols), BF16),
            pltpu.VMEM((REC, cols), BF16),
            pltpu.VMEM((3 * up8(chunks), LANES), F32),
            pltpu.VMEM((up8(tall), LANES), F32),
            pltpu.VMEM((up8(tall), LANES), F32),
            pltpu.SemaphoreType.DMA((3,)),
        ],
        compiler_params=BIG,
        cost_estimate=pl.CostEstimate(flops=10**9, bytes_accessed=2 * velocity.size, transcendentals=0),
        name="columns",
    )(velocity)
    p1, p2 = pl.pallas_call(
        side_kernel,
        out_shape=(array((planes + REC, LANES), BF16), array((planes + REC, LANES), BF16)),
        in_specs=[VMEM] * 5,
        out_specs=(VMEM, VMEM),
        compiler_params=BIG,
        name="sides",
    )(first, last, lonrec, q1r, q2r)
    p2r = send(p2, lambda p, r: ((((p + 1) ^ 1) - 1) % lon_size, r))
    p1r = send(p1, lambda p, r: (p ^ 1, r))
    got, listed, found = pl.pallas_call(
        gather_kernel,
        out_shape=(
            array((4, slots // LANES, 8, LANES), F32),
            array((slots + LANES,), I32),
            array((1,), I32),
        ),
        in_specs=[ANY, VMEM, SMEM],
        out_specs=(VMEM, SMEM, SMEM),
        scratch_shapes=[
            pltpu.VMEM((3, depth, rows, cols), BF16),
            pltpu.VMEM(((tiles * rows + 1) * stride + 8, LANES), F32),
            pltpu.VMEM((8, slots), I32),
            pltpu.SMEM((8, slots), I32),
            pltpu.SMEM((slots + LANES,), I32),
            pltpu.SemaphoreType.DMA((3,)),
            pltpu.SemaphoreType.DMA,
        ],
        compiler_params=BIG,
        cost_estimate=pl.CostEstimate(flops=10**9, bytes_accessed=2 * velocity.size, transcendentals=0),
        name="gather",
    )(velocity, stay, number)
    return pl.pallas_call(
        functools.partial(final_kernel, rows, cols, lat_size),
        out_shape=(
            array((3, 1, slots), F32),
            array((3, 1, slots), I32),
            array((1, 1), I32),
        ),
        in_specs=[VMEM, SMEM, VMEM, SMEM, SMEM] + [VMEM] * 8,
        out_specs=(VMEM, VMEM, SMEM),
        scratch_shapes=[
            pltpu.VMEM((14 * planes + 8, LANES), F32),
            pltpu.VMEM((4, slots // LANES, 8, LANES), F32),
            pltpu.VMEM((8, slots), F32),
            pltpu.VMEM((8, slots), I32),
            pltpu.SMEM((8, slots), I32),
            pltpu.SemaphoreType.DMA,
        ],
        compiler_params=BIG,
        name="final",
    )(stay, number, got, listed, found, first, last, q1, q2, q1r, q2r, p1r, p2r)


def solution(mesh):
    placed = (
        P(None, None, "lat", "lon"),
        P(None, "lat", "lon"),
        P(None, "lat", "lon"),
        P("lat", "lon"),
        P("lat", "lon"),
    )
    return jax.shard_map(
        shards,
        mesh=mesh,
        in_specs=placed,
        out_specs=(P(None, "lat", "lon"), P(None, "lat", "lon"), P("lat", "lon")),
        check_vma=False,
    )
```

```python
import functools

import jax
import jax.numpy as jnp
from jax import lax
from jax.experimental import pallas as pl
from jax.experimental.pallas import tpu as pltpu
from jax.sharding import PartitionSpec as P

CAP = 48
LANES = 128
HALF = 64
REC = 16
UNROLL = 16
F32, BF16, I32 = jnp.float32, jnp.bfloat16, jnp.int32
VMEM = pl.BlockSpec(memory_space=pltpu.VMEM)
SMEM = pl.BlockSpec(memory_space=pltpu.SMEM)
HBM = pl.BlockSpec(memory_space=pltpu.HBM)


def room(mib):
    return pltpu.CompilerParams(vmem_limit_bytes=mib << 20)


def up8(n):
    return (n + 7) // 8 * 8


def odd_stride(depth):
    lines = 3 * depth + 8
    return lines + 1 - lines % 2


def iota(shape, dim):
    return lax.broadcasted_iota(I32, shape, dim)


def nt(a, b):
    return lax.dot_general(a, b, (((1,), (1,)), ((), ())), preferred_element_type=F32)


def pieces(value):
    high = value.astype(BF16).astype(F32)
    rest = value - high
    middle = rest.astype(BF16).astype(F32)
    return [high, middle, rest - middle]


def decode(x):
    return [x[0:1] + x[1:2] + x[2:3], x[3:4] + x[4:5] + x[5:6], x[6:7] + x[7:8] + x[8:9]]


def pack_kernel(
    vel, off, cel, counts, moves, q1, q2, lonrec, record, rank0, number,
    low, high, offv, celv, movev, strips, recs, sems, small,
):
    depth, rows = vel.shape[1], vel.shape[2]
    tiles = vel.shape[3] // LANES
    slots = off.shape[2]
    stride = odd_stride(depth)
    planes = up8(3 * depth)
    inputs = [
        pltpu.make_async_copy(source, target, small.at[n])
        for n, (source, target) in enumerate(((off, offv), (cel, celv), (moves, movev)))
    ]
    for copy in inputs:
        copy.start()
    copies = []
    for comp in range(3):
        copies.append(
            pltpu.make_async_copy(vel.at[comp, :, pl.ds(0, 8), :], low.at[comp], sems.at[0, comp])
        )
        copies.append(
            pltpu.make_async_copy(
                vel.at[comp, :, pl.ds(rows - 8, 8), :], high.at[comp], sems.at[1, comp]
            )
        )
    for copy in copies:
        copy.start()
    for copy in inputs:
        copy.wait()
    live = counts[0, 0]
    rows_of = []
    for d in range(3):
        rows_of += pieces(offv[d])
    for d in range(3):
        rows_of.append(celv[d].astype(F32))
    rows_of.append(jnp.ones((1, slots), F32))
    for n, row in enumerate(rows_of):
        recs[n : n + 1, :] = row
    recs[len(rows_of) :, :] = jnp.zeros((REC - len(rows_of), slots), F32)
    packed = recs[...].astype(BF16)
    record[...] = packed
    chosen = (movev[...] == iota((8, slots), 0)) & (iota((8, slots), 1) < live)
    ones = chosen.astype(F32)
    scan_of = jnp.where(
        (iota((LANES, 2 * LANES), 0) < iota((LANES, 2 * LANES), 1))
        | (iota((LANES, 2 * LANES), 1) >= LANES),
        1.0,
        0.0,
    ).astype(BF16)
    carry = jnp.zeros((8, LANES), F32)
    ranks = []
    for block in range(slots // LANES):
        piece = ones[:, block * LANES : (block + 1) * LANES].astype(BF16)
        scanned = jnp.dot(piece, scan_of, preferred_element_type=F32)
        ranks.append(scanned[:, :LANES] + carry)
        carry = carry + scanned[:, LANES:]
    rank = jnp.where(chosen, jnp.concatenate(ranks, axis=1), -1.0).astype(I32)
    rank0[...] = rank[0:1]
    target = iota((HALF, slots), 0)
    placing = [
        jnp.where(rank[g : g + 1] == target, 1.0, 0.0).astype(BF16) for g in range(1, 5)
    ]
    lonrec[...] = nt(packed, jnp.concatenate(placing[:2], axis=0)).astype(BF16)
    latrec = nt(packed, jnp.concatenate(placing[2:], axis=0)).astype(BF16)
    number[0] = jnp.max(carry[0:1, :]).astype(I32)
    for comp in range(3):
        copies[2 * comp].wait()
        copies[2 * comp + 1].wait()

        def spread(k, _):
            for source, buffer in enumerate((low, high)):
                value = buffer[comp, k].astype(F32)
                for tile in range(tiles):
                    first = (source * tiles + tile) * 8 * stride + 3 * k + comp
                    strips[pl.ds(first, 8, stride=stride), :] = value[
                        :, tile * LANES : (tile + 1) * LANES
                    ]
            return 0

        lax.fori_loop(0, depth, spread, 0, unroll=15)
    odd = lax.rem(lax.axis_index("lat"), 2)
    for n, out in enumerate((q1, q2)):
        upper = odd if n == 0 else 1 - odd
        for tile in range(tiles):
            last = ((tiles + tile) * 8 + 7) * stride
            for line in range(2):
                first = jnp.where(upper == 1, (tile * 8 + line) * stride, last)
                at = (line * tiles + tile) * planes
                out[at : at + planes, :] = strips[pl.ds(first, planes), :].astype(BF16)
        out[2 * tiles * planes :, :] = latrec


def table_kernel(
    vel_hbm, record, rank0, number, first, last, seam, table, stay, index, vel, lines, wide, sems
):
    depth, rows, cols = vel.shape[1:]
    copies = [pltpu.make_async_copy(vel_hbm.at[c], vel.at[c], sems.at[c]) for c in range(3)]
    for copy in copies:
        copy.start()
    slots = record.shape[1]
    tiles = cols // LANES
    planes = up8(3 * depth)
    stride = odd_stride(depth)
    r, c = iota((REC, cols), 0), iota((REC, cols), 1)
    pick = (r == c) & (r < 2)
    pick = pick | ((r == 2) & (c == cols - 1)) | ((r == c - LANES + 4) & (r >= 3) & (r < 5))
    select = jnp.where(pick, 1.0, 0.0).astype(BF16)
    per = LANES // rows
    chunks = -(-depth // per)
    deep = up8(chunks)
    lane = iota((deep, LANES), 1)
    target = iota((LANES, slots), 0)
    packed = record[...]
    rank = rank0[...]
    for block in range(slots // LANES):
        where = jnp.where(rank - block * LANES == target, 1.0, 0.0).astype(BF16)
        out = nt(packed, where)
        lanes = slice(block * LANES, (block + 1) * LANES)
        for d, row in enumerate(decode(out)):
            stay[d : d + 1, lanes] = row
        stay[3:6, lanes] = out[9:12]
        stay[6:8, lanes] = out[12:14]
    i, j, k = (stay[n : n + 1, :].astype(I32) for n in (3, 4, 5))
    slot = iota((1, slots), 1)
    index[0:1, :] = ((i // LANES) * rows + j) * stride + 3 * k
    index[1:2, :] = (slot - i) & (LANES - 1)
    odd_one = (((i & (LANES - 1)) == LANES - 1) | (j == rows - 1)) & (slot < number[0])
    index[2:3, :] = odd_one.astype(I32)
    for comp in range(3):
        copies[comp].wait()
        got = nt(select, vel[comp].reshape(depth * rows, cols))
        for n in range(5):
            for q in range(chunks):
                size = min(LANES, depth * rows - q * LANES)
                lines[n * deep + q : n * deep + q + 1, 0:size] = got[
                    n : n + 1, q * LANES : q * LANES + size
                ]
        for m in range(per):

            def line(n, to):
                at = lines[n * deep : (n + 1) * deep, :]
                return pltpu.roll(at, (LANES + to - rows * m) % LANES, 1)

            values = (
                jnp.where(lane < HALF, line(0, 0), line(1, HALF)),
                line(2, 0),
                jnp.where(lane < HALF, line(3, 0), line(4, HALF)),
            )
            for n, value in enumerate(values):
                for q in range(0, deep, 8):
                    at = pl.ds(n * wide.shape[0] // 3 + 3 * (per * q + m) + comp, 8, stride=3 * per)
                    wide[at, :] = value[q : q + 8]
        def fill(k, _):
            value = vel[comp, k].astype(F32)
            for tile in range(tiles):
                for r in range(0, rows, 8):
                    at = pl.ds((tile * rows + r) * stride + 3 * k + comp, 8, stride=stride)
                    table[at, :] = value[r : r + 8, tile * LANES : (tile + 1) * LANES]
            return 0

        lax.fori_loop(0, depth, fill, 0, unroll=5)
    for n, out in enumerate((first, last, seam)):
        at = n * wide.shape[0] // 3
        out[...] = wide[at : at + planes, :]


def gather_kernel(stride, table, index, number, got, listed, found):
    lane = iota((8, LANES), 1)
    count = number[0]

    def block_of(b, n):
        acc = [jnp.zeros((8, LANES), F32)] * 4
        for p in range(LANES):
            s = b * LANES + p
            row = index[0, s]
            shift = index[1, s]
            low = pltpu.roll(table[pl.ds(row, 8), :], shift, 1)
            high = pltpu.roll(table[pl.ds(row + stride, 8), :], shift, 1)
            here = lane == p
            beside = lane == ((p + 1) % LANES)
            acc = [
                jnp.where(here, low, acc[0]),
                jnp.where(beside, low, acc[1]),
                jnp.where(here, high, acc[2]),
                jnp.where(beside, high, acc[3]),
            ]
            listed[n] = s
            n = n + index[2, s]
        got[0, b] = acc[0]
        got[1, b] = pltpu.roll(acc[1], LANES - 1, 1)
        got[2, b] = acc[2]
        got[3, b] = pltpu.roll(acc[3], LANES - 1, 1)
        return n

    found[0] = lax.fori_loop(0, (count + LANES - 1) // LANES, block_of, I32(0))


def side_kernel(first, last, lonrec, q1r, q2r, p1, p2):
    planes = first.shape[0]
    even_lat = lax.rem(lax.axis_index("lat"), 2) == 0
    odd_lon = lax.rem(lax.axis_index("lon"), 2)
    lane = iota((planes, LANES), 1)

    def strip(north, n):
        a = q1r[n * planes : (n + 1) * planes, :].astype(F32)
        b = q2r[n * planes : (n + 1) * planes, :].astype(F32)
        return jnp.where(even_lat == north, a, b)

    north0, north1, second0 = strip(True, 0), strip(True, 1), strip(True, 2)
    south0 = strip(False, 0)
    west = first[...]
    west = jnp.where(lane == 32, pltpu.roll(north0, 32, 1), west)
    west = jnp.where(lane == 33, pltpu.roll(second0, 33, 1), west)
    west = jnp.where(lane == 34, pltpu.roll(south0, 34, 1), west)
    west = jnp.where(lane == 35, pltpu.roll(north1, 36, 1), west)
    west = jnp.where(lane == 96, pltpu.roll(north0, 95, 1), west).astype(BF16)
    east = last[...]
    east = jnp.where(lane == 32, pltpu.roll(north1, 33, 1), east)
    east = jnp.where((lane == 33) | (lane == 34), pltpu.roll(north0, 33, 1), east).astype(BF16)
    p1[0:planes, :] = jnp.where(odd_lon == 1, west, east)
    p2[0:planes, :] = jnp.where(odd_lon == 1, east, west)
    p1[planes:, :] = lonrec[...]
    p2[planes:, :] = lonrec[...]


def final_kernel(
    rows, cols, lat_size,
    stay, number, got, listed, found, first, last, seam, q1, q2, q1r, q2r, p1r, p2r,
    new_off, new_cel, new_count, table, values_of, recs, idxv, idxs, isem,
):
    planes = first.shape[0]
    slots = stay.shape[1]
    values_of[...] = got[...]
    lat = lax.axis_index("lat")
    even_lat = lax.rem(lat, 2) == 0
    even_lon = lax.rem(lax.axis_index("lon"), 2) == 0
    top = lat == lat_size - 1
    both = 4 * planes

    def pick(flag, a, b, at, size):
        return jnp.where(flag, a[at : at + size, :], b[at : at + size, :]).astype(F32)

    def put(n, value):
        table[n * planes : (n + 1) * planes, :] = value

    for t in range(2):
        at = t * planes
        put(t, pick(even_lat, q2, q1, at, planes))
        put(2 + t, pick(even_lat, q1, q2, at, planes))
        put(4 + t, pick(even_lat, q1r, q2r, at, planes))
        put(6 + t, pick(even_lat, q1r, q2r, at + 2 * planes, planes))
        put(8 + t, pick(even_lat, q2r, q1r, at, planes))
    put(10, first[...])
    put(11, last[...])
    put(14, seam[...])
    put(12, pick(even_lon, p1r, p2r, 0, planes))
    put(13, pick(even_lon, p2r, p1r, 0, planes))
    lane = iota((8, LANES), 1)
    inside = iota((REC, LANES), 1) < HALF
    wrec = pick(even_lon, p2r, p1r, planes, REC)
    erec = pltpu.roll(pick(even_lon, p1r, p2r, planes, REC), HALF, 1)
    srec = pick(even_lat, q2r, q1r, both, REC)
    nrec = pick(even_lat, q1r, q2r, both, REC)
    nrec = jnp.where(top, nrec, pltpu.roll(nrec, HALF, 1))
    base = number[0]
    slot = iota((1, slots), 1)
    own = slot < base
    for n in range(8):
        recs[n : n + 1, :] = jnp.where(own, stay[n : n + 1, :], 0.0)
    group = jnp.zeros((1, slots), I32)
    stay_count = base
    for g, raw in enumerate((wrec, erec, srec, nrec)):
        raw = jnp.where(inside, raw, 0.0)
        count = jnp.sum(raw[12:13]).astype(I32)
        moved = pltpu.roll(raw, base & (LANES - 1), 1)
        values = decode(moved) + [moved[9:10], moved[10:11], moved[11:12]]
        mine = (slot >= base) & (slot < base + count)
        for b in range(slots // LANES):
            at = slice(b * LANES, (b + 1) * LANES)
            for n, row in enumerate(values):
                recs[n : n + 1, at] = jnp.where(mine[:, at], row, recs[n : n + 1, at])
        group = jnp.where(mine, g + 1, group)
        base = base + count
    fold = (group == 4) & top
    new_count[0, 0] = base
    i, j, k = (recs[n : n + 1, :].astype(I32) for n in (3, 4, 5))
    y0 = jnp.where(group == 3, -1, jnp.where((group == 4), rows, j))
    x0 = jnp.where(group == 1, -1, jnp.where(group == 2, cols, i))
    signs = []
    for n, (dj, di) in enumerate(((0, 0), (0, 1), (1, 0), (1, 1))):
        y = y0 + dj
        x = x0 + di

        def flat(strip, at):
            return strip * (planes * LANES) + at

        def row_at(strip, at):
            return flat(strip + at // LANES, at & (LANES - 1))

        inner = jnp.where(
            x < 0,
            flat(13, y),
            jnp.where(
                x == cols,
                flat(12, y),
                jnp.where(
                    x > cols,
                    flat(12, HALF + y),
                    jnp.where(
                        x == cols - 1,
                        flat(11, y),
                        jnp.where(
                            x == 0,
                            flat(10, y),
                            jnp.where(
                                x == LANES - 1,
                                flat(14, y),
                                jnp.where(
                                    x == LANES,
                                    flat(14, HALF + y),
                                    row_at(jnp.where(y == 0, 0, 2), x),
                                ),
                            ),
                        ),
                    ),
                ),
            ),
        )
        north = jnp.where(
            x < 0,
            flat(13, 32),
            jnp.where(x == cols, flat(12, 32), jnp.where(x > cols, flat(12, 96), row_at(4, x))),
        )
        u = cols - x
        folded = jnp.where(
            u < 0,
            flat(12, 35),
            jnp.where(u == cols, flat(13, 33), jnp.where(u > cols, flat(13, 34), row_at(4, u))),
        )
        second = jnp.where(x == cols, flat(12, 33), row_at(6, x))
        south = jnp.where(x == cols, flat(12, 34), row_at(8, x))
        where = jnp.where(
            y < 0,
            south,
            jnp.where(y > rows, second, jnp.where(y == rows, jnp.where(top, folded, north), inner)),
        )
        if dj == 0:
            across = jnp.where(x == cols, flat(13, 33), row_at(4, x))
            signs.append(jnp.ones((1, slots), F32))
        else:
            across = jnp.where(u == cols, flat(12, rows - 1), row_at(2, u))
            signs.append(jnp.where(fold | (top & (y == rows)), -1.0, 1.0))
        where = jnp.where(fold, across, where)
        idxv[n : n + 1, :] = where + 3 * LANES * k
    copy = pltpu.make_async_copy(idxv, idxs, isem)
    copy.start()
    copy.wait()

    def patch(chosen):
        values = []
        for s in chosen:
            for q in range(4):
                e = idxs[q, s]
                values.append(pltpu.roll(table[pl.ds(e // LANES, 8), :], (s - e) & (LANES - 1), 1))
        for s in chosen:
            mask = lane == (s & (LANES - 1))
            for q in range(4):
                pltpu.store(values_of.at[q, s // LANES], values.pop(0), mask=mask)

    def patch_listed(n, _):
        patch([listed[jnp.minimum(n * UNROLL + u, found[0] - 1)] for u in range(UNROLL)])
        return 0

    lax.fori_loop(0, (found[0] + UNROLL - 1) // UNROLL, patch_listed, 0)

    def patch_arrived(n, _):
        start = stay_count + n * UNROLL
        patch([jnp.minimum(start + u, slots - 1) for u in range(UNROLL)])
        return 0

    lax.fori_loop(0, (base - stay_count + UNROLL - 1) // UNROLL, patch_arrived, 0)
    below = iota((8, LANES), 0) < 3
    for b in range(slots // LANES):
        at = slice(b * LANES, (b + 1) * LANES)
        corner = [values_of[n, b] * signs[n][:, at] for n in range(4)]
        position = recs[0:3, at]

        def rounded(value):
            return value.astype(BF16).astype(F32)

        def sample(pos):
            pa, pb, pc = pos[0:1], pos[1:2], pos[2:3]
            near = jnp.where(below, rounded((1.0 - pb) * (1.0 - pc)), rounded((1.0 - pb) * pc))
            far = jnp.where(below, rounded(pb * (1.0 - pc)), rounded(pb * pc))
            left = near * corner[0] + far * corner[2]
            right = near * corner[1] + far * corner[3]
            mixed = (1.0 - pa) * left + pa * right
            return mixed[0:3] + mixed[3:6]

        middle = position + 0.5 * sample(position)
        moved = position + sample(middle)
        na, nb, nc = moved[0:1], moved[1:2], moved[2:3]
        g = group[:, at]
        f = fold[:, at]
        filled = slot[:, at] < base
        na = jnp.where(g == 1, na - 1.0, jnp.where(g == 2, na + 1.0, jnp.where(f, 1.0 - na, na)))
        north_b = jnp.where(f, 2.0 - nb, nb + 1.0)
        nb = jnp.where(g == 3, nb - 1.0, jnp.where(g == 4, north_b, nb))
        new_off[0, :, at] = jnp.where(filled, na, 0.0)
        new_off[1, :, at] = jnp.where(filled, nb, 0.0)
        new_off[2, :, at] = jnp.where(filled, nc, 0.0)
        ci, cj = i[:, at], j[:, at]
        ci = jnp.where(
            g == 1, 0, jnp.where(g == 2, cols - 1, jnp.where(f, cols - 1 - ci, ci))
        )
        cj = jnp.where(g == 3, 0, jnp.where(g == 4, rows - 1, cj))
        new_cel[0, :, at] = jnp.where(filled, ci, 0)
        new_cel[1, :, at] = jnp.where(filled, cj, 0)
        new_cel[2, :, at] = jnp.where(filled, k[:, at], 0)


def route(lon_size, lat_size, partner):
    pairs = []
    for p in range(lon_size):
        for r in range(lat_size):
            other = partner(p, r)
            if other is not None:
                pairs.append((p * lat_size + r, other[0] * lat_size + other[1]))
    return pairs


def shards(velocity, offsets, cells, counts, moves):
    depth, rows, cols = velocity.shape[1:]
    slots = offsets.shape[2]
    lon_size, lat_size = lax.axis_size("lon"), lax.axis_size("lat")
    axes = ("lon", "lat")
    planes = up8(3 * depth)
    stride = odd_stride(depth)
    tiles = cols // LANES
    high = 2 * tiles * planes + REC

    def send(x, partner):
        return lax.ppermute(x, axes, route(lon_size, lat_size, partner))

    def array(shape, dtype):
        return jax.ShapeDtypeStruct(shape, dtype)

    q1, q2, lonrec, record, rank0, number = pl.pallas_call(
        pack_kernel,
        out_shape=(
            array((high, LANES), BF16),
            array((high, LANES), BF16),
            array((REC, LANES), BF16),
            array((REC, slots), BF16),
            array((1, slots), I32),
            array((1,), I32),
        ),
        in_specs=[HBM, HBM, HBM, SMEM, HBM],
        out_specs=(VMEM, VMEM, VMEM, VMEM, VMEM, SMEM),
        scratch_shapes=[
            pltpu.VMEM((3, depth, 8, cols), BF16),
            pltpu.VMEM((3, depth, 8, cols), BF16),
            pltpu.VMEM((3, 1, slots), F32),
            pltpu.VMEM((3, 1, slots), I32),
            pltpu.VMEM((1, slots), I32),
            pltpu.VMEM((2 * tiles * 8 * stride, LANES), F32),
            pltpu.VMEM((REC, slots), F32),
            pltpu.SemaphoreType.DMA((2, 3)),
            pltpu.SemaphoreType.DMA((3,)),
        ],
        compiler_params=room(10),
        name="pack",
    )(*(pltpu.with_memory_space_constraint(x, pltpu.HBM) for x in (velocity, offsets, cells)), counts, pltpu.with_memory_space_constraint(moves, pltpu.HBM))

    q1r = send(q1, lambda p, r: (p, r ^ 1))

    def second(p, r):
        if r == lat_size - 1:
            return (lon_size - 1 - p, r)
        return None if r == 0 else (p, ((r + 1) ^ 1) - 1)

    q2r = send(q2, second)
    per = LANES // rows
    deep = up8(-(-depth // per))
    strips = tiles * rows + 1
    first, last, seam, table, stay, index = pl.pallas_call(
        table_kernel,
        out_shape=(
            array((planes, LANES), F32),
            array((planes, LANES), F32),
            array((planes, LANES), F32),
            array((strips * stride + 8, LANES), F32),
            array((8, slots), F32),
            array((3, slots), I32),
        ),
        in_specs=[HBM, VMEM, VMEM, SMEM],
        out_specs=(VMEM,) * 6,
        scratch_shapes=[
            pltpu.VMEM((3, depth, rows, cols), BF16),
            pltpu.VMEM((5 * deep, LANES), F32),
            pltpu.VMEM((9 * up8(per * deep), LANES), F32),
            pltpu.SemaphoreType.DMA((3,)),
        ],
        compiler_params=room(20),
        cost_estimate=pl.CostEstimate(flops=10**9, bytes_accessed=2 * velocity.size, transcendentals=0),
        name="table",
    )(pltpu.with_memory_space_constraint(velocity, pltpu.HBM), record, rank0, number)
    p1, p2 = pl.pallas_call(
        side_kernel,
        out_shape=(array((planes + REC, LANES), BF16), array((planes + REC, LANES), BF16)),
        in_specs=[VMEM] * 5,
        out_specs=(VMEM, VMEM),
        compiler_params=room(5),
        name="sides",
    )(first, last, lonrec, q1r, q2r)
    p2r = send(p2, lambda p, r: ((((p + 1) ^ 1) - 1) % lon_size, r))
    p1r = send(p1, lambda p, r: (p ^ 1, r))
    got, listed, found = pl.pallas_call(
        functools.partial(gather_kernel, stride),
        out_shape=(
            array((4, slots // LANES, 8, LANES), F32),
            array((slots + LANES,), I32),
            array((1,), I32),
        ),
        in_specs=[VMEM, SMEM, SMEM],
        out_specs=(VMEM, SMEM, SMEM),
        compiler_params=room(10),
        cost_estimate=pl.CostEstimate(flops=10**9, bytes_accessed=2 * velocity.size, transcendentals=0),
        name="gather",
    )(table, index, number)
    return pl.pallas_call(
        functools.partial(final_kernel, rows, cols, lat_size),
        out_shape=(
            array((3, 1, slots), F32),
            array((3, 1, slots), I32),
            array((1, 1), I32),
        ),
        in_specs=[VMEM, SMEM, VMEM, SMEM, SMEM] + [VMEM] * 9,
        out_specs=(VMEM, VMEM, SMEM),
        scratch_shapes=[
            pltpu.VMEM((15 * planes + 8, LANES), F32),
            pltpu.VMEM((4, slots // LANES, 8, LANES), F32),
            pltpu.VMEM((8, slots), F32),
            pltpu.VMEM((8, slots), I32),
            pltpu.SMEM((8, slots), I32),
            pltpu.SemaphoreType.DMA,
        ],
        compiler_params=room(8),
        name="final",
    )(stay, number, got, listed, found, first, last, seam, q1, q2, q1r, q2r, p1r, p2r)


def solution(mesh):
    placed = (
        P(None, None, "lat", "lon"),
        P(None, "lat", "lon"),
        P(None, "lat", "lon"),
        P("lat", "lon"),
        P("lat", "lon"),
    )
    return jax.shard_map(
        shards,
        mesh=mesh,
        in_specs=placed,
        out_specs=(P(None, "lat", "lon"), P(None, "lat", "lon"), P("lat", "lon")),
        check_vma=False,
    )
```

```python
import functools

import jax
import jax.numpy as jnp
from jax import lax
from jax.experimental import pallas as pl
from jax.experimental.pallas import tpu as pltpu
from jax.sharding import PartitionSpec as P

CAP = 48
LANES = 128
HALF = 64
REC = 16
UNROLL = 8
SHIFT = 7
F32, BF16, I32 = jnp.float32, jnp.bfloat16, jnp.int32
VMEM = pl.BlockSpec(memory_space=pltpu.VMEM)
SMEM = pl.BlockSpec(memory_space=pltpu.SMEM)
HBM = pl.BlockSpec(memory_space=pltpu.HBM)


def room(mib):
    return pltpu.CompilerParams(vmem_limit_bytes=mib << 20)


def up8(n):
    return (n + 7) // 8 * 8


def odd_stride(depth):
    lines = 3 * depth + 8
    return lines + 1 - lines % 2


def iota(shape, dim):
    return lax.broadcasted_iota(I32, shape, dim)


def nt(a, b):
    return lax.dot_general(a, b, (((1,), (1,)), ((), ())), preferred_element_type=F32)


def pieces(value):
    high = value.astype(BF16).astype(F32)
    rest = value - high
    middle = rest.astype(BF16).astype(F32)
    return [high, middle, rest - middle]


def decode(x):
    return [x[0:1] + x[1:2] + x[2:3], x[3:4] + x[4:5] + x[5:6], x[6:7] + x[7:8] + x[8:9]]


def pack_kernel(
    vel, off, cel, counts, moves, q1, q2, lonrec, record, rank0, total,
    low, high, offv, celv, movev, strips, recs, sems, small,
):
    depth, rows = vel.shape[1], vel.shape[2]
    tiles = vel.shape[3] // LANES
    slots = off.shape[2]
    stride = odd_stride(depth)
    planes = up8(3 * depth)
    inputs = [
        pltpu.make_async_copy(source, target, small.at[n])
        for n, (source, target) in enumerate(((off, offv), (cel, celv), (moves, movev)))
    ]
    for copy in inputs:
        copy.start()
    copies = []
    for comp in range(3):
        copies.append(
            pltpu.make_async_copy(vel.at[comp, :, pl.ds(0, 8), :], low.at[comp], sems.at[0, comp])
        )
        copies.append(
            pltpu.make_async_copy(
                vel.at[comp, :, pl.ds(rows - 8, 8), :], high.at[comp], sems.at[1, comp]
            )
        )
    for copy in copies:
        copy.start()
    for copy in inputs:
        copy.wait()
    live = counts[0, 0]
    rows_of = []
    for d in range(3):
        rows_of += pieces(offv[d])
    for d in range(3):
        rows_of.append(celv[d].astype(F32))
    rows_of.append(jnp.ones((1, slots), F32))
    for n, row in enumerate(rows_of):
        recs[n : n + 1, :] = row
    recs[len(rows_of) :, :] = jnp.zeros((REC - len(rows_of), slots), F32)
    packed = recs[...].astype(BF16)
    record[...] = packed
    chosen = (movev[...] == iota((8, slots), 0)) & (iota((8, slots), 1) < live)
    ones = chosen.astype(F32)
    scan_of = jnp.where(
        (iota((LANES, 2 * LANES), 0) < iota((LANES, 2 * LANES), 1))
        | (iota((LANES, 2 * LANES), 1) >= LANES),
        1.0,
        0.0,
    ).astype(BF16)
    carry = jnp.zeros((8, LANES), F32)
    ranks = []
    for block in range(slots // LANES):
        piece = ones[:, block * LANES : (block + 1) * LANES].astype(BF16)
        scanned = jnp.dot(piece, scan_of, preferred_element_type=F32)
        ranks.append(scanned[:, :LANES] + carry)
        carry = carry + scanned[:, LANES:]
    rank = jnp.where(chosen, jnp.concatenate(ranks, axis=1), -1.0).astype(I32)
    rank0[...] = rank[0:1]
    target = iota((HALF, slots), 0)
    placing = [
        jnp.where(rank[g : g + 1] == target, 1.0, 0.0).astype(BF16) for g in range(1, 5)
    ]
    lonrec[...] = nt(packed, jnp.concatenate(placing[:2], axis=0)).astype(BF16)
    latrec = nt(packed, jnp.concatenate(placing[2:], axis=0)).astype(BF16)
    total[...] = carry[0:1, :].astype(I32)
    for comp in range(3):
        copies[2 * comp].wait()
        copies[2 * comp + 1].wait()

        def spread(k, _):
            for source, buffer in enumerate((low, high)):
                value = buffer[comp, k].astype(F32)
                for tile in range(tiles):
                    first = (source * tiles + tile) * 8 * stride + 3 * k + comp
                    strips[pl.ds(first, 8, stride=stride), :] = value[
                        :, tile * LANES : (tile + 1) * LANES
                    ]
            return 0

        lax.fori_loop(0, depth, spread, 0, unroll=15)
    odd = lax.rem(lax.axis_index("lat"), 2)
    for n, out in enumerate((q1, q2)):
        upper = odd if n == 0 else 1 - odd
        for tile in range(tiles):
            last = ((tiles + tile) * 8 + 7) * stride
            for line in range(2):
                first = jnp.where(upper == 1, (tile * 8 + line) * stride, last)
                at = (line * tiles + tile) * planes
                out[at : at + planes, :] = strips[pl.ds(first, planes), :].astype(BF16)
        out[2 * tiles * planes :, :] = latrec


def table_kernel(
    vel, record, rank0, total, first, last, seam, table, stay, index, lines, wide
):
    depth, rows, cols = vel.shape[1:]
    slots = record.shape[1]
    tiles = cols // LANES
    planes = up8(3 * depth)
    stride = odd_stride(depth)
    r, c = iota((REC, cols), 0), iota((REC, cols), 1)
    pick = (r == c) & (r < 2)
    pick = pick | ((r == 2) & (c == cols - 1)) | ((r == c - LANES + 4) & (r >= 3) & (r < 5))
    select = jnp.where(pick, 1.0, 0.0).astype(BF16)
    per = LANES // rows
    chunks = -(-depth // per)
    deep = up8(chunks)
    lane = iota((deep, LANES), 1)
    target = iota((LANES, slots), 0)
    packed = record[...]
    rank = rank0[...]
    for block in range(slots // LANES):
        where = jnp.where(rank - block * LANES == target, 1.0, 0.0).astype(BF16)
        out = nt(packed, where)
        lanes = slice(block * LANES, (block + 1) * LANES)
        for d, row in enumerate(decode(out)):
            stay[d : d + 1, lanes] = row
        stay[3:6, lanes] = out[9:12]
        stay[6:8, lanes] = out[12:14]
    i, j, k = (stay[n : n + 1, :].astype(I32) for n in (3, 4, 5))
    slot = iota((1, slots), 1)
    index[0:1, :] = ((i >> SHIFT) * rows + j) * stride + 3 * k
    index[1:2, :] = (slot - i) & (LANES - 1)
    odd_one = (((i & (LANES - 1)) == LANES - 1) | (j == rows - 1)) & (slot < jnp.tile(total[...], (1, slots // LANES)))
    index[2:3, :] = odd_one.astype(I32)
    index[3:4, :] = jnp.tile(total[...], (1, slots // LANES))
    for comp in range(3):
        got = nt(select, vel[comp].reshape(depth * rows, cols))
        for n in range(5):
            for q in range(chunks):
                size = min(LANES, depth * rows - q * LANES)
                lines[n * deep + q : n * deep + q + 1, 0:size] = got[
                    n : n + 1, q * LANES : q * LANES + size
                ]
        for m in range(per):

            def line(n, to):
                at = lines[n * deep : (n + 1) * deep, :]
                return pltpu.roll(at, (LANES + to - rows * m) % LANES, 1)

            values = (
                jnp.where(lane < HALF, line(0, 0), line(1, HALF)),
                line(2, 0),
                jnp.where(lane < HALF, line(3, 0), line(4, HALF)),
            )
            for n, value in enumerate(values):
                for q in range(0, deep, 8):
                    at = pl.ds(n * wide.shape[0] // 3 + 3 * (per * q + m) + comp, 8, stride=3 * per)
                    wide[at, :] = value[q : q + 8]
        def fill(k, _):
            value = vel[comp, k].astype(F32)
            for tile in range(tiles):
                for r in range(0, rows, 8):
                    at = pl.ds((tile * rows + r) * stride + 3 * k + comp, 8, stride=stride)
                    table[at, :] = value[r : r + 8, tile * LANES : (tile + 1) * LANES]
            return 0

        lax.fori_loop(0, depth, fill, 0, unroll=5)
    for n, out in enumerate((first, last, seam)):
        at = n * wide.shape[0] // 3
        out[...] = wide[at : at + planes, :]


def gather_kernel(stride, table, index, got, listed):
    lane = iota((8, LANES), 1)
    count = index[3, 0]
    slots = index.shape[1]

    def block_of(b, n):
        acc = [jnp.zeros((8, LANES), F32)] * 4
        for p in range(LANES):
            s = b * LANES + p
            row = index[0, s]
            shift = index[1, s]
            low = pltpu.roll(table[pl.ds(row, 8), :], shift, 1)
            high = pltpu.roll(table[pl.ds(row + stride, 8), :], shift, 1)
            here = lane == p
            beside = lane == ((p + 1) % LANES)
            acc = [
                jnp.where(here, low, acc[0]),
                jnp.where(beside, low, acc[1]),
                jnp.where(here, high, acc[2]),
                jnp.where(beside, high, acc[3]),
            ]
            listed[n] = s
            n = n + index[2, s]
        got[0, b] = acc[0]
        got[1, b] = pltpu.roll(acc[1], LANES - 1, 1)
        got[2, b] = acc[2]
        got[3, b] = pltpu.roll(acc[3], LANES - 1, 1)
        return n

    listed[slots + 8] = lax.fori_loop(0, (count + LANES - 1) >> SHIFT, block_of, I32(0))
    listed[slots + 9] = count


def side_kernel(first, last, lonrec, q1r, q2r, p1, p2):
    planes = first.shape[0]
    even_lat = lax.rem(lax.axis_index("lat"), 2) == 0
    odd_lon = lax.rem(lax.axis_index("lon"), 2)
    lane = iota((planes, LANES), 1)

    def strip(north, n):
        a = q1r[n * planes : (n + 1) * planes, :].astype(F32)
        b = q2r[n * planes : (n + 1) * planes, :].astype(F32)
        return jnp.where(even_lat == north, a, b)

    north0, north1, second0 = strip(True, 0), strip(True, 1), strip(True, 2)
    south0 = strip(False, 0)
    west = first[...]
    west = jnp.where(lane == 32, pltpu.roll(north0, 32, 1), west)
    west = jnp.where(lane == 33, pltpu.roll(second0, 33, 1), west)
    west = jnp.where(lane == 34, pltpu.roll(south0, 34, 1), west)
    west = jnp.where(lane == 35, pltpu.roll(north1, 36, 1), west)
    west = jnp.where(lane == 96, pltpu.roll(north0, 95, 1), west).astype(BF16)
    east = last[...]
    east = jnp.where(lane == 32, pltpu.roll(north1, 33, 1), east)
    east = jnp.where((lane == 33) | (lane == 34), pltpu.roll(north0, 33, 1), east).astype(BF16)
    p1[0:planes, :] = jnp.where(odd_lon == 1, west, east)
    p2[0:planes, :] = jnp.where(odd_lon == 1, east, west)
    p1[planes:, :] = lonrec[...]
    p2[planes:, :] = lonrec[...]


def places(rows, cols, planes, group, top, y0, x0, k):
    fold = (group == 4) & top
    found, signs = [], []

    def flat(strip, at):
        return strip * (planes * LANES) + at

    def row_at(strip, at):
        return flat(strip + (at >> SHIFT), at & (LANES - 1))

    for dj, di in ((0, 0), (0, 1), (1, 0), (1, 1)):
        y = y0 + dj
        x = x0 + di
        inner = row_at(jnp.where(y == 0, 0, 2), x)
        inner = jnp.where(x == LANES - 1, flat(14, y), inner)
        inner = jnp.where(x == LANES, flat(14, HALF + y), inner)
        inner = jnp.where(x == 0, flat(10, y), inner)
        inner = jnp.where(x == cols - 1, flat(11, y), inner)
        inner = jnp.where(x > cols, flat(12, HALF + y), inner)
        inner = jnp.where(x == cols, flat(12, y), inner)
        inner = jnp.where(x < 0, flat(13, y), inner)
        north = jnp.where(
            x < 0,
            flat(13, 32),
            jnp.where(x == cols, flat(12, 32), jnp.where(x > cols, flat(12, 96), row_at(4, x))),
        )
        u = cols - x
        folded = jnp.where(
            u < 0,
            flat(12, 35),
            jnp.where(u == cols, flat(13, 33), jnp.where(u > cols, flat(13, 34), row_at(4, u))),
        )
        second = jnp.where(x == cols, flat(12, 33), row_at(6, x))
        south = jnp.where(x == cols, flat(12, 34), row_at(8, x))
        where = jnp.where(
            y < 0,
            south,
            jnp.where(y > rows, second, jnp.where(y == rows, jnp.where(top, folded, north), inner)),
        )
        if dj == 0:
            across = jnp.where(x == cols, flat(13, 33), row_at(4, x))
            signs.append(jnp.ones(x0.shape, F32))
        else:
            across = jnp.where(u == cols, flat(12, rows - 1), row_at(2, u))
            signs.append(jnp.where(top & (fold | (y == rows)), -1.0, 1.0))
        found.append(jnp.where(fold, across, where) + 3 * LANES * k)
    return found, signs


def final_kernel(
    rows, cols, lat_size,
    stay, got, listed_any, first, last, seam, q1, q2, q1r, q2r, p1r, p2r,
    new_off, new_cel, new_count,
    table, values_of, packed, idxv, idxs, idxlv, idxl, listed, isem,
):
    planes = first.shape[0]
    slots = stay.shape[1]
    lat = lax.axis_index("lat")
    even_lat = lax.rem(lat, 2) == 0
    even_lon = lax.rem(lax.axis_index("lon"), 2) == 0
    top = lat == lat_size - 1
    both = 4 * planes

    def pick(flag, a, b, at, size):
        return jnp.where(flag, a[at : at + size, :], b[at : at + size, :]).astype(F32)

    slot = iota((1, slots), 1)
    copy_list = pltpu.make_async_copy(listed_any, listed, isem.at[2])
    copy_list.start()
    blocks = [slice(b * LANES, (b + 1) * LANES) for b in range(slots // LANES)]
    packed[...] = jnp.zeros(packed.shape, F32)
    for n in range(3):
        for b, at in enumerate(blocks):
            packed[8 * n + b : 8 * n + b + 1, :] = stay[3 + n : 4 + n, at]
    here = [packed[8 * n : 8 * n + 8, :].astype(I32) for n in range(3)]
    e, stay_signs = places(
        rows, cols, planes, jnp.zeros((8, LANES), I32), top, here[1], here[0], here[2]
    )
    for q in range(4):
        idxlv[8 * q : 8 * q + 8, :] = e[q]
    copy_listed = pltpu.make_async_copy(idxlv, idxl, isem.at[0])
    copy_listed.start()
    inside = iota((REC, LANES), 1) < HALF
    wrec = pick(even_lon, p2r, p1r, planes, REC)
    erec = pltpu.roll(pick(even_lon, p1r, p2r, planes, REC), HALF, 1)
    srec = pick(even_lat, q2r, q1r, both, REC)
    nrec = pick(even_lat, q1r, q2r, both, REC)
    nrec = jnp.where(top, nrec, pltpu.roll(nrec, HALF, 1))
    groups = []
    for g, raw in enumerate((wrec, erec, srec, nrec)):
        raw = jnp.where(inside, raw, 0.0)
        count = jnp.sum(raw[12:13]).astype(I32)
        i, j, k = (raw[n : n + 1].astype(I32) for n in (9, 10, 11))
        y0 = (j, j, jnp.full_like(j, -1), jnp.full_like(j, rows))[g]
        x0 = (jnp.full_like(i, -1), jnp.full_like(i, cols), i, i)[g]
        e, signs = places(rows, cols, planes, jnp.full_like(i, g + 1), top, y0, x0, k)
        for q in range(4):
            row = 4 * g + q
            idxv[row : row + 1, :] = e[q]
        groups.append((raw, count, signs))
    copy = pltpu.make_async_copy(idxv, idxs, isem.at[1])
    copy.start()
    values_of[...] = got[...]

    def put(n, value):
        table[n * planes : (n + 1) * planes, :] = value

    for t in range(2):
        at = t * planes
        put(t, pick(even_lat, q2, q1, at, planes))
        put(2 + t, pick(even_lat, q1, q2, at, planes))
        put(4 + t, pick(even_lat, q1r, q2r, at, planes))
        put(6 + t, pick(even_lat, q1r, q2r, at + 2 * planes, planes))
        put(8 + t, pick(even_lat, q2r, q1r, at, planes))
    put(10, first[...])
    put(11, last[...])
    put(12, pick(even_lon, p1r, p2r, 0, planes))
    put(13, pick(even_lon, p2r, p1r, 0, planes))
    put(14, seam[...])
    lane = iota((8, LANES), 1)
    copy_listed.wait()
    copy_list.wait()
    found = listed[slots + 8]

    def patch_listed(n, _):
        chosen = [listed[jnp.minimum(n * UNROLL + u, found - 1)] for u in range(UNROLL)]
        values = []
        for s in chosen:
            for q in range(4):
                e = idxl[8 * q + (s >> SHIFT), s & (LANES - 1)]
                values.append(pltpu.roll(table[pl.ds(e >> SHIFT, 8), :], (s - e) & (LANES - 1), 1))
        for s in chosen:
            mask = lane == (s & (LANES - 1))
            for q in range(4):
                pltpu.store(values_of.at[q, s >> SHIFT], values.pop(0), mask=mask)
        return 0

    lax.fori_loop(0, lax.div(found + (UNROLL - 1), UNROLL), patch_listed, 0)
    copy.wait()
    base = listed[slots + 9]
    own = slot < base
    corner = [
        [values_of[n, b] * stay_signs[n][b : b + 1] for n in range(4)] for b in range(len(blocks))
    ]
    kept = [[jnp.where(own[:, at], stay[n : n + 1, at], 0.0) for n in range(6)] for at in blocks]
    group = jnp.zeros((1, slots), I32)
    for g, (raw, count, signs) in enumerate(groups):
        acc = []
        for q in range(4):
            total = jnp.zeros((8, LANES), F32)
            for t in range(CAP):
                e = idxs[4 * g + q, t]
                value = pltpu.roll(table[pl.ds(e >> SHIFT, 8), :], (t - e) & (LANES - 1), 1)
                total = jnp.where(lane == t, value, total)
            acc.append(pltpu.roll(total * signs[q], base & (LANES - 1), 1))
        moved = pltpu.roll(raw, base & (LANES - 1), 1)
        values = decode(moved) + [moved[9:10], moved[10:11], moved[11:12]]
        mine = (slot >= base) & (slot < base + count)
        for b, at in enumerate(blocks):
            kept[b] = [jnp.where(mine[:, at], x, y) for x, y in zip(values, kept[b])]
            corner[b] = [jnp.where(mine[:, at], x, y) for x, y in zip(acc, corner[b])]
        group = jnp.where(mine, g + 1, group)
        base = base + count
    fold = (group == 4) & top
    new_count[0, 0] = base
    below = iota((8, LANES), 0) < 3
    for b, at in enumerate(blocks):
        position = jnp.concatenate(kept[b][:3], axis=0)

        def rounded(value):
            return value.astype(BF16).astype(F32)

        def sample(pos):
            pa, pb, pc = pos[0:1], pos[1:2], pos[2:3]
            near = jnp.where(below, rounded((1.0 - pb) * (1.0 - pc)), rounded((1.0 - pb) * pc))
            far = jnp.where(below, rounded(pb * (1.0 - pc)), rounded(pb * pc))
            left = near * corner[b][0] + far * corner[b][2]
            right = near * corner[b][1] + far * corner[b][3]
            mixed = (1.0 - pa) * left + pa * right
            return mixed[0:3] + mixed[3:6]

        middle = position + 0.5 * sample(position)
        moved = position + sample(middle)
        na, nb, nc = moved[0:1], moved[1:2], moved[2:3]
        g = group[:, at]
        f = fold[:, at]
        filled = slot[:, at] < base
        na = jnp.where(g == 1, na - 1.0, jnp.where(g == 2, na + 1.0, jnp.where(f, 1.0 - na, na)))
        north_b = jnp.where(f, 2.0 - nb, nb + 1.0)
        nb = jnp.where(g == 3, nb - 1.0, jnp.where(g == 4, north_b, nb))
        new_off[0, :, at] = jnp.where(filled, na, 0.0)
        new_off[1, :, at] = jnp.where(filled, nb, 0.0)
        new_off[2, :, at] = jnp.where(filled, nc, 0.0)
        ci, cj, ck = (row.astype(I32) for row in kept[b][3:])
        ci = jnp.where(
            g == 1, 0, jnp.where(g == 2, cols - 1, jnp.where(f, cols - 1 - ci, ci))
        )
        cj = jnp.where(g == 3, 0, jnp.where(g == 4, rows - 1, cj))
        new_cel[0, :, at] = jnp.where(filled, ci, 0)
        new_cel[1, :, at] = jnp.where(filled, cj, 0)
        new_cel[2, :, at] = jnp.where(filled, ck, 0)


def route(lon_size, lat_size, partner):
    pairs = []
    for p in range(lon_size):
        for r in range(lat_size):
            other = partner(p, r)
            if other is not None:
                pairs.append((p * lat_size + r, other[0] * lat_size + other[1]))
    return pairs


def shards(velocity, offsets, cells, counts, moves):
    depth, rows, cols = velocity.shape[1:]
    slots = offsets.shape[2]
    lon_size, lat_size = lax.axis_size("lon"), lax.axis_size("lat")
    axes = ("lon", "lat")
    planes = up8(3 * depth)
    stride = odd_stride(depth)
    tiles = cols // LANES
    high = 2 * tiles * planes + REC

    def send(x, partner):
        return lax.ppermute(x, axes, route(lon_size, lat_size, partner))

    def array(shape, dtype):
        return jax.ShapeDtypeStruct(shape, dtype)

    q1, q2, lonrec, record, rank0, total = pl.pallas_call(
        pack_kernel,
        out_shape=(
            array((high, LANES), BF16),
            array((high, LANES), BF16),
            array((REC, LANES), BF16),
            array((REC, slots), BF16),
            array((1, slots), I32),
            array((1, LANES), I32),
        ),
        in_specs=[HBM, HBM, HBM, SMEM, HBM],
        out_specs=(VMEM,) * 6,
        scratch_shapes=[
            pltpu.VMEM((3, depth, 8, cols), BF16),
            pltpu.VMEM((3, depth, 8, cols), BF16),
            pltpu.VMEM((3, 1, slots), F32),
            pltpu.VMEM((3, 1, slots), I32),
            pltpu.VMEM((1, slots), I32),
            pltpu.VMEM((2 * tiles * 8 * stride, LANES), F32),
            pltpu.VMEM((REC, slots), F32),
            pltpu.SemaphoreType.DMA((2, 3)),
            pltpu.SemaphoreType.DMA((3,)),
        ],
        compiler_params=room(10),
        name="pack",
    )(*(pltpu.with_memory_space_constraint(x, pltpu.HBM) for x in (velocity, offsets, cells)), counts, pltpu.with_memory_space_constraint(moves, pltpu.HBM))

    q1r = send(q1, lambda p, r: (p, r ^ 1))

    def second(p, r):
        if r == lat_size - 1:
            return (lon_size - 1 - p, r)
        return None if r == 0 else (p, ((r + 1) ^ 1) - 1)

    q2r = send(q2, second)
    per = LANES // rows
    deep = up8(-(-depth // per))
    strips = tiles * rows + 1
    first, last, seam, table, stay, index = pl.pallas_call(
        table_kernel,
        out_shape=(
            array((planes, LANES), F32),
            array((planes, LANES), F32),
            array((planes, LANES), F32),
            array((strips * stride + 8, LANES), F32),
            array((8, slots), F32),
            array((4, slots), I32),
        ),
        in_specs=[VMEM] * 4,
        out_specs=(VMEM,) * 6,
        scratch_shapes=[
            pltpu.VMEM((5 * deep, LANES), F32),
            pltpu.VMEM((9 * up8(per * deep), LANES), F32),
        ],
        compiler_params=room(20),
        cost_estimate=pl.CostEstimate(flops=10**9, bytes_accessed=2 * velocity.size, transcendentals=0),
        name="table",
    )(pltpu.with_memory_space_constraint(velocity, pltpu.VMEM), record, rank0, total)
    p1, p2 = pl.pallas_call(
        side_kernel,
        out_shape=(array((planes + REC, LANES), BF16), array((planes + REC, LANES), BF16)),
        in_specs=[VMEM] * 5,
        out_specs=(VMEM, VMEM),
        compiler_params=room(5),
        name="sides",
    )(first, last, lonrec, q1r, q2r)
    p2r = send(p2, lambda p, r: ((((p + 1) ^ 1) - 1) % lon_size, r))
    p1r = send(p1, lambda p, r: (p ^ 1, r))
    got, listed = pl.pallas_call(
        functools.partial(gather_kernel, stride),
        out_shape=(
            array((4, slots // LANES, 8, LANES), F32),
            array((slots + LANES,), I32),
        ),
        in_specs=[VMEM, SMEM],
        out_specs=(VMEM, SMEM),
        compiler_params=room(10),
        cost_estimate=pl.CostEstimate(flops=10**9, bytes_accessed=2 * velocity.size, transcendentals=0),
        name="gather",
    )(table, index)
    return pl.pallas_call(
        functools.partial(final_kernel, rows, cols, lat_size),
        out_shape=(
            array((3, 1, slots), F32),
            array((3, 1, slots), I32),
            array((1, 1), I32),
        ),
        in_specs=[VMEM, VMEM, pl.BlockSpec(memory_space=pl.ANY)] + [VMEM] * 9,
        out_specs=(VMEM, VMEM, SMEM),
        scratch_shapes=[
            pltpu.VMEM((15 * planes + 8, LANES), F32),
            pltpu.VMEM((4, slots // LANES, 8, LANES), F32),
            pltpu.VMEM((24, LANES), F32),
            pltpu.VMEM((16, LANES), I32),
            pltpu.SMEM((16, LANES), I32),
            pltpu.VMEM((32, LANES), I32),
            pltpu.SMEM((32, LANES), I32),
            pltpu.SMEM((slots + LANES,), I32),
            pltpu.SemaphoreType.DMA((3,)),
        ],
        compiler_params=room(8),
        name="final",
    )(stay, got, listed, first, last, seam, q1, q2, q1r, q2r, p1r, p2r)


def solution(mesh):
    placed = (
        P(None, None, "lat", "lon"),
        P(None, "lat", "lon"),
        P(None, "lat", "lon"),
        P("lat", "lon"),
        P("lat", "lon"),
    )
    return jax.shard_map(
        shards,
        mesh=mesh,
        in_specs=placed,
        out_specs=(P(None, "lat", "lon"), P(None, "lat", "lon"), P("lat", "lon")),
        check_vma=False,
    )
```

```python
import functools

import jax
import jax.numpy as jnp
from jax import lax
from jax.experimental import pallas as pl
from jax.experimental.pallas import tpu as pltpu
from jax.sharding import PartitionSpec as P

CAP = 48
LANES = 128
HALF = 64
REC = 16
UNROLL = 8
SHIFT = 7
F32, BF16, I32 = jnp.float32, jnp.bfloat16, jnp.int32
VMEM = pl.BlockSpec(memory_space=pltpu.VMEM)
SMEM = pl.BlockSpec(memory_space=pltpu.SMEM)
HBM = pl.BlockSpec(memory_space=pltpu.HBM)


def room(mib):
    return pltpu.CompilerParams(vmem_limit_bytes=mib << 20)


def up8(n):
    return (n + 7) // 8 * 8


def odd_stride(depth):
    lines = 3 * depth + 8
    return lines + 1 - lines % 2


def iota(shape, dim):
    return lax.broadcasted_iota(I32, shape, dim)


def nt(a, b):
    return lax.dot_general(a, b, (((1,), (1,)), ((), ())), preferred_element_type=F32)


def pieces(value):
    high = value.astype(BF16).astype(F32)
    rest = value - high
    middle = rest.astype(BF16).astype(F32)
    return [high, middle, rest - middle]


def decode(x):
    return [x[0:1] + x[1:2] + x[2:3], x[3:4] + x[4:5] + x[5:6], x[6:7] + x[7:8] + x[8:9]]


def pack_kernel(
    vel, off, cel, counts, moves, q1, q2, lonrec, record, rank0, total,
    low, high, offv, celv, movev, strips, recs, picked, sems, small,
):
    depth, rows = vel.shape[1], vel.shape[2]
    tiles = vel.shape[3] // LANES
    slots = off.shape[2]
    stride = odd_stride(depth)
    planes = up8(3 * depth)
    inputs = [
        pltpu.make_async_copy(source, target, small.at[n])
        for n, (source, target) in enumerate(((off, offv), (cel, celv), (moves, movev)))
    ]
    for copy in inputs:
        copy.start()
    copies = []
    for comp in range(3):
        copies.append(
            pltpu.make_async_copy(vel.at[comp, :, pl.ds(0, 2), :], low.at[comp, :, pl.ds(0, 2), :], sems.at[0, comp])
        )
        copies.append(
            pltpu.make_async_copy(
                vel.at[comp, :, pl.ds(rows - 2, 2), :],
                high.at[comp, :, pl.ds(6, 2), :],
                sems.at[1, comp],
            )
        )
    for copy in copies:
        copy.start()
    for copy in inputs:
        copy.wait()
    live = counts[0, 0]
    rows_of = []
    for d in range(3):
        rows_of += pieces(offv[d])
    for d in range(3):
        rows_of.append(celv[d].astype(F32))
    rows_of.append(jnp.ones((1, slots), F32))
    for n, row in enumerate(rows_of):
        recs[n : n + 1, :] = row
    recs[len(rows_of) :, :] = jnp.zeros((REC - len(rows_of), slots), F32)
    packed = recs[...].astype(BF16)
    record[...] = packed
    chosen = (movev[...] == iota((8, slots), 0)) & (iota((8, slots), 1) < live)
    ones = chosen.astype(F32)
    scan_of = jnp.where(
        (iota((LANES, 2 * LANES), 0) < iota((LANES, 2 * LANES), 1))
        | (iota((LANES, 2 * LANES), 1) >= LANES),
        1.0,
        0.0,
    ).astype(BF16)
    carry = jnp.zeros((8, LANES), F32)
    ranks = []
    for block in range(slots // LANES):
        piece = ones[:, block * LANES : (block + 1) * LANES].astype(BF16)
        scanned = jnp.dot(piece, scan_of, preferred_element_type=F32)
        ranks.append(scanned[:, :LANES] + carry)
        carry = carry + scanned[:, LANES:]
    rank = jnp.where(chosen, jnp.concatenate(ranks, axis=1), -1.0).astype(I32)
    rank0[...] = rank[0:1]
    target = iota((HALF, slots), 0)
    placing = [
        jnp.where(rank[g : g + 1] == target, 1.0, 0.0).astype(BF16) for g in range(1, 5)
    ]
    lonrec[...] = nt(packed, jnp.concatenate(placing[:2], axis=0)).astype(BF16)
    latrec = nt(packed, jnp.concatenate(placing[2:], axis=0))
    total[...] = carry[0:1, :].astype(I32)
    for comp in range(3):
        copies[2 * comp].wait()
        copies[2 * comp + 1].wait()

        def spread(k, _):
            for source, buffer in enumerate((low, high)):
                value = buffer[comp, k].astype(F32)
                for tile in range(tiles):
                    first = (source * tiles + tile) * 8 * stride + 3 * k + comp
                    strips[pl.ds(first, 8, stride=stride), :] = value[
                        :, tile * LANES : (tile + 1) * LANES
                    ]
            return 0

        lax.fori_loop(0, depth, spread, 0, unroll=15)
    seconds = [
        strips[pl.ds((tile * 8 + 1) * stride, planes), :].astype(BF16) for tile in range(tiles)
    ]
    lane = iota((1, LANES), 1)
    south_i, south_k = latrec[9:10], latrec[11:12]
    column = jnp.where(lane < HALF, pltpu.roll(south_i, HALF, 1), south_i + 1.0).astype(I32)
    level = jnp.where(lane < HALF, pltpu.roll(south_k, HALF, 1), south_k).astype(I32)
    at_column = jnp.zeros((planes, LANES), F32)
    for tile in range(tiles):
        where = jnp.where(iota((LANES, LANES), 0) + tile * LANES == column, 1.0, 0.0).astype(BF16)
        at_column = at_column + jnp.dot(seconds[tile], where, preferred_element_type=F32)
    picked[0:planes, :] = at_column
    deep = up8(depth)
    carried = []
    for step in range(2):
        for comp in range(3):
            lines = picked[pl.ds(comp, deep, stride=3), :]
            there = iota((deep, LANES), 0) == level + step
            carried.append(jnp.sum(jnp.where(there, lines, 0.0), axis=0, keepdims=True))
    for n, row in enumerate(carried):
        recs[n : n + 1, 0:LANES] = row
    recs[len(carried) :, 0:LANES] = jnp.zeros((REC - len(carried), LANES), F32)
    corner = nt(jnp.where(iota((REC, LANES), 1) == 0, 1.0, 0.0).astype(BF16), seconds[0])
    odd = lax.rem(lax.axis_index("lat"), 2)
    for n, out in enumerate((q1, q2)):
        upper = odd if n == 0 else 1 - odd
        for tile in range(tiles):
            last = ((tiles + tile) * 8 + 7) * stride
            first = jnp.where(upper == 1, tile * 8 * stride, last)
            out[tile * planes : (tile + 1) * planes, :] = strips[pl.ds(first, planes), :].astype(BF16)
        at = tiles * planes
        out[at : at + REC, :] = latrec.astype(BF16)
        out[at + REC : at + 2 * REC, :] = recs[:, 0:LANES].astype(BF16)
        out[at + 2 * REC : at + 3 * REC, :] = corner[:, 0:LANES].astype(BF16)
        out[at + 3 * REC :, 0 : planes - LANES] = corner[:, LANES:planes].astype(BF16)


def table_kernel(
    source, record, rank0, total, first, last, seam, table, stay, index, vel, lines, wide, sems
):
    depth, rows, cols = vel.shape[1:]
    parts = 1
    step = depth // parts
    for comp in range(3):
        for part in range(parts):
            at = pl.ds(part * step, step)
            pltpu.make_async_copy(source.at[comp, at], vel.at[comp, at], sems.at[comp]).start()
    slots = record.shape[1]
    tiles = cols // LANES
    planes = up8(3 * depth)
    stride = odd_stride(depth)
    r, c = iota((REC, cols), 0), iota((REC, cols), 1)
    pick = (r == c) & (r < 2)
    pick = pick | ((r == 2) & (c == cols - 1)) | ((r == c - LANES + 4) & (r >= 3) & (r < 5))
    select = jnp.where(pick, 1.0, 0.0).astype(BF16)
    per = LANES // rows
    chunks = -(-depth // per)
    deep = up8(chunks)
    lane = iota((deep, LANES), 1)
    target = iota((LANES, slots), 0)
    packed = record[...]
    rank = rank0[...]
    for block in range(slots // LANES):
        where = jnp.where(rank - block * LANES == target, 1.0, 0.0).astype(BF16)
        out = nt(packed, where)
        lanes = slice(block * LANES, (block + 1) * LANES)
        for d, row in enumerate(decode(out)):
            stay[d : d + 1, lanes] = row
        stay[3:6, lanes] = out[9:12]
        stay[6:8, lanes] = out[12:14]
    i, j, k = (stay[n : n + 1, :].astype(I32) for n in (3, 4, 5))
    slot = iota((1, slots), 1)
    index[0:1, :] = ((i >> SHIFT) * rows + j) * stride + 3 * k
    index[1:2, :] = (slot - i) & (LANES - 1)
    odd_one = (((i & (LANES - 1)) == LANES - 1) | (j == rows - 1)) & (slot < jnp.tile(total[...], (1, slots // LANES)))
    index[2:3, :] = odd_one.astype(I32)
    index[3:4, :] = jnp.tile(total[...], (1, slots // LANES))
    for comp in range(3):
        pltpu.make_async_copy(source.at[comp], vel.at[comp], sems.at[comp]).wait()
        got = nt(select, vel[comp].reshape(depth * rows, cols))
        for n in range(5):
            for q in range(chunks):
                size = min(LANES, depth * rows - q * LANES)
                lines[n * deep + q : n * deep + q + 1, 0:size] = got[
                    n : n + 1, q * LANES : q * LANES + size
                ]
        for m in range(per):

            def line(n, to):
                at = lines[n * deep : (n + 1) * deep, :]
                return pltpu.roll(at, (LANES + to - rows * m) % LANES, 1)

            values = (
                jnp.where(lane < HALF, line(0, 0), line(1, HALF)),
                line(2, 0),
                jnp.where(lane < HALF, line(3, 0), line(4, HALF)),
            )
            for n, value in enumerate(values):
                for q in range(0, deep, 8):
                    at = pl.ds(n * wide.shape[0] // 3 + 3 * (per * q + m) + comp, 8, stride=3 * per)
                    wide[at, :] = value[q : q + 8]
        def fill(k, _):
            value = vel[comp, k].astype(F32)
            for tile in range(tiles):
                for r in range(0, rows, 8):
                    at = pl.ds((tile * rows + r) * stride + 3 * k + comp, 8, stride=stride)
                    table[at, :] = value[r : r + 8, tile * LANES : (tile + 1) * LANES]
            return 0

        lax.fori_loop(0, depth, fill, 0, unroll=5)
    for n, out in enumerate((first, last, seam)):
        at = n * wide.shape[0] // 3
        out[...] = wide[at : at + planes, :]


def gather_kernel(stride, table, index, got, listed):
    lane = iota((8, LANES), 1)
    count = index[3, 0]
    slots = index.shape[1]

    def block_of(b, n):
        acc = [jnp.zeros((8, LANES), F32)] * 4
        for p in range(LANES):
            s = b * LANES + p
            row = index[0, s]
            shift = index[1, s]
            low = pltpu.roll(table[pl.ds(row, 8), :], shift, 1)
            high = pltpu.roll(table[pl.ds(row + stride, 8), :], shift, 1)
            here = lane == p
            beside = lane == ((p + 1) % LANES)
            acc = [
                jnp.where(here, low, acc[0]),
                jnp.where(beside, low, acc[1]),
                jnp.where(here, high, acc[2]),
                jnp.where(beside, high, acc[3]),
            ]
            listed[n] = s
            n = n + index[2, s]
        got[0, b] = acc[0]
        got[1, b] = pltpu.roll(acc[1], LANES - 1, 1)
        got[2, b] = acc[2]
        got[3, b] = pltpu.roll(acc[3], LANES - 1, 1)
        return n

    listed[slots + 8] = lax.fori_loop(0, (count + LANES - 1) >> SHIFT, block_of, I32(0))
    listed[slots + 9] = count


def side_kernel(first, last, lonrec, q1r, q2r, p1, p2):
    planes = first.shape[0]
    even_lat = lax.rem(lax.axis_index("lat"), 2) == 0
    odd_lon = lax.rem(lax.axis_index("lon"), 2)
    lane = iota((planes, LANES), 1)

    def strip(north, n):
        a = q1r[n * planes : (n + 1) * planes, :].astype(F32)
        b = q2r[n * planes : (n + 1) * planes, :].astype(F32)
        return jnp.where(even_lat == north, a, b)

    north0, north1, south0 = strip(True, 0), strip(True, 1), strip(False, 0)
    second0 = []
    for n in range(2):
        at = 2 * planes + (2 + n) * REC
        line = jnp.where(even_lat, q1r[at : at + REC, :], q2r[at : at + REC, :]).astype(F32)
        second0.append(jnp.transpose(jnp.broadcast_to(line[0:1], (LANES, LANES))))
    second0 = jnp.concatenate([second0[0], second0[1][0 : planes - LANES]], axis=0)
    west = first[...]
    west = jnp.where(lane == 32, pltpu.roll(north0, 32, 1), west)
    west = jnp.where(lane == 33, second0, west)
    west = jnp.where(lane == 34, pltpu.roll(south0, 34, 1), west)
    west = jnp.where(lane == 35, pltpu.roll(north1, 36, 1), west)
    west = jnp.where(lane == 96, pltpu.roll(north0, 95, 1), west).astype(BF16)
    east = last[...]
    east = jnp.where(lane == 32, pltpu.roll(north1, 33, 1), east)
    east = jnp.where((lane == 33) | (lane == 34), pltpu.roll(north0, 33, 1), east).astype(BF16)
    p1[0:planes, :] = jnp.where(odd_lon == 1, west, east)
    p2[0:planes, :] = jnp.where(odd_lon == 1, east, west)
    p1[planes:, :] = lonrec[...]
    p2[planes:, :] = lonrec[...]


def places(rows, cols, planes, group, top, y0, x0, k):
    fold = (group == 4) & top
    found, signs = [], []

    def flat(strip, at):
        return strip * (planes * LANES) + at

    def row_at(strip, at):
        return flat(strip + (at >> SHIFT), at & (LANES - 1))

    for dj, di in ((0, 0), (0, 1), (1, 0), (1, 1)):
        y = y0 + dj
        x = x0 + di
        inner = row_at(jnp.where(y == 0, 0, 2), x)
        inner = jnp.where(x == LANES - 1, flat(14, y), inner)
        inner = jnp.where(x == LANES, flat(14, HALF + y), inner)
        inner = jnp.where(x == 0, flat(10, y), inner)
        inner = jnp.where(x == cols - 1, flat(11, y), inner)
        inner = jnp.where(x > cols, flat(12, HALF + y), inner)
        inner = jnp.where(x == cols, flat(12, y), inner)
        inner = jnp.where(x < 0, flat(13, y), inner)
        north = jnp.where(
            x < 0,
            flat(13, 32),
            jnp.where(x == cols, flat(12, 32), jnp.where(x > cols, flat(12, 96), row_at(4, x))),
        )
        u = cols - x
        folded = jnp.where(
            u < 0,
            flat(12, 35),
            jnp.where(u == cols, flat(13, 33), jnp.where(u > cols, flat(13, 34), row_at(4, u))),
        )
        second = flat(12, 33)
        south = jnp.where(x == cols, flat(12, 34), row_at(8, x))
        where = jnp.where(
            y < 0,
            south,
            jnp.where(y > rows, second, jnp.where(y == rows, jnp.where(top, folded, north), inner)),
        )
        if dj == 0:
            across = jnp.where(x == cols, flat(13, 33), row_at(4, x))
            signs.append(jnp.ones(x0.shape, F32))
        else:
            across = jnp.where(u == cols, flat(12, rows - 1), row_at(2, u))
            signs.append(jnp.where(top & (fold | (y == rows)), -1.0, 1.0))
        found.append(jnp.where(fold, across, where) + 3 * LANES * k)
    return found, signs


def final_kernel(
    rows, cols, lat_size,
    stay, got, listed_any, first, last, seam, q1, q2, q1r, q2r, p1r, p2r,
    new_off, new_cel, new_count,
    table, values_of, packed, idxv, idxs, idxlv, idxl, listed, isem,
):
    planes = first.shape[0]
    slots = stay.shape[1]
    lat = lax.axis_index("lat")
    even_lat = lax.rem(lat, 2) == 0
    even_lon = lax.rem(lax.axis_index("lon"), 2) == 0
    top = lat == lat_size - 1
    both = 2 * planes

    def pick(flag, a, b, at, size):
        return jnp.where(flag, a[at : at + size, :], b[at : at + size, :]).astype(F32)

    slot = iota((1, slots), 1)
    copy_list = pltpu.make_async_copy(listed_any, listed, isem.at[2])
    copy_list.start()
    blocks = [slice(b * LANES, (b + 1) * LANES) for b in range(slots // LANES)]
    packed[...] = jnp.zeros(packed.shape, F32)
    for n in range(3):
        for b, at in enumerate(blocks):
            packed[8 * n + b : 8 * n + b + 1, :] = stay[3 + n : 4 + n, at]
    here = [packed[8 * n : 8 * n + 8, :].astype(I32) for n in range(3)]
    e, stay_signs = places(
        rows, cols, planes, jnp.zeros((8, LANES), I32), top, here[1], here[0], here[2]
    )
    for q in range(4):
        idxlv[8 * q : 8 * q + 8, :] = e[q]
    copy_listed = pltpu.make_async_copy(idxlv, idxl, isem.at[0])
    copy_listed.start()
    inside = iota((REC, LANES), 1) < HALF
    wrec = pick(even_lon, p2r, p1r, planes, REC)
    erec = pltpu.roll(pick(even_lon, p1r, p2r, planes, REC), HALF, 1)
    srec = pick(even_lat, q2r, q1r, both, REC)
    nrec = pick(even_lat, q1r, q2r, both, REC)
    nrec = jnp.where(top, nrec, pltpu.roll(nrec, HALF, 1))
    carried = pick(even_lat, q1r, q2r, both + REC, REC)[0:8]
    groups = []
    for g, raw in enumerate((wrec, erec, srec, nrec)):
        raw = jnp.where(inside, raw, 0.0)
        count = jnp.sum(raw[12:13]).astype(I32)
        i, j, k = (raw[n : n + 1].astype(I32) for n in (9, 10, 11))
        y0 = (j, j, jnp.full_like(j, -1), jnp.full_like(j, rows))[g]
        x0 = (jnp.full_like(i, -1), jnp.full_like(i, cols), i, i)[g]
        e, signs = places(rows, cols, planes, jnp.full_like(i, g + 1), top, y0, x0, k)
        for q in range(4):
            row = 4 * g + q
            idxv[row : row + 1, :] = e[q]
        groups.append((raw, count, signs))
    copy = pltpu.make_async_copy(idxv, idxs, isem.at[1])
    copy.start()
    values_of[...] = got[...]

    def put(n, value):
        table[n * planes : (n + 1) * planes, :] = value

    for t in range(2):
        at = t * planes
        put(t, pick(even_lat, q2, q1, at, planes))
        put(2 + t, pick(even_lat, q1, q2, at, planes))
        put(4 + t, pick(even_lat, q1r, q2r, at, planes))
        put(8 + t, pick(even_lat, q2r, q1r, at, planes))
    put(10, first[...])
    put(11, last[...])
    put(12, pick(even_lon, p1r, p2r, 0, planes))
    put(13, pick(even_lon, p2r, p1r, 0, planes))
    put(14, seam[...])
    lane = iota((8, LANES), 1)
    copy_listed.wait()
    copy_list.wait()
    found = listed[slots + 8]

    def patch_listed(n, _):
        chosen = [listed[jnp.minimum(n * UNROLL + u, found - 1)] for u in range(UNROLL)]
        values = []
        for s in chosen:
            for q in range(4):
                e = idxl[8 * q + (s >> SHIFT), s & (LANES - 1)]
                values.append(pltpu.roll(table[pl.ds(e >> SHIFT, 8), :], (s - e) & (LANES - 1), 1))
        for s in chosen:
            mask = lane == (s & (LANES - 1))
            for q in range(4):
                pltpu.store(values_of.at[q, s >> SHIFT], values.pop(0), mask=mask)
        return 0

    lax.fori_loop(0, lax.div(found + (UNROLL - 1), UNROLL), patch_listed, 0)
    copy.wait()
    base = listed[slots + 9]
    own = slot < base
    corner = [
        [values_of[n, b] * stay_signs[n][b : b + 1] for n in range(4)] for b in range(len(blocks))
    ]
    kept = [[jnp.where(own[:, at], stay[n : n + 1, at], 0.0) for n in range(6)] for at in blocks]
    group = jnp.zeros((1, slots), I32)
    for g, (raw, count, signs) in enumerate(groups):
        acc = []
        for q in range(4):
            total = jnp.zeros((8, LANES), F32)
            for t in range(CAP):
                e = idxs[4 * g + q, t]
                value = pltpu.roll(table[pl.ds(e >> SHIFT, 8), :], (t - e) & (LANES - 1), 1)
                total = jnp.where(lane == t, value, total)
            if g == 3 and q > 1:
                sent = carried if q == 2 else pltpu.roll(carried, HALF, 1)
                beyond = top if q == 2 else top | (raw[9:10].astype(I32) == cols - 1)
                total = jnp.where(beyond, total, sent)
            acc.append(pltpu.roll(total * signs[q], base & (LANES - 1), 1))
        moved = pltpu.roll(raw, base & (LANES - 1), 1)
        values = decode(moved) + [moved[9:10], moved[10:11], moved[11:12]]
        mine = (slot >= base) & (slot < base + count)
        for b, at in enumerate(blocks):
            kept[b] = [jnp.where(mine[:, at], x, y) for x, y in zip(values, kept[b])]
            corner[b] = [jnp.where(mine[:, at], x, y) for x, y in zip(acc, corner[b])]
        group = jnp.where(mine, g + 1, group)
        base = base + count
    fold = (group == 4) & top
    new_count[0, 0] = base
    below = iota((8, LANES), 0) < 3
    for b, at in enumerate(blocks):
        position = jnp.concatenate(kept[b][:3], axis=0)

        def rounded(value):
            return value.astype(BF16).astype(F32)

        def sample(pos):
            pa, pb, pc = pos[0:1], pos[1:2], pos[2:3]
            near = jnp.where(below, rounded((1.0 - pb) * (1.0 - pc)), rounded((1.0 - pb) * pc))
            far = jnp.where(below, rounded(pb * (1.0 - pc)), rounded(pb * pc))
            left = near * corner[b][0] + far * corner[b][2]
            right = near * corner[b][1] + far * corner[b][3]
            mixed = (1.0 - pa) * left + pa * right
            return mixed[0:3] + mixed[3:6]

        middle = position + 0.5 * sample(position)
        moved = position + sample(middle)
        na, nb, nc = moved[0:1], moved[1:2], moved[2:3]
        g = group[:, at]
        f = fold[:, at]
        filled = slot[:, at] < base
        na = jnp.where(g == 1, na - 1.0, jnp.where(g == 2, na + 1.0, jnp.where(f, 1.0 - na, na)))
        north_b = jnp.where(f, 2.0 - nb, nb + 1.0)
        nb = jnp.where(g == 3, nb - 1.0, jnp.where(g == 4, north_b, nb))
        new_off[0, :, at] = jnp.where(filled, na, 0.0)
        new_off[1, :, at] = jnp.where(filled, nb, 0.0)
        new_off[2, :, at] = jnp.where(filled, nc, 0.0)
        ci, cj, ck = (row.astype(I32) for row in kept[b][3:])
        ci = jnp.where(
            g == 1, 0, jnp.where(g == 2, cols - 1, jnp.where(f, cols - 1 - ci, ci))
        )
        cj = jnp.where(g == 3, 0, jnp.where(g == 4, rows - 1, cj))
        new_cel[0, :, at] = jnp.where(filled, ci, 0)
        new_cel[1, :, at] = jnp.where(filled, cj, 0)
        new_cel[2, :, at] = jnp.where(filled, ck, 0)


def route(lon_size, lat_size, partner):
    pairs = []
    for p in range(lon_size):
        for r in range(lat_size):
            other = partner(p, r)
            if other is not None:
                pairs.append((p * lat_size + r, other[0] * lat_size + other[1]))
    return pairs


def shards(velocity, offsets, cells, counts, moves):
    depth, rows, cols = velocity.shape[1:]
    slots = offsets.shape[2]
    lon_size, lat_size = lax.axis_size("lon"), lax.axis_size("lat")
    axes = ("lon", "lat")
    planes = up8(3 * depth)
    stride = odd_stride(depth)
    tiles = cols // LANES
    high = tiles * planes + 4 * REC

    def send(x, partner):
        return lax.ppermute(x, axes, route(lon_size, lat_size, partner))

    def array(shape, dtype):
        return jax.ShapeDtypeStruct(shape, dtype)

    q1, q2, lonrec, record, rank0, total = pl.pallas_call(
        pack_kernel,
        out_shape=(
            array((high, LANES), BF16),
            array((high, LANES), BF16),
            array((REC, LANES), BF16),
            array((REC, slots), BF16),
            array((1, slots), I32),
            array((1, LANES), I32),
        ),
        in_specs=[HBM, HBM, HBM, SMEM, HBM],
        out_specs=(VMEM,) * 6,
        scratch_shapes=[
            pltpu.VMEM((3, depth, 8, cols), BF16),
            pltpu.VMEM((3, depth, 8, cols), BF16),
            pltpu.VMEM((3, 1, slots), F32),
            pltpu.VMEM((3, 1, slots), I32),
            pltpu.VMEM((1, slots), I32),
            pltpu.VMEM((2 * tiles * 8 * stride, LANES), F32),
            pltpu.VMEM((REC, slots), F32),
            pltpu.VMEM((3 * up8(depth) + 8, LANES), F32),
            pltpu.SemaphoreType.DMA((2, 3)),
            pltpu.SemaphoreType.DMA((3,)),
        ],
        compiler_params=room(10),
        name="pack",
    )(*(pltpu.with_memory_space_constraint(x, pltpu.HBM) for x in (velocity, offsets, cells)), counts, pltpu.with_memory_space_constraint(moves, pltpu.HBM))

    q1r = send(q1, lambda p, r: (p, r ^ 1))

    def second(p, r):
        if r == lat_size - 1:
            return (lon_size - 1 - p, r)
        return None if r == 0 else (p, ((r + 1) ^ 1) - 1)

    q2r = send(q2, second)
    per = LANES // rows
    deep = up8(-(-depth // per))
    strips = tiles * rows + 1
    first, last, seam, table, stay, index = pl.pallas_call(
        table_kernel,
        out_shape=(
            array((planes, LANES), F32),
            array((planes, LANES), F32),
            array((planes, LANES), F32),
            array((strips * stride + 8, LANES), F32),
            array((8, slots), F32),
            array((4, slots), I32),
        ),
        in_specs=[HBM] + [VMEM] * 3,
        out_specs=(VMEM,) * 6,
        scratch_shapes=[
            pltpu.VMEM((3, depth, rows, cols), BF16),
            pltpu.VMEM((5 * deep, LANES), F32),
            pltpu.VMEM((9 * up8(per * deep), LANES), F32),
            pltpu.SemaphoreType.DMA((3,)),
        ],
        compiler_params=room(20),
        cost_estimate=pl.CostEstimate(flops=10**9, bytes_accessed=2 * velocity.size, transcendentals=0),
        name="table",
    )(pltpu.with_memory_space_constraint(velocity, pltpu.HBM), record, rank0, total)
    p1, p2 = pl.pallas_call(
        side_kernel,
        out_shape=(array((planes + REC, LANES), BF16), array((planes + REC, LANES), BF16)),
        in_specs=[VMEM] * 5,
        out_specs=(VMEM, VMEM),
        compiler_params=room(5),
        name="sides",
    )(first, last, lonrec, q1r, q2r)
    p2r = send(p2, lambda p, r: ((((p + 1) ^ 1) - 1) % lon_size, r))
    p1r = send(p1, lambda p, r: (p ^ 1, r))
    got, listed = pl.pallas_call(
        functools.partial(gather_kernel, stride),
        out_shape=(
            array((4, slots // LANES, 8, LANES), F32),
            array((slots + LANES,), I32),
        ),
        in_specs=[VMEM, SMEM],
        out_specs=(VMEM, SMEM),
        compiler_params=room(10),
        cost_estimate=pl.CostEstimate(flops=10**9, bytes_accessed=2 * velocity.size, transcendentals=0),
        name="gather",
    )(table, index)
    return pl.pallas_call(
        functools.partial(final_kernel, rows, cols, lat_size),
        out_shape=(
            array((3, 1, slots), F32),
            array((3, 1, slots), I32),
            array((1, 1), I32),
        ),
        in_specs=[VMEM, VMEM, pl.BlockSpec(memory_space=pl.ANY)] + [VMEM] * 9,
        out_specs=(VMEM, VMEM, SMEM),
        scratch_shapes=[
            pltpu.VMEM((15 * planes + 8, LANES), F32),
            pltpu.VMEM((4, slots // LANES, 8, LANES), F32),
            pltpu.VMEM((24, LANES), F32),
            pltpu.VMEM((16, LANES), I32),
            pltpu.SMEM((16, LANES), I32),
            pltpu.VMEM((32, LANES), I32),
            pltpu.SMEM((32, LANES), I32),
            pltpu.SMEM((slots + LANES,), I32),
            pltpu.SemaphoreType.DMA((3,)),
        ],
        compiler_params=room(8),
        name="final",
    )(stay, got, listed, first, last, seam, q1, q2, q1r, q2r, p1r, p2r)


def solution(mesh):
    placed = (
        P(None, None, "lat", "lon"),
        P(None, "lat", "lon"),
        P(None, "lat", "lon"),
        P("lat", "lon"),
        P("lat", "lon"),
    )
    return jax.shard_map(
        shards,
        mesh=mesh,
        in_specs=placed,
        out_specs=(P(None, "lat", "lon"), P(None, "lat", "lon"), P("lat", "lon")),
        check_vma=False,
    )
```

```python
import functools

import jax
import jax.numpy as jnp
from jax import lax
from jax.experimental import pallas as pl
from jax.experimental.pallas import tpu as pltpu
from jax.sharding import PartitionSpec as P

CAP = 48
LANES = 128
HALF = 64
REC = 16
UNROLL = 8
SHIFT = 7
F32, BF16, I32 = jnp.float32, jnp.bfloat16, jnp.int32
VMEM = pl.BlockSpec(memory_space=pltpu.VMEM)
SMEM = pl.BlockSpec(memory_space=pltpu.SMEM)
HBM = pl.BlockSpec(memory_space=pltpu.HBM)


def room(mib):
    return pltpu.CompilerParams(vmem_limit_bytes=mib << 20)


def up8(n):
    return (n + 7) // 8 * 8


def odd_stride(depth):
    lines = 3 * depth + 8
    return lines + 1 - lines % 2


def iota(shape, dim):
    return lax.broadcasted_iota(I32, shape, dim)


def nt(a, b):
    return lax.dot_general(a, b, (((1,), (1,)), ((), ())), preferred_element_type=F32)


def pieces(value):
    high = value.astype(BF16).astype(F32)
    rest = value - high
    middle = rest.astype(BF16).astype(F32)
    return [high, middle, rest - middle]


def decode(x):
    return [x[0:1] + x[1:2] + x[2:3], x[3:4] + x[4:5] + x[5:6], x[6:7] + x[7:8] + x[8:9]]


def pack_kernel(
    vel, off, cel, counts, moves, q1, q2, lonrec, record, rank0, total, zonal,
    low, high, offv, celv, movev, strips, recs, picked, sems, small,
):
    depth, rows = vel.shape[1], vel.shape[2]
    tiles = vel.shape[3] // LANES
    slots = off.shape[2]
    stride = odd_stride(depth)
    planes = up8(3 * depth)
    inputs = [
        pltpu.make_async_copy(source, target, small.at[n])
        for n, (source, target) in enumerate(((off, offv), (cel, celv), (moves, movev)))
    ]
    for copy in inputs:
        copy.start()
    copies = []
    for comp in range(3):
        copies.append(
            pltpu.make_async_copy(vel.at[comp, :, pl.ds(0, 2), :], low.at[comp, :, pl.ds(0, 2), :], sems.at[0, comp])
        )
        copies.append(
            pltpu.make_async_copy(
                vel.at[comp, :, pl.ds(rows - 2, 2), :],
                high.at[comp, :, pl.ds(6, 2), :],
                sems.at[1, comp],
            )
        )
    for copy in copies:
        copy.start()
    whole = pltpu.make_async_copy(vel.at[0], zonal, small.at[3])
    whole.start()
    for copy in inputs:
        copy.wait()
    live = counts[0, 0]
    rows_of = []
    for d in range(3):
        rows_of += pieces(offv[d])
    for d in range(3):
        rows_of.append(celv[d].astype(F32))
    rows_of.append(jnp.ones((1, slots), F32))
    for n, row in enumerate(rows_of):
        recs[n : n + 1, :] = row
    recs[len(rows_of) :, :] = jnp.zeros((REC - len(rows_of), slots), F32)
    packed = recs[...].astype(BF16)
    record[...] = packed
    chosen = (movev[...] == iota((8, slots), 0)) & (iota((8, slots), 1) < live)
    ones = chosen.astype(F32)
    scan_of = jnp.where(
        (iota((LANES, 2 * LANES), 0) < iota((LANES, 2 * LANES), 1))
        | (iota((LANES, 2 * LANES), 1) >= LANES),
        1.0,
        0.0,
    ).astype(BF16)
    carry = jnp.zeros((8, LANES), F32)
    ranks = []
    for block in range(slots // LANES):
        piece = ones[:, block * LANES : (block + 1) * LANES].astype(BF16)
        scanned = jnp.dot(piece, scan_of, preferred_element_type=F32)
        ranks.append(scanned[:, :LANES] + carry)
        carry = carry + scanned[:, LANES:]
    rank = jnp.where(chosen, jnp.concatenate(ranks, axis=1), -1.0).astype(I32)
    rank0[...] = rank[0:1]
    target = iota((HALF, slots), 0)
    placing = [
        jnp.where(rank[g : g + 1] == target, 1.0, 0.0).astype(BF16) for g in range(1, 5)
    ]
    lonrec[...] = nt(packed, jnp.concatenate(placing[:2], axis=0)).astype(BF16)
    latrec = nt(packed, jnp.concatenate(placing[2:], axis=0))
    total[...] = carry[0:1, :].astype(I32)
    for comp in range(3):
        copies[2 * comp].wait()
        copies[2 * comp + 1].wait()

        def spread(k, _):
            for source, buffer in enumerate((low, high)):
                value = buffer[comp, k].astype(F32)
                for tile in range(tiles):
                    first = (source * tiles + tile) * 8 * stride + 3 * k + comp
                    strips[pl.ds(first, 8, stride=stride), :] = value[
                        :, tile * LANES : (tile + 1) * LANES
                    ]
            return 0

        lax.fori_loop(0, depth, spread, 0, unroll=15)
    seconds = [
        strips[pl.ds((tile * 8 + 1) * stride, planes), :].astype(BF16) for tile in range(tiles)
    ]
    lane = iota((1, LANES), 1)
    south_i, south_k = latrec[9:10], latrec[11:12]
    column = jnp.where(lane < HALF, pltpu.roll(south_i, HALF, 1), south_i + 1.0).astype(I32)
    level = jnp.where(lane < HALF, pltpu.roll(south_k, HALF, 1), south_k).astype(I32)
    at_column = jnp.zeros((planes, LANES), F32)
    for tile in range(tiles):
        where = jnp.where(iota((LANES, LANES), 0) + tile * LANES == column, 1.0, 0.0).astype(BF16)
        at_column = at_column + jnp.dot(seconds[tile], where, preferred_element_type=F32)
    picked[0:planes, :] = at_column
    deep = up8(depth)
    carried = []
    for step in range(2):
        for comp in range(3):
            lines = picked[pl.ds(comp, deep, stride=3), :]
            there = iota((deep, LANES), 0) == level + step
            carried.append(jnp.sum(jnp.where(there, lines, 0.0), axis=0, keepdims=True))
    for n, row in enumerate(carried):
        recs[n : n + 1, 0:LANES] = row
    recs[len(carried) :, 0:LANES] = jnp.zeros((REC - len(carried), LANES), F32)
    corner = nt(jnp.where(iota((REC, LANES), 1) == 0, 1.0, 0.0).astype(BF16), seconds[0])
    odd = lax.rem(lax.axis_index("lat"), 2)
    for n, out in enumerate((q1, q2)):
        upper = odd if n == 0 else 1 - odd
        for tile in range(tiles):
            last = ((tiles + tile) * 8 + 7) * stride
            first = jnp.where(upper == 1, tile * 8 * stride, last)
            out[tile * planes : (tile + 1) * planes, :] = strips[pl.ds(first, planes), :].astype(BF16)
        at = tiles * planes
        out[at : at + REC, :] = latrec.astype(BF16)
        out[at + REC : at + 2 * REC, :] = recs[:, 0:LANES].astype(BF16)
        out[at + 2 * REC : at + 3 * REC, :] = corner[:, 0:LANES].astype(BF16)
        out[at + 3 * REC :, 0 : planes - LANES] = corner[:, LANES:planes].astype(BF16)
    whole.wait()


def table_kernel(
    source, zonal, record, rank0, total, first, last, seam, table, stay, index, vel, lines, wide, sems
):
    depth, rows, cols = vel.shape[1:]
    copies = [
        pltpu.make_async_copy(source.at[comp + 1], vel.at[comp], sems.at[comp]) for comp in range(2)
    ]
    for copy in copies:
        copy.start()
    slots = record.shape[1]
    tiles = cols // LANES
    planes = up8(3 * depth)
    stride = odd_stride(depth)
    r, c = iota((REC, cols), 0), iota((REC, cols), 1)
    pick = (r == c) & (r < 2)
    pick = pick | ((r == 2) & (c == cols - 1)) | ((r == c - LANES + 4) & (r >= 3) & (r < 5))
    select = jnp.where(pick, 1.0, 0.0).astype(BF16)
    per = LANES // rows
    chunks = -(-depth // per)
    deep = up8(chunks)
    lane = iota((deep, LANES), 1)
    target = iota((LANES, slots), 0)
    packed = record[...]
    rank = rank0[...]
    for block in range(slots // LANES):
        where = jnp.where(rank - block * LANES == target, 1.0, 0.0).astype(BF16)
        out = nt(packed, where)
        lanes = slice(block * LANES, (block + 1) * LANES)
        for d, row in enumerate(decode(out)):
            stay[d : d + 1, lanes] = row
        stay[3:6, lanes] = out[9:12]
        stay[6:8, lanes] = out[12:14]
    i, j, k = (stay[n : n + 1, :].astype(I32) for n in (3, 4, 5))
    slot = iota((1, slots), 1)
    index[0:1, :] = ((i >> SHIFT) * rows + j) * stride + 3 * k
    index[1:2, :] = (slot - i) & (LANES - 1)
    odd_one = (((i & (LANES - 1)) == LANES - 1) | (j == rows - 1)) & (slot < jnp.tile(total[...], (1, slots // LANES)))
    index[2:3, :] = odd_one.astype(I32)
    index[3:4, :] = jnp.tile(total[...], (1, slots // LANES))
    for comp in range(3):
        if comp > 0:
            copies[comp - 1].wait()
        block = vel.at[comp - 1] if comp > 0 else zonal
        got = nt(select, block[...].reshape(depth * rows, cols))
        for n in range(5):
            for q in range(chunks):
                size = min(LANES, depth * rows - q * LANES)
                lines[n * deep + q : n * deep + q + 1, 0:size] = got[
                    n : n + 1, q * LANES : q * LANES + size
                ]
        for m in range(per):

            def line(n, to):
                at = lines[n * deep : (n + 1) * deep, :]
                return pltpu.roll(at, (LANES + to - rows * m) % LANES, 1)

            values = (
                jnp.where(lane < HALF, line(0, 0), line(1, HALF)),
                line(2, 0),
                jnp.where(lane < HALF, line(3, 0), line(4, HALF)),
            )
            for n, value in enumerate(values):
                for q in range(0, deep, 8):
                    at = pl.ds(n * wide.shape[0] // 3 + 3 * (per * q + m) + comp, 8, stride=3 * per)
                    wide[at, :] = value[q : q + 8]
        def fill(k, _):
            value = block[k].astype(F32)
            for tile in range(tiles):
                for r in range(0, rows, 8):
                    at = pl.ds((tile * rows + r) * stride + 3 * k + comp, 8, stride=stride)
                    table[at, :] = value[r : r + 8, tile * LANES : (tile + 1) * LANES]
            return 0

        lax.fori_loop(0, depth, fill, 0, unroll=5)
    for n, out in enumerate((first, last, seam)):
        at = n * wide.shape[0] // 3
        out[...] = wide[at : at + planes, :]


def gather_kernel(stride, table, index, got, listed):
    lane = iota((8, LANES), 1)
    count = index[3, 0]
    slots = index.shape[1]

    def block_of(b, n):
        acc = [jnp.zeros((8, LANES), F32)] * 4
        for p in range(LANES):
            s = b * LANES + p
            row = index[0, s]
            shift = index[1, s]
            low = pltpu.roll(table[pl.ds(row, 8), :], shift, 1)
            high = pltpu.roll(table[pl.ds(row + stride, 8), :], shift, 1)
            here = lane == p
            beside = lane == ((p + 1) % LANES)
            acc = [
                jnp.where(here, low, acc[0]),
                jnp.where(beside, low, acc[1]),
                jnp.where(here, high, acc[2]),
                jnp.where(beside, high, acc[3]),
            ]
            listed[n] = s
            n = n + index[2, s]
        got[0, b] = acc[0]
        got[1, b] = pltpu.roll(acc[1], LANES - 1, 1)
        got[2, b] = acc[2]
        got[3, b] = pltpu.roll(acc[3], LANES - 1, 1)
        return n

    full = (count + LANES - 1) >> SHIFT
    listed[slots + 8] = lax.fori_loop(0, full, block_of, I32(0))
    listed[slots + 9] = count


def group_places(rows, cols, planes, g, top, raw, lines):
    i, j, k = (raw[n : n + 1].astype(I32) for n in (9, 10, 11))
    y0 = (j, j, jnp.full_like(j, -1), jnp.full_like(j, rows))[g]
    x0 = (jnp.full_like(i, -1), jnp.full_like(i, cols), i, i)[g]
    e, signs = places(rows, cols, planes, jnp.full_like(i, g + 1), top, y0, x0, k)
    half = lines.shape[0] // 2
    for q in range(4):
        row = 4 * (g % (half // 4)) + q
        lines[row : row + 1, :] = e[q] >> SHIFT
        lines[half + row : half + row + 1, :] = (iota((1, LANES), 1) - e[q]) & (LANES - 1)
    return signs


def group_corner(table, lines, row):
    lane = iota((8, LANES), 1)
    half = lines.shape[0] // 2
    total = jnp.zeros((8, LANES), F32)
    for t in range(CAP):
        value = pltpu.roll(table[pl.ds(lines[row, t], 8), :], lines[half + row, t], 1)
        total = jnp.where(lane == t, value, total)
    return total


def lat_records(planes, top, even_lat, q1r, q2r):
    at = slice(2 * planes, 2 * planes + REC)
    inside = iota((REC, LANES), 1) < HALF
    srec = jnp.where(even_lat, q2r[at, :], q1r[at, :]).astype(F32)
    nrec = jnp.where(even_lat, q1r[at, :], q2r[at, :]).astype(F32)
    nrec = jnp.where(top, nrec, pltpu.roll(nrec, HALF, 1))
    return jnp.where(inside, srec, 0.0), jnp.where(inside, nrec, 0.0)


def put_rows(table, planes, even_lat, q1, q2, q1r, q2r, first, last, seam):
    def put(n, value):
        table[n * planes : (n + 1) * planes, :] = value

    def pick(a, b, at):
        at = slice(at, at + planes)
        return jnp.where(even_lat, a[at, :], b[at, :]).astype(F32)

    for t in range(2):
        put(t, pick(q2, q1, t * planes))
        put(2 + t, pick(q1, q2, t * planes))
        put(4 + t, pick(q1r, q2r, t * planes))
        put(8 + t, pick(q2r, q1r, t * planes))
    put(10, first[...])
    put(11, last[...])
    put(14, seam[...])


def side_kernel(first, last, lonrec, q1r, q2r, p1, p2):
    planes = first.shape[0]
    even_lat = lax.rem(lax.axis_index("lat"), 2) == 0
    odd_lon = lax.rem(lax.axis_index("lon"), 2)
    lane = iota((planes, LANES), 1)

    def strip(north, n):
        a = q1r[n * planes : (n + 1) * planes, :].astype(F32)
        b = q2r[n * planes : (n + 1) * planes, :].astype(F32)
        return jnp.where(even_lat == north, a, b)

    north0, north1, south0 = strip(True, 0), strip(True, 1), strip(False, 0)
    second0 = []
    for n in range(2):
        at = 2 * planes + (2 + n) * REC
        line = jnp.where(even_lat, q1r[at : at + REC, :], q2r[at : at + REC, :]).astype(F32)
        second0.append(jnp.transpose(jnp.broadcast_to(line[0:1], (LANES, LANES))))
    second0 = jnp.concatenate([second0[0], second0[1][0 : planes - LANES]], axis=0)
    west = first[...]
    west = jnp.where(lane == 32, pltpu.roll(north0, 32, 1), west)
    west = jnp.where(lane == 33, second0, west)
    west = jnp.where(lane == 34, pltpu.roll(south0, 34, 1), west)
    west = jnp.where(lane == 35, pltpu.roll(north1, 36, 1), west)
    west = jnp.where(lane == 96, pltpu.roll(north0, 95, 1), west).astype(BF16)
    east = last[...]
    east = jnp.where(lane == 32, pltpu.roll(north1, 33, 1), east)
    east = jnp.where((lane == 33) | (lane == 34), pltpu.roll(north0, 33, 1), east).astype(BF16)
    p1[0:planes, :] = jnp.where(odd_lon == 1, west, east)
    p2[0:planes, :] = jnp.where(odd_lon == 1, east, west)
    p1[planes:, :] = lonrec[...]
    p2[planes:, :] = lonrec[...]


def places(rows, cols, planes, group, top, y0, x0, k):
    fold = (group == 4) & top
    found, signs = [], []

    def flat(strip, at):
        return strip * (planes * LANES) + at

    def row_at(strip, at):
        return flat(strip + (at >> SHIFT), at & (LANES - 1))

    for dj, di in ((0, 0), (0, 1), (1, 0), (1, 1)):
        y = y0 + dj
        x = x0 + di
        inner = row_at(jnp.where(y == 0, 0, 2), x)
        inner = jnp.where(x == LANES - 1, flat(14, y), inner)
        inner = jnp.where(x == LANES, flat(14, HALF + y), inner)
        inner = jnp.where(x == 0, flat(10, y), inner)
        inner = jnp.where(x == cols - 1, flat(11, y), inner)
        inner = jnp.where(x > cols, flat(12, HALF + y), inner)
        inner = jnp.where(x == cols, flat(12, y), inner)
        inner = jnp.where(x < 0, flat(13, y), inner)
        north = jnp.where(
            x < 0,
            flat(13, 32),
            jnp.where(x == cols, flat(12, 32), jnp.where(x > cols, flat(12, 96), row_at(4, x))),
        )
        u = cols - x
        folded = jnp.where(
            u < 0,
            flat(12, 35),
            jnp.where(u == cols, flat(13, 33), jnp.where(u > cols, flat(13, 34), row_at(4, u))),
        )
        second = flat(12, 33)
        south = jnp.where(x == cols, flat(12, 34), row_at(8, x))
        where = jnp.where(
            y < 0,
            south,
            jnp.where(y > rows, second, jnp.where(y == rows, jnp.where(top, folded, north), inner)),
        )
        if dj == 0:
            across = jnp.where(x == cols, flat(13, 33), row_at(4, x))
            signs.append(jnp.ones(x0.shape, F32))
        else:
            across = jnp.where(u == cols, flat(12, rows - 1), row_at(2, u))
            signs.append(jnp.where(top & (fold | (y == rows)), -1.0, 1.0))
        found.append(jnp.where(fold, across, where) + 3 * LANES * k)
    return found, signs


def final_kernel(
    rows, cols, lat_size,
    stay, got, listed_any, first, last, seam, q1, q2, q1r, q2r, p1r, p2r,
    new_off, new_cel, new_count,
    table, values_of, packed, idxv, idxs, idxlv, idxl, listed, isem,
):
    planes = first.shape[0]
    slots = stay.shape[1]
    lat = lax.axis_index("lat")
    even_lat = lax.rem(lat, 2) == 0
    even_lon = lax.rem(lax.axis_index("lon"), 2) == 0
    top = lat == lat_size - 1
    both = 2 * planes

    def pick(flag, a, b, at, size):
        return jnp.where(flag, a[at : at + size, :], b[at : at + size, :]).astype(F32)

    slot = iota((1, slots), 1)
    copy_list = pltpu.make_async_copy(listed_any, listed, isem.at[2])
    copy_list.start()
    blocks = [slice(b * LANES, (b + 1) * LANES) for b in range(slots // LANES)]
    packed[...] = jnp.zeros(packed.shape, F32)
    for n in range(3):
        for b, at in enumerate(blocks):
            packed[8 * n + b : 8 * n + b + 1, :] = stay[3 + n : 4 + n, at]
    here = [packed[8 * n : 8 * n + 8, :].astype(I32) for n in range(3)]
    e, stay_signs = places(
        rows, cols, planes, jnp.zeros((8, LANES), I32), top, here[1], here[0], here[2]
    )
    for q in range(4):
        idxlv[8 * q : 8 * q + 8, :] = e[q]
    copy_listed = pltpu.make_async_copy(idxlv, idxl, isem.at[0])
    copy_listed.start()
    inside = iota((REC, LANES), 1) < HALF
    wrec = pick(even_lon, p2r, p1r, planes, REC)
    erec = pltpu.roll(pick(even_lon, p1r, p2r, planes, REC), HALF, 1)
    srec, nrec = lat_records(planes, top, even_lat, q1r, q2r)
    carried = pick(even_lat, q1r, q2r, both + REC, REC)[0:8]
    groups = []
    for g, raw in enumerate((wrec, erec, srec, nrec)):
        raw = jnp.where(inside, raw, 0.0)
        count = jnp.sum(raw[12:13]).astype(I32)
        groups.append((raw, count, group_places(rows, cols, planes, g, top, raw, idxv)))
    copy = pltpu.make_async_copy(idxv, idxs, isem.at[1])
    copy.start()
    values_of[...] = got[...]
    put_rows(table, planes, even_lat, q1, q2, q1r, q2r, first, last, seam)
    table[12 * planes : 13 * planes, :] = pick(even_lon, p1r, p2r, 0, planes)
    table[13 * planes : 14 * planes, :] = pick(even_lon, p2r, p1r, 0, planes)
    lane = iota((8, LANES), 1)
    copy_listed.wait()
    copy_list.wait()
    found = listed[slots + 8]

    def patch_listed(n, _):
        chosen = [listed[jnp.minimum(n * UNROLL + u, found - 1)] for u in range(UNROLL)]
        values = []
        for s in chosen:
            for q in range(4):
                e = idxl[8 * q + (s >> SHIFT), s & (LANES - 1)]
                line = table[pl.ds(e >> SHIFT, 8), :]
                values.append(pltpu.roll(line, (s - e) & (LANES - 1), 1))
        for s in chosen:
            mask = lane == (s & (LANES - 1))
            for q in range(4):
                pltpu.store(values_of.at[q, s >> SHIFT], values.pop(0), mask=mask)
        return 0

    lax.fori_loop(0, lax.div(found + (UNROLL - 1), UNROLL), patch_listed, 0)
    copy.wait()
    base = listed[slots + 9]
    own = slot < base
    corner = [
        [values_of[n, b] * stay_signs[n][b : b + 1] for n in range(4)] for b in range(len(blocks))
    ]
    kept = [[jnp.where(own[:, at], stay[n : n + 1, at], 0.0) for n in range(6)] for at in blocks]
    group = jnp.zeros((1, slots), I32)
    for g, (raw, count, signs) in enumerate(groups):
        corners = [group_corner(table, idxs, 4 * g + q) for q in range(4)]
        acc = []
        for q in range(4):
            total = corners[q]
            if g == 3 and q > 1:
                sent = carried if q == 2 else pltpu.roll(carried, HALF, 1)
                beyond = top if q == 2 else top | (raw[9:10].astype(I32) == cols - 1)
                total = jnp.where(beyond, total, sent)
            acc.append(pltpu.roll(total * signs[q], base & (LANES - 1), 1))
        moved = pltpu.roll(raw, base & (LANES - 1), 1)
        values = decode(moved) + [moved[9:10], moved[10:11], moved[11:12]]
        mine = (slot >= base) & (slot < base + count)
        for b, at in enumerate(blocks):
            kept[b] = [jnp.where(mine[:, at], x, y) for x, y in zip(values, kept[b])]
            corner[b] = [jnp.where(mine[:, at], x, y) for x, y in zip(acc, corner[b])]
        group = jnp.where(mine, g + 1, group)
        base = base + count
    fold = (group == 4) & top
    new_count[0, 0] = base
    below = iota((8, LANES), 0) < 3
    for b, at in enumerate(blocks):
        position = jnp.concatenate(kept[b][:3], axis=0)

        def rounded(value):
            return value.astype(BF16).astype(F32)

        def sample(pos):
            pa, pb, pc = pos[0:1], pos[1:2], pos[2:3]
            near = jnp.where(below, rounded((1.0 - pb) * (1.0 - pc)), rounded((1.0 - pb) * pc))
            far = jnp.where(below, rounded(pb * (1.0 - pc)), rounded(pb * pc))
            left = near * corner[b][0] + far * corner[b][2]
            right = near * corner[b][1] + far * corner[b][3]
            mixed = (1.0 - pa) * left + pa * right
            return mixed[0:3] + mixed[3:6]

        middle = position + 0.5 * sample(position)
        moved = position + sample(middle)
        na, nb, nc = moved[0:1], moved[1:2], moved[2:3]
        g = group[:, at]
        f = fold[:, at]
        filled = slot[:, at] < base
        na = jnp.where(g == 1, na - 1.0, jnp.where(g == 2, na + 1.0, jnp.where(f, 1.0 - na, na)))
        north_b = jnp.where(f, 2.0 - nb, nb + 1.0)
        nb = jnp.where(g == 3, nb - 1.0, jnp.where(g == 4, north_b, nb))
        new_off[0, :, at] = jnp.where(filled, na, 0.0)
        new_off[1, :, at] = jnp.where(filled, nb, 0.0)
        new_off[2, :, at] = jnp.where(filled, nc, 0.0)
        ci, cj, ck = (row.astype(I32) for row in kept[b][3:])
        ci = jnp.where(
            g == 1, 0, jnp.where(g == 2, cols - 1, jnp.where(f, cols - 1 - ci, ci))
        )
        cj = jnp.where(g == 3, 0, jnp.where(g == 4, rows - 1, cj))
        new_cel[0, :, at] = jnp.where(filled, ci, 0)
        new_cel[1, :, at] = jnp.where(filled, cj, 0)
        new_cel[2, :, at] = jnp.where(filled, ck, 0)


def route(lon_size, lat_size, partner):
    pairs = []
    for p in range(lon_size):
        for r in range(lat_size):
            other = partner(p, r)
            if other is not None:
                pairs.append((p * lat_size + r, other[0] * lat_size + other[1]))
    return pairs


def shards(velocity, offsets, cells, counts, moves):
    depth, rows, cols = velocity.shape[1:]
    slots = offsets.shape[2]
    lon_size, lat_size = lax.axis_size("lon"), lax.axis_size("lat")
    axes = ("lon", "lat")
    planes = up8(3 * depth)
    stride = odd_stride(depth)
    tiles = cols // LANES
    high = tiles * planes + 4 * REC

    def send(x, partner):
        return lax.ppermute(x, axes, route(lon_size, lat_size, partner))

    def array(shape, dtype):
        return jax.ShapeDtypeStruct(shape, dtype)

    q1, q2, lonrec, record, rank0, total, zonal = pl.pallas_call(
        pack_kernel,
        out_shape=(
            array((high, LANES), BF16),
            array((high, LANES), BF16),
            array((REC, LANES), BF16),
            array((REC, slots), BF16),
            array((1, slots), I32),
            array((1, LANES), I32),
            array((depth, rows, cols), BF16),
        ),
        in_specs=[HBM, HBM, HBM, SMEM, HBM],
        out_specs=(VMEM,) * 7,
        scratch_shapes=[
            pltpu.VMEM((3, depth, 8, cols), BF16),
            pltpu.VMEM((3, depth, 8, cols), BF16),
            pltpu.VMEM((3, 1, slots), F32),
            pltpu.VMEM((3, 1, slots), I32),
            pltpu.VMEM((1, slots), I32),
            pltpu.VMEM((2 * tiles * 8 * stride, LANES), F32),
            pltpu.VMEM((REC, slots), F32),
            pltpu.VMEM((3 * up8(depth) + 8, LANES), F32),
            pltpu.SemaphoreType.DMA((2, 3)),
            pltpu.SemaphoreType.DMA((4,)),
        ],
        compiler_params=room(14),
        name="pack",
    )(*(pltpu.with_memory_space_constraint(x, pltpu.HBM) for x in (velocity, offsets, cells)), counts, pltpu.with_memory_space_constraint(moves, pltpu.HBM))

    q1r = send(q1, lambda p, r: (p, r ^ 1))

    def second(p, r):
        if r == lat_size - 1:
            return (lon_size - 1 - p, r)
        return None if r == 0 else (p, ((r + 1) ^ 1) - 1)

    q2r = send(q2, second)
    per = LANES // rows
    deep = up8(-(-depth // per))
    strips = tiles * rows + 1
    first, last, seam, table, stay, index = pl.pallas_call(
        table_kernel,
        out_shape=(
            array((planes, LANES), F32),
            array((planes, LANES), F32),
            array((planes, LANES), F32),
            array((strips * stride + 8, LANES), F32),
            array((8, slots), F32),
            array((4, slots), I32),
        ),
        in_specs=[HBM] + [VMEM] * 4,
        out_specs=(VMEM,) * 6,
        scratch_shapes=[
            pltpu.VMEM((2, depth, rows, cols), BF16),
            pltpu.VMEM((5 * deep, LANES), F32),
            pltpu.VMEM((9 * up8(per * deep), LANES), F32),
            pltpu.SemaphoreType.DMA((2,)),
        ],
        compiler_params=room(20),
        cost_estimate=pl.CostEstimate(flops=10**9, bytes_accessed=2 * velocity.size, transcendentals=0),
        name="table",
    )(pltpu.with_memory_space_constraint(velocity, pltpu.HBM), zonal, record, rank0, total)
    p1, p2 = pl.pallas_call(
        side_kernel,
        out_shape=(array((planes + REC, LANES), BF16), array((planes + REC, LANES), BF16)),
        in_specs=[VMEM] * 5,
        out_specs=(VMEM, VMEM),
        compiler_params=room(5),
        name="sides",
    )(first, last, lonrec, q1r, q2r)
    p2r = send(p2, lambda p, r: ((((p + 1) ^ 1) - 1) % lon_size, r))
    p1r = send(p1, lambda p, r: (p ^ 1, r))
    got, listed = pl.pallas_call(
        functools.partial(gather_kernel, stride),
        out_shape=(array((4, slots // LANES, 8, LANES), F32), array((slots + LANES,), I32)),
        in_specs=[VMEM, SMEM],
        out_specs=(VMEM, SMEM),
        compiler_params=room(10),
        cost_estimate=pl.CostEstimate(flops=10**9, bytes_accessed=2 * velocity.size, transcendentals=0),
        name="gather",
    )(table, index)
    return pl.pallas_call(
        functools.partial(final_kernel, rows, cols, lat_size),
        out_shape=(
            array((3, 1, slots), F32),
            array((3, 1, slots), I32),
            array((1, 1), I32),
        ),
        in_specs=[VMEM, VMEM, pl.BlockSpec(memory_space=pl.ANY)] + [VMEM] * 9,
        out_specs=(VMEM, VMEM, SMEM),
        scratch_shapes=[
            pltpu.VMEM((15 * planes + 8, LANES), F32),
            pltpu.VMEM((4, slots // LANES, 8, LANES), F32),
            pltpu.VMEM((24, LANES), F32),
            pltpu.VMEM((32, LANES), I32),
            pltpu.SMEM((32, LANES), I32),
            pltpu.VMEM((32, LANES), I32),
            pltpu.SMEM((32, LANES), I32),
            pltpu.SMEM((slots + LANES,), I32),
            pltpu.SemaphoreType.DMA((3,)),
        ],
        compiler_params=room(8),
        name="final",
    )(stay, got, listed, first, last, seam, q1, q2, q1r, q2r, p1r, p2r)


def solution(mesh):
    placed = (
        P(None, None, "lat", "lon"),
        P(None, "lat", "lon"),
        P(None, "lat", "lon"),
        P("lat", "lon"),
        P("lat", "lon"),
    )
    return jax.shard_map(
        shards,
        mesh=mesh,
        in_specs=placed,
        out_specs=(P(None, "lat", "lon"), P(None, "lat", "lon"), P("lat", "lon")),
        check_vma=False,
    )
```

```python
import functools

import jax
import jax.numpy as jnp
from jax import lax
from jax.experimental import pallas as pl
from jax.experimental.pallas import tpu as pltpu
from jax.sharding import PartitionSpec as P

CAP = 48
LANES = 128
HALF = 64
REC = 16
UNROLL = 8
SHIFT = 7
F32, BF16, I32 = jnp.float32, jnp.bfloat16, jnp.int32
VMEM = pl.BlockSpec(memory_space=pltpu.VMEM)
SMEM = pl.BlockSpec(memory_space=pltpu.SMEM)
HBM = pl.BlockSpec(memory_space=pltpu.HBM)


def room(mib):
    return pltpu.CompilerParams(vmem_limit_bytes=mib << 20)


def up8(n):
    return (n + 7) // 8 * 8


def odd_stride(depth):
    lines = 3 * depth + 8
    return lines + 1 - lines % 2


def iota(shape, dim):
    return lax.broadcasted_iota(I32, shape, dim)


def nt(a, b):
    return lax.dot_general(a, b, (((1,), (1,)), ((), ())), preferred_element_type=F32)


def pieces(value):
    high = value.astype(BF16).astype(F32)
    rest = value - high
    middle = rest.astype(BF16).astype(F32)
    return [high, middle, rest - middle]


def decode(x):
    return [x[0:1] + x[1:2] + x[2:3], x[3:4] + x[4:5] + x[5:6], x[6:7] + x[7:8] + x[8:9]]


def pack_kernel(
    vel, off, cel, counts, moves, q1, q2, lonrec, record, rank0, total, zonal,
    edge, offv, celv, movev, strips, recs, picked, sems, small,
):
    depth, rows = vel.shape[1], vel.shape[2]
    tiles = vel.shape[3] // LANES
    slots = off.shape[2]
    stride = odd_stride(depth)
    planes = up8(3 * depth)
    inputs = [
        pltpu.make_async_copy(source, target, small.at[n])
        for n, (source, target) in enumerate(((off, offv), (cel, celv), (moves, movev)))
    ]
    for copy in inputs:
        copy.start()
    copies = []
    for comp in range(3):
        copies.append(
            pltpu.make_async_copy(vel.at[comp, :, pl.ds(0, 2), :], edge.at[comp, :, pl.ds(0, 2), :], sems.at[0, comp])
        )
        copies.append(
            pltpu.make_async_copy(
                vel.at[comp, :, pl.ds(rows - 2, 2), :],
                edge.at[comp, :, pl.ds(6, 2), :],
                sems.at[1, comp],
            )
        )
    for copy in copies:
        copy.start()
    whole = pltpu.make_async_copy(vel.at[0], zonal, small.at[3])
    whole.start()
    for copy in inputs:
        copy.wait()
    live = counts[0, 0]
    rows_of = []
    for d in range(3):
        rows_of += pieces(offv[d])
    for d in range(3):
        rows_of.append(celv[d].astype(F32))
    rows_of.append(jnp.ones((1, slots), F32))
    for n, row in enumerate(rows_of):
        recs[n : n + 1, :] = row
    recs[len(rows_of) :, :] = jnp.zeros((REC - len(rows_of), slots), F32)
    packed = recs[...].astype(BF16)
    record[...] = packed
    chosen = (movev[...] == iota((8, slots), 0)) & (iota((8, slots), 1) < live)
    ones = chosen.astype(F32)
    scan_of = jnp.where(
        (iota((LANES, 2 * LANES), 0) < iota((LANES, 2 * LANES), 1))
        | (iota((LANES, 2 * LANES), 1) >= LANES),
        1.0,
        0.0,
    ).astype(BF16)
    carry = jnp.zeros((8, LANES), F32)
    ranks = []
    for block in range(slots // LANES):
        piece = ones[:, block * LANES : (block + 1) * LANES].astype(BF16)
        scanned = jnp.dot(piece, scan_of, preferred_element_type=F32)
        ranks.append(scanned[:, :LANES] + carry)
        carry = carry + scanned[:, LANES:]
    rank = jnp.where(chosen, jnp.concatenate(ranks, axis=1), -1.0).astype(I32)
    rank0[...] = rank[0:1]
    target = iota((HALF, slots), 0)
    placing = [
        jnp.where(rank[g : g + 1] == target, 1.0, 0.0).astype(BF16) for g in range(1, 5)
    ]
    lonrec[...] = nt(packed, jnp.concatenate(placing[:2], axis=0)).astype(BF16)
    latrec = nt(packed, jnp.concatenate(placing[2:], axis=0))
    total[...] = carry[0:1, :].astype(I32)
    for comp in range(3):
        copies[2 * comp].wait()
        copies[2 * comp + 1].wait()

        def spread(k, _):
            value = edge[comp, k].astype(F32)
            for tile in range(tiles):
                first = tile * 8 * stride + 3 * k + comp
                strips[pl.ds(first, 8, stride=stride), :] = value[
                    :, tile * LANES : (tile + 1) * LANES
                ]
            return 0

        lax.fori_loop(0, depth, spread, 0, unroll=15)
    seconds = [
        strips[pl.ds((tile * 8 + 1) * stride, planes), :].astype(BF16) for tile in range(tiles)
    ]
    lane = iota((1, LANES), 1)
    south_i, south_k = latrec[9:10], latrec[11:12]
    column = jnp.where(lane < HALF, pltpu.roll(south_i, HALF, 1), south_i + 1.0).astype(I32)
    level = jnp.where(lane < HALF, pltpu.roll(south_k, HALF, 1), south_k).astype(I32)
    at_column = jnp.zeros((planes, LANES), F32)
    for tile in range(tiles):
        where = jnp.where(iota((LANES, LANES), 0) + tile * LANES == column, 1.0, 0.0).astype(BF16)
        at_column = at_column + jnp.dot(seconds[tile], where, preferred_element_type=F32)
    picked[0:planes, :] = at_column
    deep = up8(depth)
    carried = []
    for step in range(2):
        for comp in range(3):
            lines = picked[pl.ds(comp, deep, stride=3), :]
            there = iota((deep, LANES), 0) == level + step
            carried.append(jnp.sum(jnp.where(there, lines, 0.0), axis=0, keepdims=True))
    for n, row in enumerate(carried):
        recs[n : n + 1, 0:LANES] = row
    corner = nt(jnp.where(iota((REC, LANES), 1) == 0, 1.0, 0.0).astype(BF16), seconds[0])
    recs[6:7, 0:LANES] = corner[0:1, 0:LANES]
    recs[7:8, 0:LANES] = jnp.zeros((1, LANES), F32)
    recs[7:8, 0 : planes - LANES] = corner[0:1, LANES:planes]
    odd = lax.rem(lax.axis_index("lat"), 2)
    for n, out in enumerate((q1, q2)):
        upper = odd if n == 0 else 1 - odd
        for tile in range(tiles):
            last = (tile * 8 + 7) * stride
            first = jnp.where(upper == 1, tile * 8 * stride, last)
            out[tile * planes : (tile + 1) * planes, :] = strips[pl.ds(first, planes), :].astype(BF16)
        at = tiles * planes
        out[at : at + REC, :] = latrec.astype(BF16)
        out[at + REC :, :] = recs[0:8, 0:LANES].astype(BF16)
    whole.wait()


def table_kernel(
    source, zonal, record, rank0, total, first, last, seam, table, stay, index, vel, lines, wide, sems
):
    depth, rows, cols = vel.shape[1:]
    copies = [
        pltpu.make_async_copy(source.at[comp + 1], vel.at[comp], sems.at[comp]) for comp in range(2)
    ]
    for copy in copies:
        copy.start()
    slots = record.shape[1]
    tiles = cols // LANES
    planes = up8(3 * depth)
    stride = odd_stride(depth)
    r, c = iota((REC, cols), 0), iota((REC, cols), 1)
    pick = (r == c) & (r < 2)
    pick = pick | ((r == 2) & (c == cols - 1)) | ((r == c - LANES + 4) & (r >= 3) & (r < 5))
    select = jnp.where(pick, 1.0, 0.0).astype(BF16)
    per = LANES // rows
    chunks = -(-depth // per)
    deep = up8(chunks)
    lane = iota((deep, LANES), 1)
    target = iota((LANES, slots), 0)
    packed = record[...]
    rank = rank0[...]
    for block in range(slots // LANES):
        where = jnp.where(rank - block * LANES == target, 1.0, 0.0).astype(BF16)
        out = nt(packed, where)
        lanes = slice(block * LANES, (block + 1) * LANES)
        for d, row in enumerate(decode(out)):
            stay[d : d + 1, lanes] = row
        stay[3:6, lanes] = out[9:12]
        stay[6:8, lanes] = out[12:14]
    i, j, k = (stay[n : n + 1, :].astype(I32) for n in (3, 4, 5))
    slot = iota((1, slots), 1)
    index[0:1, :] = ((i >> SHIFT) * rows + j) * stride + 3 * k
    index[1:2, :] = (slot - i) & (LANES - 1)
    odd_one = (((i & (LANES - 1)) == LANES - 1) | (j == rows - 1)) & (slot < jnp.tile(total[...], (1, slots // LANES)))
    index[2:3, :] = odd_one.astype(I32)
    index[3:4, :] = jnp.tile(total[...], (1, slots // LANES))
    for comp in range(3):
        if comp > 0:
            copies[comp - 1].wait()
        block = vel.at[comp - 1] if comp > 0 else zonal
        got = nt(select, block[...].reshape(depth * rows, cols))
        for n in range(5):
            for q in range(chunks):
                size = min(LANES, depth * rows - q * LANES)
                lines[n * deep + q : n * deep + q + 1, 0:size] = got[
                    n : n + 1, q * LANES : q * LANES + size
                ]
        for m in range(per):

            def line(n, to):
                at = lines[n * deep : (n + 1) * deep, :]
                return pltpu.roll(at, (LANES + to - rows * m) % LANES, 1)

            values = (
                jnp.where(lane < HALF, line(0, 0), line(1, HALF)),
                line(2, 0),
                jnp.where(lane < HALF, line(3, 0), line(4, HALF)),
            )
            for n, value in enumerate(values):
                for q in range(0, deep, 8):
                    at = pl.ds(n * wide.shape[0] // 3 + 3 * (per * q + m) + comp, 8, stride=3 * per)
                    wide[at, :] = value[q : q + 8]
        def fill(k, _):
            value = block[k].astype(F32)
            for tile in range(tiles):
                for r in range(0, rows, 8):
                    at = pl.ds((tile * rows + r) * stride + 3 * k + comp, 8, stride=stride)
                    table[at, :] = value[r : r + 8, tile * LANES : (tile + 1) * LANES]
            return 0

        lax.fori_loop(0, depth, fill, 0, unroll=5)
    for n, out in enumerate((first, last, seam)):
        at = n * wide.shape[0] // 3
        out[...] = wide[at : at + planes, :]


def gather_kernel(stride, table, index, got, listed):
    lane = iota((8, LANES), 1)
    count = index[3, 0]
    slots = index.shape[1]

    def block_of(b, n):
        acc = [jnp.zeros((8, LANES), F32)] * 4
        for p in range(LANES):
            s = b * LANES + p
            row = index[0, s]
            shift = index[1, s]
            low = pltpu.roll(table[pl.ds(row, 8), :], shift, 1)
            high = pltpu.roll(table[pl.ds(row + stride, 8), :], shift, 1)
            here = lane == p
            beside = lane == ((p + 1) % LANES)
            acc = [
                jnp.where(here, low, acc[0]),
                jnp.where(beside, low, acc[1]),
                jnp.where(here, high, acc[2]),
                jnp.where(beside, high, acc[3]),
            ]
            listed[n] = s
            n = n + index[2, s]
        got[0, b] = acc[0]
        got[1, b] = pltpu.roll(acc[1], LANES - 1, 1)
        got[2, b] = acc[2]
        got[3, b] = pltpu.roll(acc[3], LANES - 1, 1)
        return n

    full = (count + LANES - 1) >> SHIFT
    listed[slots + 8] = lax.fori_loop(0, full, block_of, I32(0))
    listed[slots + 9] = count


def group_places(rows, cols, planes, g, top, raw, lines):
    i, j, k = (raw[n : n + 1].astype(I32) for n in (9, 10, 11))
    y0 = (j, j, jnp.full_like(j, -1), jnp.full_like(j, rows))[g]
    x0 = (jnp.full_like(i, -1), jnp.full_like(i, cols), i, i)[g]
    e, signs = places(rows, cols, planes, jnp.full_like(i, g + 1), top, y0, x0, k)
    half = lines.shape[0] // 2
    for q in range(4):
        row = 4 * (g % (half // 4)) + q
        lines[row : row + 1, :] = e[q] >> SHIFT
        lines[half + row : half + row + 1, :] = (iota((1, LANES), 1) - e[q]) & (LANES - 1)
    return signs


def group_corner(table, lines, row):
    lane = iota((8, LANES), 1)
    half = lines.shape[0] // 2
    total = jnp.zeros((8, LANES), F32)
    for t in range(CAP):
        value = pltpu.roll(table[pl.ds(lines[row, t], 8), :], lines[half + row, t], 1)
        total = jnp.where(lane == t, value, total)
    return total


def lat_records(planes, top, even_lat, q1r, q2r):
    at = slice(2 * planes, 2 * planes + REC)
    inside = iota((REC, LANES), 1) < HALF
    srec = jnp.where(even_lat, q2r[at, :], q1r[at, :]).astype(F32)
    nrec = jnp.where(even_lat, q1r[at, :], q2r[at, :]).astype(F32)
    nrec = jnp.where(top, nrec, pltpu.roll(nrec, HALF, 1))
    return jnp.where(inside, srec, 0.0), jnp.where(inside, nrec, 0.0)


def put_rows(table, planes, even_lat, q1, q2, q1r, q2r, first, last, seam):
    def put(n, value):
        table[n * planes : (n + 1) * planes, :] = value

    def pick(a, b, at):
        at = slice(at, at + planes)
        return jnp.where(even_lat, a[at, :], b[at, :]).astype(F32)

    for t in range(2):
        put(t, pick(q2, q1, t * planes))
        put(2 + t, pick(q1, q2, t * planes))
        put(4 + t, pick(q1r, q2r, t * planes))
        put(8 + t, pick(q2r, q1r, t * planes))
    put(10, first[...])
    put(11, last[...])
    put(14, seam[...])


def side_kernel(first, last, lonrec, q1r, q2r, p1, p2):
    planes = first.shape[0]
    even_lat = lax.rem(lax.axis_index("lat"), 2) == 0
    odd_lon = lax.rem(lax.axis_index("lon"), 2)
    lane = iota((planes, LANES), 1)

    def strip(north, n):
        a = q1r[n * planes : (n + 1) * planes, :].astype(F32)
        b = q2r[n * planes : (n + 1) * planes, :].astype(F32)
        return jnp.where(even_lat == north, a, b)

    north0, north1, south0 = strip(True, 0), strip(True, 1), strip(False, 0)
    second0 = []
    at = slice(2 * planes + REC, 2 * planes + REC + 8)
    lines = jnp.where(even_lat, q1r[at, :], q2r[at, :]).astype(F32)
    for n in range(2):
        line = jnp.broadcast_to(lines[6 + n : 7 + n], (LANES, LANES))
        second0.append(jnp.transpose(line))
    second0 = jnp.concatenate([second0[0], second0[1][0 : planes - LANES]], axis=0)
    west = first[...]
    west = jnp.where(lane == 32, pltpu.roll(north0, 32, 1), west)
    west = jnp.where(lane == 33, second0, west)
    west = jnp.where(lane == 34, pltpu.roll(south0, 34, 1), west)
    west = jnp.where(lane == 35, pltpu.roll(north1, 36, 1), west)
    west = jnp.where(lane == 96, pltpu.roll(north0, 95, 1), west).astype(BF16)
    east = last[...]
    east = jnp.where(lane == 32, pltpu.roll(north1, 33, 1), east)
    east = jnp.where((lane == 33) | (lane == 34), pltpu.roll(north0, 33, 1), east).astype(BF16)
    p1[0:planes, :] = jnp.where(odd_lon == 1, west, east)
    p2[0:planes, :] = jnp.where(odd_lon == 1, east, west)
    p1[planes:, :] = lonrec[...]
    p2[planes:, :] = lonrec[...]


def places(rows, cols, planes, group, top, y0, x0, k):
    fold = (group == 4) & top
    found, signs = [], []

    def flat(strip, at):
        return strip * (planes * LANES) + at

    def row_at(strip, at):
        return flat(strip + (at >> SHIFT), at & (LANES - 1))

    for dj, di in ((0, 0), (0, 1), (1, 0), (1, 1)):
        y = y0 + dj
        x = x0 + di
        inner = row_at(jnp.where(y == 0, 0, 2), x)
        inner = jnp.where(x == LANES - 1, flat(14, y), inner)
        inner = jnp.where(x == LANES, flat(14, HALF + y), inner)
        inner = jnp.where(x == 0, flat(10, y), inner)
        inner = jnp.where(x == cols - 1, flat(11, y), inner)
        inner = jnp.where(x > cols, flat(12, HALF + y), inner)
        inner = jnp.where(x == cols, flat(12, y), inner)
        inner = jnp.where(x < 0, flat(13, y), inner)
        north = jnp.where(
            x < 0,
            flat(13, 32),
            jnp.where(x == cols, flat(12, 32), jnp.where(x > cols, flat(12, 96), row_at(4, x))),
        )
        u = cols - x
        folded = jnp.where(
            u < 0,
            flat(12, 35),
            jnp.where(u == cols, flat(13, 33), jnp.where(u > cols, flat(13, 34), row_at(4, u))),
        )
        second = flat(12, 33)
        south = jnp.where(x == cols, flat(12, 34), row_at(8, x))
        where = jnp.where(
            y < 0,
            south,
            jnp.where(y > rows, second, jnp.where(y == rows, jnp.where(top, folded, north), inner)),
        )
        if dj == 0:
            across = jnp.where(x == cols, flat(13, 33), row_at(4, x))
            signs.append(jnp.ones(x0.shape, F32))
        else:
            across = jnp.where(u == cols, flat(12, rows - 1), row_at(2, u))
            signs.append(jnp.where(top & (fold | (y == rows)), -1.0, 1.0))
        found.append(jnp.where(fold, across, where) + 3 * LANES * k)
    return found, signs


def final_kernel(
    rows, cols, lat_size,
    stay, got, listed_any, first, last, seam, q1, q2, q1r, q2r, p1r, p2r,
    new_off, new_cel, new_count,
    table, values_of, packed, idxv, idxs, idxt, idxlv, idxl, listed, isem,
):
    planes = first.shape[0]
    slots = stay.shape[1]
    lat = lax.axis_index("lat")
    even_lat = lax.rem(lat, 2) == 0
    even_lon = lax.rem(lax.axis_index("lon"), 2) == 0
    top = lat == lat_size - 1
    both = 2 * planes

    def pick(flag, a, b, at, size):
        return jnp.where(flag, a[at : at + size, :], b[at : at + size, :]).astype(F32)

    slot = iota((1, slots), 1)
    copy_list = pltpu.make_async_copy(listed_any, listed, isem.at[2])
    copy_list.start()
    blocks = [slice(b * LANES, (b + 1) * LANES) for b in range(slots // LANES)]
    packed[...] = jnp.zeros(packed.shape, F32)
    for n in range(3):
        for b, at in enumerate(blocks):
            packed[8 * n + b : 8 * n + b + 1, :] = stay[3 + n : 4 + n, at]
    here = [packed[8 * n : 8 * n + 8, :].astype(I32) for n in range(3)]
    e, stay_signs = places(
        rows, cols, planes, jnp.zeros((8, LANES), I32), top, here[1], here[0], here[2]
    )
    for q in range(4):
        idxlv[8 * q : 8 * q + 8, :] = e[q]
    copy_listed = pltpu.make_async_copy(idxlv, idxl, isem.at[3])
    copy_listed.start()
    inside = iota((REC, LANES), 1) < HALF
    wrec = pick(even_lon, p2r, p1r, planes, REC)
    erec = pltpu.roll(pick(even_lon, p1r, p2r, planes, REC), HALF, 1)
    srec, nrec = lat_records(planes, top, even_lat, q1r, q2r)
    carried = pick(even_lat, q1r, q2r, both + REC, 8)
    groups = [None] * 4
    copies = []
    for pair, raws in ((1, (srec, nrec)), (0, (wrec, erec))):
        lines = idxv.at[pair]
        for n, raw in enumerate(raws):
            g = 2 * pair + n
            raw = jnp.where(inside, raw, 0.0)
            signs = group_places(rows, cols, planes, g, top, raw, lines)
            groups[g] = (raw, jnp.sum(raw[12:13]).astype(I32), signs)
        copies.append(pltpu.make_async_copy(lines, (idxs, idxt)[pair], isem.at[pair]))
        copies[-1].start()
    values_of[...] = got[...]
    put_rows(table, planes, even_lat, q1, q2, q1r, q2r, first, last, seam)
    table[12 * planes : 13 * planes, :] = pick(even_lon, p1r, p2r, 0, planes)
    table[13 * planes : 14 * planes, :] = pick(even_lon, p2r, p1r, 0, planes)
    lane = iota((8, LANES), 1)
    copy_listed.wait()
    copy_list.wait()
    found = listed[slots + 8]

    def patch_listed(n, _):
        chosen = [listed[jnp.minimum(n * UNROLL + u, found - 1)] for u in range(UNROLL)]
        values = []
        for s in chosen:
            for q in range(4):
                e = idxl[8 * q + (s >> SHIFT), s & (LANES - 1)]
                line = table[pl.ds(e >> SHIFT, 8), :]
                values.append(pltpu.roll(line, (s - e) & (LANES - 1), 1))
        for s in chosen:
            mask = lane == (s & (LANES - 1))
            for q in range(4):
                pltpu.store(values_of.at[q, s >> SHIFT], values.pop(0), mask=mask)
        return 0

    lax.fori_loop(0, lax.div(found + (UNROLL - 1), UNROLL), patch_listed, 0)
    corners = [None] * 4
    for pair in (1, 0):
        copies[1 - pair].wait()
        for n in range(2):
            lines = (idxs, idxt)[pair]
            corners[2 * pair + n] = [group_corner(table, lines, 4 * n + q) for q in range(4)]
    base = listed[slots + 9]
    own = slot < base
    corner = [
        [values_of[n, b] * stay_signs[n][b : b + 1] for n in range(4)] for b in range(len(blocks))
    ]
    kept = [[jnp.where(own[:, at], stay[n : n + 1, at], 0.0) for n in range(6)] for at in blocks]
    group = jnp.zeros((1, slots), I32)
    for g, (raw, count, signs) in enumerate(groups):
        acc = []
        for q in range(4):
            total = corners[g][q]
            if g == 3 and q > 1:
                sent = carried if q == 2 else pltpu.roll(carried, HALF, 1)
                beyond = top if q == 2 else top | (raw[9:10].astype(I32) == cols - 1)
                total = jnp.where(beyond, total, sent)
            acc.append(pltpu.roll(total * signs[q], base & (LANES - 1), 1))
        moved = pltpu.roll(raw, base & (LANES - 1), 1)
        values = decode(moved) + [moved[9:10], moved[10:11], moved[11:12]]
        mine = (slot >= base) & (slot < base + count)
        for b, at in enumerate(blocks):
            kept[b] = [jnp.where(mine[:, at], x, y) for x, y in zip(values, kept[b])]
            corner[b] = [jnp.where(mine[:, at], x, y) for x, y in zip(acc, corner[b])]
        group = jnp.where(mine, g + 1, group)
        base = base + count
    fold = (group == 4) & top
    new_count[0, 0] = base
    below = iota((8, LANES), 0) < 3
    for b, at in enumerate(blocks):
        position = jnp.concatenate(kept[b][:3], axis=0)

        def rounded(value):
            return value.astype(BF16).astype(F32)

        def sample(pos):
            pa, pb, pc = pos[0:1], pos[1:2], pos[2:3]
            near = jnp.where(below, rounded((1.0 - pb) * (1.0 - pc)), rounded((1.0 - pb) * pc))
            far = jnp.where(below, rounded(pb * (1.0 - pc)), rounded(pb * pc))
            left = near * corner[b][0] + far * corner[b][2]
            right = near * corner[b][1] + far * corner[b][3]
            mixed = (1.0 - pa) * left + pa * right
            return mixed[0:3] + mixed[3:6]

        middle = position + 0.5 * sample(position)
        moved = position + sample(middle)
        na, nb, nc = moved[0:1], moved[1:2], moved[2:3]
        g = group[:, at]
        f = fold[:, at]
        filled = slot[:, at] < base
        na = jnp.where(g == 1, na - 1.0, jnp.where(g == 2, na + 1.0, jnp.where(f, 1.0 - na, na)))
        north_b = jnp.where(f, 2.0 - nb, nb + 1.0)
        nb = jnp.where(g == 3, nb - 1.0, jnp.where(g == 4, north_b, nb))
        new_off[0, :, at] = jnp.where(filled, na, 0.0)
        new_off[1, :, at] = jnp.where(filled, nb, 0.0)
        new_off[2, :, at] = jnp.where(filled, nc, 0.0)
        ci, cj, ck = (row.astype(I32) for row in kept[b][3:])
        ci = jnp.where(
            g == 1, 0, jnp.where(g == 2, cols - 1, jnp.where(f, cols - 1 - ci, ci))
        )
        cj = jnp.where(g == 3, 0, jnp.where(g == 4, rows - 1, cj))
        new_cel[0, :, at] = jnp.where(filled, ci, 0)
        new_cel[1, :, at] = jnp.where(filled, cj, 0)
        new_cel[2, :, at] = jnp.where(filled, ck, 0)


def route(lon_size, lat_size, partner):
    pairs = []
    for p in range(lon_size):
        for r in range(lat_size):
            other = partner(p, r)
            if other is not None:
                pairs.append((p * lat_size + r, other[0] * lat_size + other[1]))
    return pairs


def shards(velocity, offsets, cells, counts, moves):
    depth, rows, cols = velocity.shape[1:]
    slots = offsets.shape[2]
    lon_size, lat_size = lax.axis_size("lon"), lax.axis_size("lat")
    axes = ("lon", "lat")
    planes = up8(3 * depth)
    stride = odd_stride(depth)
    tiles = cols // LANES
    high = tiles * planes + REC + 8

    def send(x, partner):
        return lax.ppermute(x, axes, route(lon_size, lat_size, partner))

    def array(shape, dtype):
        return jax.ShapeDtypeStruct(shape, dtype)

    q1, q2, lonrec, record, rank0, total, zonal = pl.pallas_call(
        pack_kernel,
        out_shape=(
            array((high, LANES), BF16),
            array((high, LANES), BF16),
            array((REC, LANES), BF16),
            array((REC, slots), BF16),
            array((1, slots), I32),
            array((1, LANES), I32),
            array((depth, rows, cols), BF16),
        ),
        in_specs=[HBM, HBM, HBM, SMEM, HBM],
        out_specs=(VMEM,) * 7,
        scratch_shapes=[
            pltpu.VMEM((3, depth, 8, cols), BF16),
            pltpu.VMEM((3, 1, slots), F32),
            pltpu.VMEM((3, 1, slots), I32),
            pltpu.VMEM((1, slots), I32),
            pltpu.VMEM((tiles * 8 * stride, LANES), F32),
            pltpu.VMEM((REC, slots), F32),
            pltpu.VMEM((3 * up8(depth) + 8, LANES), F32),
            pltpu.SemaphoreType.DMA((2, 3)),
            pltpu.SemaphoreType.DMA((4,)),
        ],
        compiler_params=room(14),
        name="pack",
    )(*(pltpu.with_memory_space_constraint(x, pltpu.HBM) for x in (velocity, offsets, cells)), counts, pltpu.with_memory_space_constraint(moves, pltpu.HBM))

    q1r = send(q1, lambda p, r: (p, r ^ 1))

    def second(p, r):
        if r == lat_size - 1:
            return (lon_size - 1 - p, r)
        return None if r == 0 else (p, ((r + 1) ^ 1) - 1)

    q2r = send(q2, second)
    per = LANES // rows
    deep = up8(-(-depth // per))
    strips = tiles * rows + 1
    first, last, seam, table, stay, index = pl.pallas_call(
        table_kernel,
        out_shape=(
            array((planes, LANES), F32),
            array((planes, LANES), F32),
            array((planes, LANES), F32),
            array((strips * stride + 8, LANES), F32),
            array((8, slots), F32),
            array((4, slots), I32),
        ),
        in_specs=[HBM] + [VMEM] * 4,
        out_specs=(VMEM,) * 6,
        scratch_shapes=[
            pltpu.VMEM((2, depth, rows, cols), BF16),
            pltpu.VMEM((5 * deep, LANES), F32),
            pltpu.VMEM((9 * up8(per * deep), LANES), F32),
            pltpu.SemaphoreType.DMA((2,)),
        ],
        compiler_params=room(20),
        cost_estimate=pl.CostEstimate(flops=10**9, bytes_accessed=2 * velocity.size, transcendentals=0),
        name="table",
    )(pltpu.with_memory_space_constraint(velocity, pltpu.HBM), zonal, record, rank0, total)
    p1, p2 = pl.pallas_call(
        side_kernel,
        out_shape=(array((planes + REC, LANES), BF16), array((planes + REC, LANES), BF16)),
        in_specs=[VMEM] * 5,
        out_specs=(VMEM, VMEM),
        compiler_params=room(5),
        name="sides",
    )(first, last, lonrec, q1r, q2r)
    p2r = send(p2, lambda p, r: ((((p + 1) ^ 1) - 1) % lon_size, r))
    p1r = send(p1, lambda p, r: (p ^ 1, r))
    got, listed = pl.pallas_call(
        functools.partial(gather_kernel, stride),
        out_shape=(array((4, slots // LANES, 8, LANES), F32), array((slots + LANES,), I32)),
        in_specs=[VMEM, SMEM],
        out_specs=(VMEM, SMEM),
        compiler_params=room(10),
        cost_estimate=pl.CostEstimate(flops=10**9, bytes_accessed=2 * velocity.size, transcendentals=0),
        name="gather",
    )(table, index)
    return pl.pallas_call(
        functools.partial(final_kernel, rows, cols, lat_size),
        out_shape=(
            array((3, 1, slots), F32),
            array((3, 1, slots), I32),
            array((1, 1), I32),
        ),
        in_specs=[VMEM, VMEM, pl.BlockSpec(memory_space=pl.ANY)] + [VMEM] * 9,
        out_specs=(VMEM, VMEM, SMEM),
        scratch_shapes=[
            pltpu.VMEM((15 * planes + 8, LANES), F32),
            pltpu.VMEM((4, slots // LANES, 8, LANES), F32),
            pltpu.VMEM((24, LANES), F32),
            pltpu.VMEM((2, 16, LANES), I32),
            pltpu.SMEM((16, LANES), I32),
            pltpu.SMEM((16, LANES), I32),
            pltpu.VMEM((32, LANES), I32),
            pltpu.SMEM((32, LANES), I32),
            pltpu.SMEM((slots + LANES,), I32),
            pltpu.SemaphoreType.DMA((4,)),
        ],
        compiler_params=room(8),
        name="final",
    )(stay, got, listed, first, last, seam, q1, q2, q1r, q2r, p1r, p2r)


def solution(mesh):
    placed = (
        P(None, None, "lat", "lon"),
        P(None, "lat", "lon"),
        P(None, "lat", "lon"),
        P("lat", "lon"),
        P("lat", "lon"),
    )
    return jax.shard_map(
        shards,
        mesh=mesh,
        in_specs=placed,
        out_specs=(P(None, "lat", "lon"), P(None, "lat", "lon"), P("lat", "lon")),
        check_vma=False,
    )
```

```python
import functools

import jax
import jax.numpy as jnp
from jax import lax
from jax.experimental import pallas as pl
from jax.experimental.pallas import tpu as pltpu
from jax.sharding import PartitionSpec as P

CAP = 48
LANES = 128
HALF = 64
REC = 16
UNROLL = 8
SHIFT = 7
F32, BF16, I32 = jnp.float32, jnp.bfloat16, jnp.int32
VMEM = pl.BlockSpec(memory_space=pltpu.VMEM)
SMEM = pl.BlockSpec(memory_space=pltpu.SMEM)
HBM = pl.BlockSpec(memory_space=pltpu.HBM)


def room(mib):
    return pltpu.CompilerParams(vmem_limit_bytes=mib << 20)


def up8(n):
    return (n + 7) // 8 * 8


def reach_of(slots):
    return -(-(slots - 4 * CAP) // LANES) * LANES


def odd_stride(depth):
    lines = 3 * depth + 8
    return lines + 1 - lines % 2


def iota(shape, dim):
    return lax.broadcasted_iota(I32, shape, dim)


def nt(a, b):
    return lax.dot_general(a, b, (((1,), (1,)), ((), ())), preferred_element_type=F32)


def pieces(value):
    high = value.astype(BF16).astype(F32)
    rest = value - high
    middle = rest.astype(BF16).astype(F32)
    return [high, middle, rest - middle]


def decode(x):
    return [x[0:1] + x[1:2] + x[2:3], x[3:4] + x[4:5] + x[5:6], x[6:7] + x[7:8] + x[8:9]]


def pack_kernel(
    vel, off, cel, counts, moves, q1, q2, lonrec, record, rank0, total, zonal,
    edge, offv, celv, movev, strips, recs, picked, sems, small,
):
    depth, rows = vel.shape[1], vel.shape[2]
    tiles = vel.shape[3] // LANES
    slots = reach_of(off.shape[2])
    stride = odd_stride(depth)
    planes = up8(3 * depth)
    inputs = [
        pltpu.make_async_copy(source, target, small.at[n])
        for n, (source, target) in enumerate(((off, offv), (cel, celv), (moves, movev)))
    ]
    for copy in inputs:
        copy.start()
    copies = []
    for comp in range(3):
        copies.append(
            pltpu.make_async_copy(vel.at[comp, :, pl.ds(0, 2), :], edge.at[comp, :, pl.ds(0, 2), :], sems.at[0, comp])
        )
        copies.append(
            pltpu.make_async_copy(
                vel.at[comp, :, pl.ds(rows - 2, 2), :],
                edge.at[comp, :, pl.ds(6, 2), :],
                sems.at[1, comp],
            )
        )
    for copy in copies:
        copy.start()
    whole = pltpu.make_async_copy(vel.at[0], zonal, small.at[3])
    whole.start()
    for copy in inputs:
        copy.wait()
    live = counts[0, 0]
    rows_of = []
    for d in range(3):
        rows_of += pieces(offv[d][:, 0:slots])
    for d in range(3):
        rows_of.append(celv[d][:, 0:slots].astype(F32))
    rows_of.append(jnp.ones((1, slots), F32))
    for n, row in enumerate(rows_of):
        recs[n : n + 1, :] = row
    recs[len(rows_of) :, :] = jnp.zeros((REC - len(rows_of), slots), F32)
    packed = recs[...].astype(BF16)
    record[...] = packed
    chosen = (movev[:, 0:slots] == iota((8, slots), 0)) & (iota((8, slots), 1) < live)
    ones = chosen.astype(F32)
    scan_of = jnp.where(
        (iota((LANES, 2 * LANES), 0) < iota((LANES, 2 * LANES), 1))
        | (iota((LANES, 2 * LANES), 1) >= LANES),
        1.0,
        0.0,
    ).astype(BF16)
    carry = jnp.zeros((8, LANES), F32)
    ranks = []
    for block in range(slots // LANES):
        piece = ones[:, block * LANES : (block + 1) * LANES].astype(BF16)
        scanned = jnp.dot(piece, scan_of, preferred_element_type=F32)
        ranks.append(scanned[:, :LANES] + carry)
        carry = carry + scanned[:, LANES:]
    rank = jnp.where(chosen, jnp.concatenate(ranks, axis=1), -1.0).astype(I32)
    rank0[...] = rank[0:1]
    target = iota((HALF, slots), 0)
    placing = [
        jnp.where(rank[g : g + 1] == target, 1.0, 0.0).astype(BF16) for g in range(1, 5)
    ]
    lonrec[...] = nt(packed, jnp.concatenate(placing[:2], axis=0)).astype(BF16)
    latrec = nt(packed, jnp.concatenate(placing[2:], axis=0))
    total[...] = carry[0:1, :].astype(I32)
    for comp in range(3):
        copies[2 * comp].wait()
        copies[2 * comp + 1].wait()

        def spread(k, _):
            value = edge[comp, k].astype(F32)
            for tile in range(tiles):
                first = tile * 8 * stride + 3 * k + comp
                strips[pl.ds(first, 8, stride=stride), :] = value[
                    :, tile * LANES : (tile + 1) * LANES
                ]
            return 0

        lax.fori_loop(0, depth, spread, 0, unroll=15)
    seconds = [
        strips[pl.ds((tile * 8 + 1) * stride, planes), :].astype(BF16) for tile in range(tiles)
    ]
    lane = iota((1, LANES), 1)
    south_i, south_k = latrec[9:10], latrec[11:12]
    column = jnp.where(lane < HALF, pltpu.roll(south_i, HALF, 1), south_i + 1.0).astype(I32)
    level = jnp.where(lane < HALF, pltpu.roll(south_k, HALF, 1), south_k).astype(I32)
    at_column = jnp.zeros((planes, LANES), F32)
    for tile in range(tiles):
        where = jnp.where(iota((LANES, LANES), 0) + tile * LANES == column, 1.0, 0.0).astype(BF16)
        at_column = at_column + jnp.dot(seconds[tile], where, preferred_element_type=F32)
    picked[0:planes, :] = at_column
    deep = up8(depth)
    carried = []
    for step in range(2):
        for comp in range(3):
            lines = picked[pl.ds(comp, deep, stride=3), :]
            there = iota((deep, LANES), 0) == level + step
            carried.append(jnp.sum(jnp.where(there, lines, 0.0), axis=0, keepdims=True))
    for n, row in enumerate(carried):
        recs[n : n + 1, 0:LANES] = row
    corner = nt(jnp.where(iota((REC, LANES), 1) == 0, 1.0, 0.0).astype(BF16), seconds[0])
    recs[6:7, 0:LANES] = corner[0:1, 0:LANES]
    recs[7:8, 0:LANES] = jnp.zeros((1, LANES), F32)
    recs[7:8, 0 : planes - LANES] = corner[0:1, LANES:planes]
    odd = lax.rem(lax.axis_index("lat"), 2)
    for n, out in enumerate((q1, q2)):
        upper = odd if n == 0 else 1 - odd
        for tile in range(tiles):
            last = (tile * 8 + 7) * stride
            first = jnp.where(upper == 1, tile * 8 * stride, last)
            out[tile * planes : (tile + 1) * planes, :] = strips[pl.ds(first, planes), :].astype(BF16)
        at = tiles * planes
        out[at : at + REC, :] = latrec.astype(BF16)
        out[at + REC :, :] = recs[0:8, 0:LANES].astype(BF16)
    whole.wait()


def table_kernel(
    source, zonal, record, rank0, total, first, last, seam, table, stay, index, vel, lines, wide, sems
):
    depth, rows, cols = vel.shape[1:]
    copies = [
        pltpu.make_async_copy(source.at[comp + 1], vel.at[comp], sems.at[comp]) for comp in range(2)
    ]
    for copy in copies:
        copy.start()
    reach, slots = record.shape[1], stay.shape[1]
    tiles = cols // LANES
    planes = up8(3 * depth)
    stride = odd_stride(depth)
    r, c = iota((REC, cols), 0), iota((REC, cols), 1)
    pick = (r == c) & (r < 2)
    pick = pick | ((r == 2) & (c == cols - 1)) | ((r == c - LANES + 4) & (r >= 3) & (r < 5))
    select = jnp.where(pick, 1.0, 0.0).astype(BF16)
    per = LANES // rows
    chunks = -(-depth // per)
    deep = up8(chunks)
    lane = iota((deep, LANES), 1)
    target = iota((LANES, reach), 0)
    stay[:, reach:] = jnp.zeros((8, slots - reach), F32)
    packed = record[...]
    rank = rank0[...]
    for block in range(reach // LANES):
        where = jnp.where(rank - block * LANES == target, 1.0, 0.0).astype(BF16)
        out = nt(packed, where)
        lanes = slice(block * LANES, (block + 1) * LANES)
        for d, row in enumerate(decode(out)):
            stay[d : d + 1, lanes] = row
        stay[3:6, lanes] = out[9:12]
        stay[6:8, lanes] = out[12:14]
    i, j, k = (stay[n : n + 1, :].astype(I32) for n in (3, 4, 5))
    slot = iota((1, slots), 1)
    index[0:1, :] = ((i >> SHIFT) * rows + j) * stride + 3 * k
    index[1:2, :] = (slot - i) & (LANES - 1)
    odd_one = (((i & (LANES - 1)) == LANES - 1) | (j == rows - 1)) & (slot < jnp.tile(total[...], (1, slots // LANES)))
    index[2:3, :] = odd_one.astype(I32)
    index[3:4, :] = jnp.tile(total[...], (1, slots // LANES))
    for comp in range(3):
        if comp > 0:
            copies[comp - 1].wait()
        block = vel.at[comp - 1] if comp > 0 else zonal
        got = nt(select, block[...].reshape(depth * rows, cols))
        for n in range(5):
            for q in range(chunks):
                size = min(LANES, depth * rows - q * LANES)
                lines[n * deep + q : n * deep + q + 1, 0:size] = got[
                    n : n + 1, q * LANES : q * LANES + size
                ]
        for m in range(per):

            def line(n, to):
                at = lines[n * deep : (n + 1) * deep, :]
                return pltpu.roll(at, (LANES + to - rows * m) % LANES, 1)

            values = (
                jnp.where(lane < HALF, line(0, 0), line(1, HALF)),
                line(2, 0),
                jnp.where(lane < HALF, line(3, 0), line(4, HALF)),
            )
            for n, value in enumerate(values):
                for q in range(0, deep, 8):
                    at = pl.ds(n * wide.shape[0] // 3 + 3 * (per * q + m) + comp, 8, stride=3 * per)
                    wide[at, :] = value[q : q + 8]
        def fill(k, _):
            value = block[k].astype(F32)
            for tile in range(tiles):
                for r in range(0, rows, 8):
                    at = pl.ds((tile * rows + r) * stride + 3 * k + comp, 8, stride=stride)
                    table[at, :] = value[r : r + 8, tile * LANES : (tile + 1) * LANES]
            return 0

        lax.fori_loop(0, depth, fill, 0, unroll=5)
    for n, out in enumerate((first, last, seam)):
        at = n * wide.shape[0] // 3
        out[...] = wide[at : at + planes, :]


def gather_kernel(stride, table, index, got, listed):
    lane = iota((8, LANES), 1)
    count = index[3, 0]
    slots = index.shape[1]

    def block_of(b, n):
        acc = [jnp.zeros((8, LANES), F32)] * 4
        for p in range(LANES):
            s = b * LANES + p
            row = index[0, s]
            shift = index[1, s]
            low = pltpu.roll(table[pl.ds(row, 8), :], shift, 1)
            high = pltpu.roll(table[pl.ds(row + stride, 8), :], shift, 1)
            here = lane == p
            beside = lane == ((p + 1) % LANES)
            acc = [
                jnp.where(here, low, acc[0]),
                jnp.where(beside, low, acc[1]),
                jnp.where(here, high, acc[2]),
                jnp.where(beside, high, acc[3]),
            ]
            listed[n] = s
            n = n + index[2, s]
        got[0, b] = acc[0]
        got[1, b] = pltpu.roll(acc[1], LANES - 1, 1)
        got[2, b] = acc[2]
        got[3, b] = pltpu.roll(acc[3], LANES - 1, 1)
        return n

    full = (count + LANES - 1) >> SHIFT
    listed[slots + 8] = lax.fori_loop(0, full, block_of, I32(0))
    listed[slots + 9] = count


def group_places(rows, cols, planes, g, top, raw, lines):
    i, j, k = (raw[n : n + 1].astype(I32) for n in (9, 10, 11))
    y0 = (j, j, jnp.full_like(j, -1), jnp.full_like(j, rows))[g]
    x0 = (jnp.full_like(i, -1), jnp.full_like(i, cols), i, i)[g]
    e, signs = places(rows, cols, planes, jnp.full_like(i, g + 1), top, y0, x0, k)
    half = lines.shape[0] // 2
    for q in range(4):
        row = 4 * (g % (half // 4)) + q
        lines[row : row + 1, :] = e[q] >> SHIFT
        lines[half + row : half + row + 1, :] = (iota((1, LANES), 1) - e[q]) & (LANES - 1)
    return signs


def group_corner(table, lines, row):
    lane = iota((8, LANES), 1)
    half = lines.shape[0] // 2
    total = jnp.zeros((8, LANES), F32)
    for t in range(CAP):
        value = pltpu.roll(table[pl.ds(lines[row, t], 8), :], lines[half + row, t], 1)
        total = jnp.where(lane == t, value, total)
    return total


def lat_records(planes, top, even_lat, q1r, q2r):
    at = slice(2 * planes, 2 * planes + REC)
    inside = iota((REC, LANES), 1) < HALF
    srec = jnp.where(even_lat, q2r[at, :], q1r[at, :]).astype(F32)
    nrec = jnp.where(even_lat, q1r[at, :], q2r[at, :]).astype(F32)
    nrec = jnp.where(top, nrec, pltpu.roll(nrec, HALF, 1))
    return jnp.where(inside, srec, 0.0), jnp.where(inside, nrec, 0.0)


def put_rows(table, planes, even_lat, q1, q2, q1r, q2r, first, last, seam):
    def put(n, value):
        table[n * planes : (n + 1) * planes, :] = value

    def pick(a, b, at):
        at = slice(at, at + planes)
        return jnp.where(even_lat, a[at, :], b[at, :]).astype(F32)

    for t in range(2):
        put(t, pick(q2, q1, t * planes))
        put(2 + t, pick(q1, q2, t * planes))
        put(4 + t, pick(q1r, q2r, t * planes))
        put(8 + t, pick(q2r, q1r, t * planes))
    put(10, first[...])
    put(11, last[...])
    put(14, seam[...])


def side_kernel(first, last, lonrec, q1r, q2r, p1, p2):
    planes = first.shape[0]
    even_lat = lax.rem(lax.axis_index("lat"), 2) == 0
    odd_lon = lax.rem(lax.axis_index("lon"), 2)
    lane = iota((planes, LANES), 1)

    def strip(north, n):
        a = q1r[n * planes : (n + 1) * planes, :].astype(F32)
        b = q2r[n * planes : (n + 1) * planes, :].astype(F32)
        return jnp.where(even_lat == north, a, b)

    north0, north1, south0 = strip(True, 0), strip(True, 1), strip(False, 0)
    second0 = []
    at = slice(2 * planes + REC, 2 * planes + REC + 8)
    lines = jnp.where(even_lat, q1r[at, :], q2r[at, :]).astype(F32)
    for n in range(2):
        line = jnp.broadcast_to(lines[6 + n : 7 + n], (LANES, LANES))
        second0.append(jnp.transpose(line))
    second0 = jnp.concatenate([second0[0], second0[1][0 : planes - LANES]], axis=0)
    west = first[...]
    west = jnp.where(lane == 32, pltpu.roll(north0, 32, 1), west)
    west = jnp.where(lane == 33, second0, west)
    west = jnp.where(lane == 34, pltpu.roll(south0, 34, 1), west)
    west = jnp.where(lane == 35, pltpu.roll(north1, 36, 1), west)
    west = jnp.where(lane == 96, pltpu.roll(north0, 95, 1), west).astype(BF16)
    east = last[...]
    east = jnp.where(lane == 32, pltpu.roll(north1, 33, 1), east)
    east = jnp.where((lane == 33) | (lane == 34), pltpu.roll(north0, 33, 1), east).astype(BF16)
    p1[0:planes, :] = jnp.where(odd_lon == 1, west, east)
    p2[0:planes, :] = jnp.where(odd_lon == 1, east, west)
    p1[planes:, :] = lonrec[...]
    p2[planes:, :] = lonrec[...]


def places(rows, cols, planes, group, top, y0, x0, k):
    fold = (group == 4) & top
    found, signs = [], []

    def flat(strip, at):
        return strip * (planes * LANES) + at

    def row_at(strip, at):
        return flat(strip + (at >> SHIFT), at & (LANES - 1))

    for dj, di in ((0, 0), (0, 1), (1, 0), (1, 1)):
        y = y0 + dj
        x = x0 + di
        inner = row_at(jnp.where(y == 0, 0, 2), x)
        inner = jnp.where(x == LANES - 1, flat(14, y), inner)
        inner = jnp.where(x == LANES, flat(14, HALF + y), inner)
        inner = jnp.where(x == 0, flat(10, y), inner)
        inner = jnp.where(x == cols - 1, flat(11, y), inner)
        inner = jnp.where(x > cols, flat(12, HALF + y), inner)
        inner = jnp.where(x == cols, flat(12, y), inner)
        inner = jnp.where(x < 0, flat(13, y), inner)
        north = jnp.where(
            x < 0,
            flat(13, 32),
            jnp.where(x == cols, flat(12, 32), jnp.where(x > cols, flat(12, 96), row_at(4, x))),
        )
        u = cols - x
        folded = jnp.where(
            u < 0,
            flat(12, 35),
            jnp.where(u == cols, flat(13, 33), jnp.where(u > cols, flat(13, 34), row_at(4, u))),
        )
        second = flat(12, 33)
        south = jnp.where(x == cols, flat(12, 34), row_at(8, x))
        where = jnp.where(
            y < 0,
            south,
            jnp.where(y > rows, second, jnp.where(y == rows, jnp.where(top, folded, north), inner)),
        )
        if dj == 0:
            across = jnp.where(x == cols, flat(13, 33), row_at(4, x))
            signs.append(jnp.ones(x0.shape, F32))
        else:
            across = jnp.where(u == cols, flat(12, rows - 1), row_at(2, u))
            signs.append(jnp.where(top & (fold | (y == rows)), -1.0, 1.0))
        found.append(jnp.where(fold, across, where) + 3 * LANES * k)
    return found, signs


def final_kernel(
    rows, cols, lat_size,
    stay, got, listed_any, first, last, seam, q1, q2, q1r, q2r, p1r, p2r,
    new_off, new_cel, new_count,
    table, values_of, packed, idxv, idxs, idxt, idxlv, idxl, listed, isem,
):
    planes = first.shape[0]
    slots = stay.shape[1]
    lat = lax.axis_index("lat")
    even_lat = lax.rem(lat, 2) == 0
    even_lon = lax.rem(lax.axis_index("lon"), 2) == 0
    top = lat == lat_size - 1
    both = 2 * planes

    def pick(flag, a, b, at, size):
        return jnp.where(flag, a[at : at + size, :], b[at : at + size, :]).astype(F32)

    slot = iota((1, slots), 1)
    copy_list = pltpu.make_async_copy(listed_any, listed, isem.at[2])
    copy_list.start()
    blocks = [slice(b * LANES, (b + 1) * LANES) for b in range(slots // LANES)]
    packed[...] = jnp.zeros(packed.shape, F32)
    for n in range(3):
        for b, at in enumerate(blocks):
            packed[8 * n + b : 8 * n + b + 1, :] = stay[3 + n : 4 + n, at]
    here = [packed[8 * n : 8 * n + 8, :].astype(I32) for n in range(3)]
    e, stay_signs = places(
        rows, cols, planes, jnp.zeros((8, LANES), I32), top, here[1], here[0], here[2]
    )
    for q in range(4):
        idxlv[8 * q : 8 * q + 8, :] = e[q]
    copy_listed = pltpu.make_async_copy(idxlv, idxl, isem.at[3])
    copy_listed.start()
    inside = iota((REC, LANES), 1) < HALF
    wrec = pick(even_lon, p2r, p1r, planes, REC)
    erec = pltpu.roll(pick(even_lon, p1r, p2r, planes, REC), HALF, 1)
    srec, nrec = lat_records(planes, top, even_lat, q1r, q2r)
    carried = pick(even_lat, q1r, q2r, both + REC, 8)
    groups = [None] * 4
    copies = []
    for pair, raws in ((1, (srec, nrec)), (0, (wrec, erec))):
        lines = idxv.at[pair]
        for n, raw in enumerate(raws):
            g = 2 * pair + n
            raw = jnp.where(inside, raw, 0.0)
            signs = group_places(rows, cols, planes, g, top, raw, lines)
            groups[g] = (raw, jnp.sum(raw[12:13]).astype(I32), signs)
        copies.append(pltpu.make_async_copy(lines, (idxs, idxt)[pair], isem.at[pair]))
        copies[-1].start()
    values_of[...] = got[...]
    put_rows(table, planes, even_lat, q1, q2, q1r, q2r, first, last, seam)
    table[12 * planes : 13 * planes, :] = pick(even_lon, p1r, p2r, 0, planes)
    table[13 * planes : 14 * planes, :] = pick(even_lon, p2r, p1r, 0, planes)
    lane = iota((8, LANES), 1)
    copy_listed.wait()
    copy_list.wait()
    found = listed[slots + 8]

    def patch_listed(n, _):
        chosen = [listed[jnp.minimum(n * UNROLL + u, found - 1)] for u in range(UNROLL)]
        values = []
        for s in chosen:
            for q in range(4):
                e = idxl[8 * q + (s >> SHIFT), s & (LANES - 1)]
                line = table[pl.ds(e >> SHIFT, 8), :]
                values.append(pltpu.roll(line, (s - e) & (LANES - 1), 1))
        for s in chosen:
            mask = lane == (s & (LANES - 1))
            for q in range(4):
                pltpu.store(values_of.at[q, s >> SHIFT], values.pop(0), mask=mask)
        return 0

    lax.fori_loop(0, lax.div(found + (UNROLL - 1), UNROLL), patch_listed, 0)
    corners = [None] * 4
    for pair in (1, 0):
        copies[1 - pair].wait()
        for n in range(2):
            lines = (idxs, idxt)[pair]
            corners[2 * pair + n] = [group_corner(table, lines, 4 * n + q) for q in range(4)]
    base = listed[slots + 9]
    own = slot < base
    corner = [
        [values_of[n, b] * stay_signs[n][b : b + 1] for n in range(4)] for b in range(len(blocks))
    ]
    kept = [[jnp.where(own[:, at], stay[n : n + 1, at], 0.0) for n in range(6)] for at in blocks]
    group = jnp.zeros((1, slots), I32)
    for g, (raw, count, signs) in enumerate(groups):
        acc = []
        for q in range(4):
            total = corners[g][q]
            if g == 3 and q > 1:
                sent = carried if q == 2 else pltpu.roll(carried, HALF, 1)
                beyond = top if q == 2 else top | (raw[9:10].astype(I32) == cols - 1)
                total = jnp.where(beyond, total, sent)
            acc.append(pltpu.roll(total * signs[q], base & (LANES - 1), 1))
        moved = pltpu.roll(raw, base & (LANES - 1), 1)
        values = decode(moved) + [moved[9:10], moved[10:11], moved[11:12]]
        mine = (slot >= base) & (slot < base + count)
        for b, at in enumerate(blocks):
            kept[b] = [jnp.where(mine[:, at], x, y) for x, y in zip(values, kept[b])]
            corner[b] = [jnp.where(mine[:, at], x, y) for x, y in zip(acc, corner[b])]
        group = jnp.where(mine, g + 1, group)
        base = base + count
    fold = (group == 4) & top
    new_count[0, 0] = base
    below = iota((8, LANES), 0) < 3
    for b, at in enumerate(blocks):
        position = jnp.concatenate(kept[b][:3], axis=0)

        def rounded(value):
            return value.astype(BF16).astype(F32)

        def sample(pos):
            pa, pb, pc = pos[0:1], pos[1:2], pos[2:3]
            near = jnp.where(below, rounded((1.0 - pb) * (1.0 - pc)), rounded((1.0 - pb) * pc))
            far = jnp.where(below, rounded(pb * (1.0 - pc)), rounded(pb * pc))
            left = near * corner[b][0] + far * corner[b][2]
            right = near * corner[b][1] + far * corner[b][3]
            mixed = (1.0 - pa) * left + pa * right
            return mixed[0:3] + mixed[3:6]

        middle = position + 0.5 * sample(position)
        moved = position + sample(middle)
        na, nb, nc = moved[0:1], moved[1:2], moved[2:3]
        g = group[:, at]
        f = fold[:, at]
        filled = slot[:, at] < base
        na = jnp.where(g == 1, na - 1.0, jnp.where(g == 2, na + 1.0, jnp.where(f, 1.0 - na, na)))
        north_b = jnp.where(f, 2.0 - nb, nb + 1.0)
        nb = jnp.where(g == 3, nb - 1.0, jnp.where(g == 4, north_b, nb))
        new_off[0, :, at] = jnp.where(filled, na, 0.0)
        new_off[1, :, at] = jnp.where(filled, nb, 0.0)
        new_off[2, :, at] = jnp.where(filled, nc, 0.0)
        ci, cj, ck = (row.astype(I32) for row in kept[b][3:])
        ci = jnp.where(
            g == 1, 0, jnp.where(g == 2, cols - 1, jnp.where(f, cols - 1 - ci, ci))
        )
        cj = jnp.where(g == 3, 0, jnp.where(g == 4, rows - 1, cj))
        new_cel[0, :, at] = jnp.where(filled, ci, 0)
        new_cel[1, :, at] = jnp.where(filled, cj, 0)
        new_cel[2, :, at] = jnp.where(filled, ck, 0)


def route(lon_size, lat_size, partner):
    pairs = []
    for p in range(lon_size):
        for r in range(lat_size):
            other = partner(p, r)
            if other is not None:
                pairs.append((p * lat_size + r, other[0] * lat_size + other[1]))
    return pairs


def shards(velocity, offsets, cells, counts, moves):
    depth, rows, cols = velocity.shape[1:]
    slots = offsets.shape[2]
    lon_size, lat_size = lax.axis_size("lon"), lax.axis_size("lat")
    axes = ("lon", "lat")
    planes = up8(3 * depth)
    stride = odd_stride(depth)
    tiles = cols // LANES
    high = tiles * planes + REC + 8

    def send(x, partner):
        return lax.ppermute(x, axes, route(lon_size, lat_size, partner))

    def array(shape, dtype):
        return jax.ShapeDtypeStruct(shape, dtype)

    q1, q2, lonrec, record, rank0, total, zonal = pl.pallas_call(
        pack_kernel,
        out_shape=(
            array((high, LANES), BF16),
            array((high, LANES), BF16),
            array((REC, LANES), BF16),
            array((REC, reach_of(slots)), BF16),
            array((1, reach_of(slots)), I32),
            array((1, LANES), I32),
            array((depth, rows, cols), BF16),
        ),
        in_specs=[HBM, HBM, HBM, SMEM, HBM],
        out_specs=(VMEM,) * 7,
        scratch_shapes=[
            pltpu.VMEM((3, depth, 8, cols), BF16),
            pltpu.VMEM((3, 1, slots), F32),
            pltpu.VMEM((3, 1, slots), I32),
            pltpu.VMEM((1, slots), I32),
            pltpu.VMEM((tiles * 8 * stride, LANES), F32),
            pltpu.VMEM((REC, reach_of(slots)), F32),
            pltpu.VMEM((3 * up8(depth) + 8, LANES), F32),
            pltpu.SemaphoreType.DMA((2, 3)),
            pltpu.SemaphoreType.DMA((4,)),
        ],
        compiler_params=room(14),
        name="pack",
    )(*(pltpu.with_memory_space_constraint(x, pltpu.HBM) for x in (velocity, offsets, cells)), counts, pltpu.with_memory_space_constraint(moves, pltpu.HBM))

    q1r = send(q1, lambda p, r: (p, r ^ 1))

    def second(p, r):
        if r == lat_size - 1:
            return (lon_size - 1 - p, r)
        return None if r == 0 else (p, ((r + 1) ^ 1) - 1)

    q2r = send(q2, second)
    per = LANES // rows
    deep = up8(-(-depth // per))
    strips = tiles * rows + 1
    first, last, seam, table, stay, index = pl.pallas_call(
        table_kernel,
        out_shape=(
            array((planes, LANES), F32),
            array((planes, LANES), F32),
            array((planes, LANES), F32),
            array((strips * stride + 8, LANES), F32),
            array((8, slots), F32),
            array((4, slots), I32),
        ),
        in_specs=[HBM] + [VMEM] * 4,
        out_specs=(VMEM,) * 6,
        scratch_shapes=[
            pltpu.VMEM((2, depth, rows, cols), BF16),
            pltpu.VMEM((5 * deep, LANES), F32),
            pltpu.VMEM((9 * up8(per * deep), LANES), F32),
            pltpu.SemaphoreType.DMA((2,)),
        ],
        compiler_params=room(20),
        cost_estimate=pl.CostEstimate(flops=10**9, bytes_accessed=2 * velocity.size, transcendentals=0),
        name="table",
    )(pltpu.with_memory_space_constraint(velocity, pltpu.HBM), zonal, record, rank0, total)
    p1, p2 = pl.pallas_call(
        side_kernel,
        out_shape=(array((planes + REC, LANES), BF16), array((planes + REC, LANES), BF16)),
        in_specs=[VMEM] * 5,
        out_specs=(VMEM, VMEM),
        compiler_params=room(5),
        name="sides",
    )(first, last, lonrec, q1r, q2r)
    p2r = send(p2, lambda p, r: ((((p + 1) ^ 1) - 1) % lon_size, r))
    p1r = send(p1, lambda p, r: (p ^ 1, r))
    got, listed = pl.pallas_call(
        functools.partial(gather_kernel, stride),
        out_shape=(array((4, slots // LANES, 8, LANES), F32), array((slots + LANES,), I32)),
        in_specs=[VMEM, SMEM],
        out_specs=(VMEM, SMEM),
        compiler_params=room(10),
        cost_estimate=pl.CostEstimate(flops=10**9, bytes_accessed=2 * velocity.size, transcendentals=0),
        name="gather",
    )(table, index)
    return pl.pallas_call(
        functools.partial(final_kernel, rows, cols, lat_size),
        out_shape=(
            array((3, 1, slots), F32),
            array((3, 1, slots), I32),
            array((1, 1), I32),
        ),
        in_specs=[VMEM, VMEM, pl.BlockSpec(memory_space=pl.ANY)] + [VMEM] * 9,
        out_specs=(VMEM, VMEM, SMEM),
        scratch_shapes=[
            pltpu.VMEM((15 * planes + 8, LANES), F32),
            pltpu.VMEM((4, slots // LANES, 8, LANES), F32),
            pltpu.VMEM((24, LANES), F32),
            pltpu.VMEM((2, 16, LANES), I32),
            pltpu.SMEM((16, LANES), I32),
            pltpu.SMEM((16, LANES), I32),
            pltpu.VMEM((32, LANES), I32),
            pltpu.SMEM((32, LANES), I32),
            pltpu.SMEM((slots + LANES,), I32),
            pltpu.SemaphoreType.DMA((4,)),
        ],
        compiler_params=room(8),
        name="final",
    )(stay, got, listed, first, last, seam, q1, q2, q1r, q2r, p1r, p2r)


def solution(mesh):
    placed = (
        P(None, None, "lat", "lon"),
        P(None, "lat", "lon"),
        P(None, "lat", "lon"),
        P("lat", "lon"),
        P("lat", "lon"),
    )
    return jax.shard_map(
        shards,
        mesh=mesh,
        in_specs=placed,
        out_specs=(P(None, "lat", "lon"), P(None, "lat", "lon"), P("lat", "lon")),
        check_vma=False,
    )
```

```python
import functools

import jax
import jax.numpy as jnp
from jax import lax
from jax.experimental import pallas as pl
from jax.experimental.pallas import tpu as pltpu
from jax.sharding import PartitionSpec as P

CAP = 48
LANES = 128
HALF = 64
REC = 16
UNROLL = 8
SHIFT = 7
F32, BF16, I32 = jnp.float32, jnp.bfloat16, jnp.int32
VMEM = pl.BlockSpec(memory_space=pltpu.VMEM)
SMEM = pl.BlockSpec(memory_space=pltpu.SMEM)
HBM = pl.BlockSpec(memory_space=pltpu.HBM)


def room(mib):
    return pltpu.CompilerParams(vmem_limit_bytes=mib << 20)


def up8(n):
    return (n + 7) // 8 * 8


def reach_of(slots):
    return -(-(slots - 4 * CAP) // LANES) * LANES


def odd_stride(depth):
    lines = 3 * depth + 8
    return lines + 1 - lines % 2


def iota(shape, dim):
    return lax.broadcasted_iota(I32, shape, dim)


def nt(a, b):
    return lax.dot_general(a, b, (((1,), (1,)), ((), ())), preferred_element_type=F32)


def pieces(value):
    high = value.astype(BF16).astype(F32)
    rest = value - high
    middle = rest.astype(BF16).astype(F32)
    return [high, middle, rest - middle]


def decode(x):
    return [x[0:1] + x[1:2] + x[2:3], x[3:4] + x[4:5] + x[5:6], x[6:7] + x[7:8] + x[8:9]]


def pack_kernel(
    vel, off, cel, counts, moves, q1, q2, lonrec, record, rank0, total, zonal,
    edge, offv, celv, movev, strips, recs, picked, sems, small,
):
    depth, rows = vel.shape[1], vel.shape[2]
    tiles = vel.shape[3] // LANES
    slots = reach_of(off.shape[2])
    stride = odd_stride(depth)
    planes = up8(3 * depth)
    inputs = [
        pltpu.make_async_copy(source, target, small.at[n])
        for n, (source, target) in enumerate(((off, offv), (cel, celv), (moves, movev)))
    ]
    for copy in inputs:
        copy.start()
    copies = []
    for comp in range(3):
        copies.append(
            pltpu.make_async_copy(vel.at[comp, :, pl.ds(0, 2), :], edge.at[comp, :, pl.ds(0, 2), :], sems.at[0, comp])
        )
        copies.append(
            pltpu.make_async_copy(
                vel.at[comp, :, pl.ds(rows - 2, 2), :],
                edge.at[comp, :, pl.ds(6, 2), :],
                sems.at[1, comp],
            )
        )
    for copy in copies:
        copy.start()
    whole = pltpu.make_async_copy(vel.at[0], zonal, small.at[3])
    whole.start()
    for copy in inputs:
        copy.wait()
    live = counts[0, 0]
    rows_of = []
    for d in range(3):
        rows_of += pieces(offv[d][:, 0:slots])
    for d in range(3):
        rows_of.append(celv[d][:, 0:slots].astype(F32))
    rows_of.append(jnp.ones((1, slots), F32))
    for n, row in enumerate(rows_of):
        recs[n : n + 1, :] = row
    recs[len(rows_of) :, :] = jnp.zeros((REC - len(rows_of), slots), F32)
    packed = recs[...].astype(BF16)
    record[...] = packed
    chosen = (movev[:, 0:slots] == iota((8, slots), 0)) & (iota((8, slots), 1) < live)
    ones = chosen.astype(F32)
    scan_of = jnp.where(
        (iota((LANES, 2 * LANES), 0) < iota((LANES, 2 * LANES), 1))
        | (iota((LANES, 2 * LANES), 1) >= LANES),
        1.0,
        0.0,
    ).astype(BF16)
    carry = jnp.zeros((8, LANES), F32)
    ranks = []
    for block in range(slots // LANES):
        piece = ones[:, block * LANES : (block + 1) * LANES].astype(BF16)
        scanned = jnp.dot(piece, scan_of, preferred_element_type=F32)
        ranks.append(scanned[:, :LANES] + carry)
        carry = carry + scanned[:, LANES:]
    rank = jnp.where(chosen, jnp.concatenate(ranks, axis=1), -1.0).astype(I32)
    rank0[...] = rank[0:1]
    target = iota((HALF, slots), 0)
    placing = [
        jnp.where(rank[g : g + 1] == target, 1.0, 0.0).astype(BF16) for g in range(1, 5)
    ]
    lonrec[...] = nt(packed, jnp.concatenate(placing[:2], axis=0)).astype(BF16)
    latrec = nt(packed, jnp.concatenate(placing[2:], axis=0))
    total[...] = carry[0:1, :].astype(I32)
    for comp in range(3):
        copies[2 * comp].wait()
        copies[2 * comp + 1].wait()

        def spread(k, _):
            value = edge[comp, k].astype(F32)
            for tile in range(tiles):
                first = tile * 8 * stride + 3 * k + comp
                strips[pl.ds(first, 8, stride=stride), :] = value[
                    :, tile * LANES : (tile + 1) * LANES
                ]
            return 0

        lax.fori_loop(0, depth, spread, 0, unroll=15)
    seconds = [
        strips[pl.ds((tile * 8 + 1) * stride, planes), :].astype(BF16) for tile in range(tiles)
    ]
    lane = iota((1, LANES), 1)
    south_i, south_k = latrec[9:10], latrec[11:12]
    column = jnp.where(lane < HALF, pltpu.roll(south_i, HALF, 1), south_i + 1.0).astype(I32)
    level = jnp.where(lane < HALF, pltpu.roll(south_k, HALF, 1), south_k).astype(I32)
    at_column = jnp.zeros((planes, LANES), F32)
    for tile in range(tiles):
        where = jnp.where(iota((LANES, LANES), 0) + tile * LANES == column, 1.0, 0.0).astype(BF16)
        at_column = at_column + jnp.dot(seconds[tile], where, preferred_element_type=F32)
    picked[0:planes, :] = at_column
    deep = up8(depth)
    carried = []
    for step in range(2):
        for comp in range(3):
            lines = picked[pl.ds(comp, deep, stride=3), :]
            there = iota((deep, LANES), 0) == level + step
            carried.append(jnp.sum(jnp.where(there, lines, 0.0), axis=0, keepdims=True))
    for n, row in enumerate(carried):
        recs[n : n + 1, 0:LANES] = row
    corner = nt(jnp.where(iota((REC, LANES), 1) == 0, 1.0, 0.0).astype(BF16), seconds[0])
    recs[6:7, 0:LANES] = corner[0:1, 0:LANES]
    recs[7:8, 0:LANES] = jnp.zeros((1, LANES), F32)
    recs[7:8, 0 : planes - LANES] = corner[0:1, LANES:planes]
    odd = lax.rem(lax.axis_index("lat"), 2)
    for n, out in enumerate((q1, q2)):
        upper = odd if n == 0 else 1 - odd
        for tile in range(tiles):
            last = (tile * 8 + 7) * stride
            first = jnp.where(upper == 1, tile * 8 * stride, last)
            out[tile * planes : (tile + 1) * planes, :] = strips[pl.ds(first, planes), :].astype(BF16)
        at = tiles * planes
        out[at : at + REC, :] = latrec.astype(BF16)
        out[at + REC :, :] = recs[0:8, 0:LANES].astype(BF16)
    whole.wait()


def table_kernel(
    source, zonal, record, rank0, total, first, last, seam, table, stay, index, vel, lines, wide, sems
):
    depth, rows, cols = vel.shape[1:]
    copies = [
        pltpu.make_async_copy(source.at[comp + 1], vel.at[comp], sems.at[comp]) for comp in range(2)
    ]
    for copy in copies:
        copy.start()
    reach, slots = record.shape[1], stay.shape[1]
    tiles = cols // LANES
    planes = up8(3 * depth)
    stride = odd_stride(depth)
    r, c = iota((REC, cols), 0), iota((REC, cols), 1)
    pick = (r == c) & (r < 2)
    pick = pick | ((r == 2) & (c == cols - 1)) | ((r == c - LANES + 4) & (r >= 3) & (r < 5))
    select = jnp.where(pick, 1.0, 0.0).astype(BF16)
    per = LANES // rows
    chunks = -(-depth // per)
    deep = up8(chunks)
    lane = iota((deep, LANES), 1)
    target = iota((LANES, reach), 0)
    stay[:, reach:] = jnp.zeros((8, slots - reach), F32)
    packed = record[...]
    rank = rank0[...]
    for block in range(reach // LANES):
        where = jnp.where(rank - block * LANES == target, 1.0, 0.0).astype(BF16)
        out = nt(packed, where)
        lanes = slice(block * LANES, (block + 1) * LANES)
        for d, row in enumerate(decode(out)):
            stay[d : d + 1, lanes] = row
        stay[3:6, lanes] = out[9:12]
        stay[6:8, lanes] = out[12:14]
    i, j, k = (stay[n : n + 1, :].astype(I32) for n in (3, 4, 5))
    slot = iota((1, slots), 1)
    index[0:1, :] = ((i >> SHIFT) * rows + j) * stride + 3 * k
    index[1:2, :] = (slot - i) & (LANES - 1)
    odd_one = (((i & (LANES - 1)) == LANES - 1) | (j == rows - 1)) & (slot < jnp.tile(total[...], (1, slots // LANES)))
    index[2:3, :] = odd_one.astype(I32)
    index[3:4, :] = jnp.tile(total[...], (1, slots // LANES))
    for comp in range(3):
        if comp > 0:
            copies[comp - 1].wait()
        block = vel.at[comp - 1] if comp > 0 else zonal
        got = nt(select, block[...].reshape(depth * rows, cols))
        for n in range(5):
            for q in range(chunks):
                size = min(LANES, depth * rows - q * LANES)
                lines[n * deep + q : n * deep + q + 1, 0:size] = got[
                    n : n + 1, q * LANES : q * LANES + size
                ]
        for m in range(per):

            def line(n, to):
                at = lines[n * deep : (n + 1) * deep, :]
                return pltpu.roll(at, (LANES + to - rows * m) % LANES, 1)

            values = (
                jnp.where(lane < HALF, line(0, 0), line(1, HALF)),
                line(2, 0),
                jnp.where(lane < HALF, line(3, 0), line(4, HALF)),
            )
            for n, value in enumerate(values):
                for q in range(0, deep, 8):
                    at = pl.ds(n * wide.shape[0] // 3 + 3 * (per * q + m) + comp, 8, stride=3 * per)
                    wide[at, :] = value[q : q + 8]
        def fill(k, _):
            value = block[k].astype(F32)
            for tile in range(tiles):
                for r in range(0, rows, 8):
                    at = pl.ds((tile * rows + r) * stride + 3 * k + comp, 8, stride=stride)
                    table[at, :] = value[r : r + 8, tile * LANES : (tile + 1) * LANES]
            return 0

        lax.fori_loop(0, depth, fill, 0, unroll=15)
    for n, out in enumerate((first, last, seam)):
        at = n * wide.shape[0] // 3
        out[...] = wide[at : at + planes, :]


def gather_kernel(stride, table, index, got, listed):
    lane = iota((8, LANES), 1)
    count = index[3, 0]
    slots = index.shape[1]

    def block_of(b, n):
        acc = [jnp.zeros((8, LANES), F32)] * 4
        for p in range(LANES):
            s = b * LANES + p
            row = index[0, s]
            shift = index[1, s]
            low = pltpu.roll(table[pl.ds(row, 8), :], shift, 1)
            high = pltpu.roll(table[pl.ds(row + stride, 8), :], shift, 1)
            here = lane == p
            beside = lane == ((p + 1) % LANES)
            acc = [
                jnp.where(here, low, acc[0]),
                jnp.where(beside, low, acc[1]),
                jnp.where(here, high, acc[2]),
                jnp.where(beside, high, acc[3]),
            ]
            listed[n] = s
            n = n + index[2, s]
        got[0, b] = acc[0]
        got[1, b] = pltpu.roll(acc[1], LANES - 1, 1)
        got[2, b] = acc[2]
        got[3, b] = pltpu.roll(acc[3], LANES - 1, 1)
        return n

    full = (count + LANES - 1) >> SHIFT
    listed[slots + 8] = lax.fori_loop(0, full, block_of, I32(0))
    listed[slots + 9] = count


def group_places(rows, cols, planes, g, top, raw, lines):
    i, j, k = (raw[n : n + 1].astype(I32) for n in (9, 10, 11))
    y0 = (j, j, jnp.full_like(j, -1), jnp.full_like(j, rows))[g]
    x0 = (jnp.full_like(i, -1), jnp.full_like(i, cols), i, i)[g]
    e, signs = places(rows, cols, planes, jnp.full_like(i, g + 1), top, y0, x0, k)
    half = lines.shape[0] // 2
    for q in range(4):
        row = 4 * (g % (half // 4)) + q
        lines[row : row + 1, :] = e[q] >> SHIFT
        lines[half + row : half + row + 1, :] = (iota((1, LANES), 1) - e[q]) & (LANES - 1)
    return signs


def group_corner(table, lines, row):
    lane = iota((8, LANES), 1)
    half = lines.shape[0] // 2
    total = jnp.zeros((8, LANES), F32)
    for t in range(CAP):
        value = pltpu.roll(table[pl.ds(lines[row, t], 8), :], lines[half + row, t], 1)
        total = jnp.where(lane == t, value, total)
    return total


def lat_records(planes, top, even_lat, q1r, q2r):
    at = slice(2 * planes, 2 * planes + REC)
    inside = iota((REC, LANES), 1) < HALF
    srec = jnp.where(even_lat, q2r[at, :], q1r[at, :]).astype(F32)
    nrec = jnp.where(even_lat, q1r[at, :], q2r[at, :]).astype(F32)
    nrec = jnp.where(top, nrec, pltpu.roll(nrec, HALF, 1))
    return jnp.where(inside, srec, 0.0), jnp.where(inside, nrec, 0.0)


def put_rows(table, planes, even_lat, q1, q2, q1r, q2r, first, last, seam):
    def put(n, value):
        table[n * planes : (n + 1) * planes, :] = value

    def pick(a, b, at):
        at = slice(at, at + planes)
        return jnp.where(even_lat, a[at, :], b[at, :]).astype(F32)

    for t in range(2):
        put(t, pick(q2, q1, t * planes))
        put(2 + t, pick(q1, q2, t * planes))
        put(4 + t, pick(q1r, q2r, t * planes))
        put(8 + t, pick(q2r, q1r, t * planes))
    put(10, first[...])
    put(11, last[...])
    put(14, seam[...])


def side_kernel(first, last, lonrec, q1r, q2r, p1, p2):
    planes = first.shape[0]
    even_lat = lax.rem(lax.axis_index("lat"), 2) == 0
    odd_lon = lax.rem(lax.axis_index("lon"), 2)
    lane = iota((planes, LANES), 1)

    def strip(north, n):
        a = q1r[n * planes : (n + 1) * planes, :].astype(F32)
        b = q2r[n * planes : (n + 1) * planes, :].astype(F32)
        return jnp.where(even_lat == north, a, b)

    north0, north1, south0 = strip(True, 0), strip(True, 1), strip(False, 0)
    second0 = []
    at = slice(2 * planes + REC, 2 * planes + REC + 8)
    lines = jnp.where(even_lat, q1r[at, :], q2r[at, :]).astype(F32)
    for n in range(2):
        line = jnp.broadcast_to(lines[6 + n : 7 + n], (LANES, LANES))
        second0.append(jnp.transpose(line))
    second0 = jnp.concatenate([second0[0], second0[1][0 : planes - LANES]], axis=0)
    west = first[...]
    west = jnp.where(lane == 32, pltpu.roll(north0, 32, 1), west)
    west = jnp.where(lane == 33, second0, west)
    west = jnp.where(lane == 34, pltpu.roll(south0, 34, 1), west)
    west = jnp.where(lane == 35, pltpu.roll(north1, 36, 1), west)
    west = jnp.where(lane == 96, pltpu.roll(north0, 95, 1), west).astype(BF16)
    east = last[...]
    east = jnp.where(lane == 32, pltpu.roll(north1, 33, 1), east)
    east = jnp.where((lane == 33) | (lane == 34), pltpu.roll(north0, 33, 1), east).astype(BF16)
    p1[0:planes, :] = jnp.where(odd_lon == 1, west, east)
    p2[0:planes, :] = jnp.where(odd_lon == 1, east, west)
    p1[planes:, :] = lonrec[...]
    p2[planes:, :] = lonrec[...]


def places(rows, cols, planes, group, top, y0, x0, k):
    fold = (group == 4) & top
    found, signs = [], []

    def flat(strip, at):
        return strip * (planes * LANES) + at

    def row_at(strip, at):
        return flat(strip + (at >> SHIFT), at & (LANES - 1))

    for dj, di in ((0, 0), (0, 1), (1, 0), (1, 1)):
        y = y0 + dj
        x = x0 + di
        inner = row_at(jnp.where(y == 0, 0, 2), x)
        inner = jnp.where(x == LANES - 1, flat(14, y), inner)
        inner = jnp.where(x == LANES, flat(14, HALF + y), inner)
        inner = jnp.where(x == 0, flat(10, y), inner)
        inner = jnp.where(x == cols - 1, flat(11, y), inner)
        inner = jnp.where(x > cols, flat(12, HALF + y), inner)
        inner = jnp.where(x == cols, flat(12, y), inner)
        inner = jnp.where(x < 0, flat(13, y), inner)
        north = jnp.where(
            x < 0,
            flat(13, 32),
            jnp.where(x == cols, flat(12, 32), jnp.where(x > cols, flat(12, 96), row_at(4, x))),
        )
        u = cols - x
        folded = jnp.where(
            u < 0,
            flat(12, 35),
            jnp.where(u == cols, flat(13, 33), jnp.where(u > cols, flat(13, 34), row_at(4, u))),
        )
        second = flat(12, 33)
        south = jnp.where(x == cols, flat(12, 34), row_at(8, x))
        where = jnp.where(
            y < 0,
            south,
            jnp.where(y > rows, second, jnp.where(y == rows, jnp.where(top, folded, north), inner)),
        )
        if dj == 0:
            across = jnp.where(x == cols, flat(13, 33), row_at(4, x))
            signs.append(jnp.ones(x0.shape, F32))
        else:
            across = jnp.where(u == cols, flat(12, rows - 1), row_at(2, u))
            signs.append(jnp.where(top & (fold | (y == rows)), -1.0, 1.0))
        found.append(jnp.where(fold, across, where) + 3 * LANES * k)
    return found, signs


def final_kernel(
    rows, cols, lat_size,
    stay, got, listed_any, first, last, seam, q1, q2, q1r, q2r, p1r, p2r,
    new_off, new_cel, new_count,
    table, values_of, packed, idxv, idxs, idxt, idxlv, idxl, listed, isem,
):
    planes = first.shape[0]
    slots = stay.shape[1]
    lat = lax.axis_index("lat")
    even_lat = lax.rem(lat, 2) == 0
    even_lon = lax.rem(lax.axis_index("lon"), 2) == 0
    top = lat == lat_size - 1
    both = 2 * planes

    def pick(flag, a, b, at, size):
        return jnp.where(flag, a[at : at + size, :], b[at : at + size, :]).astype(F32)

    slot = iota((1, slots), 1)
    copy_list = pltpu.make_async_copy(listed_any, listed, isem.at[2])
    copy_list.start()
    blocks = [slice(b * LANES, (b + 1) * LANES) for b in range(slots // LANES)]
    packed[...] = jnp.zeros(packed.shape, F32)
    for n in range(3):
        for b, at in enumerate(blocks):
            packed[8 * n + b : 8 * n + b + 1, :] = stay[3 + n : 4 + n, at]
    here = [packed[8 * n : 8 * n + 8, :].astype(I32) for n in range(3)]
    e, stay_signs = places(
        rows, cols, planes, jnp.zeros((8, LANES), I32), top, here[1], here[0], here[2]
    )
    for q in range(4):
        idxlv[8 * q : 8 * q + 8, :] = e[q]
    copy_listed = pltpu.make_async_copy(idxlv, idxl, isem.at[3])
    copy_listed.start()
    inside = iota((REC, LANES), 1) < HALF
    wrec = pick(even_lon, p2r, p1r, planes, REC)
    erec = pltpu.roll(pick(even_lon, p1r, p2r, planes, REC), HALF, 1)
    srec, nrec = lat_records(planes, top, even_lat, q1r, q2r)
    carried = pick(even_lat, q1r, q2r, both + REC, 8)
    groups = [None] * 4
    copies = []
    for pair, raws in ((1, (srec, nrec)), (0, (wrec, erec))):
        lines = idxv.at[pair]
        for n, raw in enumerate(raws):
            g = 2 * pair + n
            raw = jnp.where(inside, raw, 0.0)
            signs = group_places(rows, cols, planes, g, top, raw, lines)
            groups[g] = (raw, jnp.sum(raw[12:13]).astype(I32), signs)
        copies.append(pltpu.make_async_copy(lines, (idxs, idxt)[pair], isem.at[pair]))
        copies[-1].start()
    values_of[...] = got[...]
    put_rows(table, planes, even_lat, q1, q2, q1r, q2r, first, last, seam)
    table[12 * planes : 13 * planes, :] = pick(even_lon, p1r, p2r, 0, planes)
    table[13 * planes : 14 * planes, :] = pick(even_lon, p2r, p1r, 0, planes)
    lane = iota((8, LANES), 1)
    copy_listed.wait()
    copy_list.wait()
    found = listed[slots + 8]

    def patch_listed(n, _):
        chosen = [listed[jnp.minimum(n * UNROLL + u, found - 1)] for u in range(UNROLL)]
        values = []
        for s in chosen:
            for q in range(4):
                e = idxl[8 * q + (s >> SHIFT), s & (LANES - 1)]
                line = table[pl.ds(e >> SHIFT, 8), :]
                values.append(pltpu.roll(line, (s - e) & (LANES - 1), 1))
        for s in chosen:
            mask = lane == (s & (LANES - 1))
            for q in range(4):
                pltpu.store(values_of.at[q, s >> SHIFT], values.pop(0), mask=mask)
        return 0

    lax.fori_loop(0, lax.div(found + (UNROLL - 1), UNROLL), patch_listed, 0)
    corners = [None] * 4
    for pair in (1, 0):
        copies[1 - pair].wait()
        for n in range(2):
            lines = (idxs, idxt)[pair]
            corners[2 * pair + n] = [group_corner(table, lines, 4 * n + q) for q in range(4)]
    base = listed[slots + 9]
    own = slot < base
    corner = [
        [values_of[n, b] * stay_signs[n][b : b + 1] for n in range(4)] for b in range(len(blocks))
    ]
    kept = [[jnp.where(own[:, at], stay[n : n + 1, at], 0.0) for n in range(6)] for at in blocks]
    group = jnp.zeros((1, slots), I32)
    for g, (raw, count, signs) in enumerate(groups):
        acc = []
        for q in range(4):
            total = corners[g][q]
            if g == 3 and q > 1:
                sent = carried if q == 2 else pltpu.roll(carried, HALF, 1)
                beyond = top if q == 2 else top | (raw[9:10].astype(I32) == cols - 1)
                total = jnp.where(beyond, total, sent)
            acc.append(pltpu.roll(total * signs[q], base & (LANES - 1), 1))
        moved = pltpu.roll(raw, base & (LANES - 1), 1)
        values = decode(moved) + [moved[9:10], moved[10:11], moved[11:12]]
        mine = (slot >= base) & (slot < base + count)
        for b, at in enumerate(blocks):
            kept[b] = [jnp.where(mine[:, at], x, y) for x, y in zip(values, kept[b])]
            corner[b] = [jnp.where(mine[:, at], x, y) for x, y in zip(acc, corner[b])]
        group = jnp.where(mine, g + 1, group)
        base = base + count
    fold = (group == 4) & top
    new_count[0, 0] = base
    below = iota((8, LANES), 0) < 3
    for b, at in enumerate(blocks):
        position = jnp.concatenate(kept[b][:3], axis=0)

        def rounded(value):
            return value.astype(BF16).astype(F32)

        def sample(pos):
            pa, pb, pc = pos[0:1], pos[1:2], pos[2:3]
            near = jnp.where(below, rounded((1.0 - pb) * (1.0 - pc)), rounded((1.0 - pb) * pc))
            far = jnp.where(below, rounded(pb * (1.0 - pc)), rounded(pb * pc))
            left = near * corner[b][0] + far * corner[b][2]
            right = near * corner[b][1] + far * corner[b][3]
            mixed = (1.0 - pa) * left + pa * right
            return mixed[0:3] + mixed[3:6]

        middle = position + 0.5 * sample(position)
        moved = position + sample(middle)
        na, nb, nc = moved[0:1], moved[1:2], moved[2:3]
        g = group[:, at]
        f = fold[:, at]
        filled = slot[:, at] < base
        na = jnp.where(g == 1, na - 1.0, jnp.where(g == 2, na + 1.0, jnp.where(f, 1.0 - na, na)))
        north_b = jnp.where(f, 2.0 - nb, nb + 1.0)
        nb = jnp.where(g == 3, nb - 1.0, jnp.where(g == 4, north_b, nb))
        new_off[0, :, at] = jnp.where(filled, na, 0.0)
        new_off[1, :, at] = jnp.where(filled, nb, 0.0)
        new_off[2, :, at] = jnp.where(filled, nc, 0.0)
        ci, cj, ck = (row.astype(I32) for row in kept[b][3:])
        ci = jnp.where(
            g == 1, 0, jnp.where(g == 2, cols - 1, jnp.where(f, cols - 1 - ci, ci))
        )
        cj = jnp.where(g == 3, 0, jnp.where(g == 4, rows - 1, cj))
        new_cel[0, :, at] = jnp.where(filled, ci, 0)
        new_cel[1, :, at] = jnp.where(filled, cj, 0)
        new_cel[2, :, at] = jnp.where(filled, ck, 0)


def route(lon_size, lat_size, partner):
    pairs = []
    for p in range(lon_size):
        for r in range(lat_size):
            other = partner(p, r)
            if other is not None:
                pairs.append((p * lat_size + r, other[0] * lat_size + other[1]))
    return pairs


def shards(velocity, offsets, cells, counts, moves):
    depth, rows, cols = velocity.shape[1:]
    slots = offsets.shape[2]
    lon_size, lat_size = lax.axis_size("lon"), lax.axis_size("lat")
    axes = ("lon", "lat")
    planes = up8(3 * depth)
    stride = odd_stride(depth)
    tiles = cols // LANES
    high = tiles * planes + REC + 8

    def send(x, partner):
        return lax.ppermute(x, axes, route(lon_size, lat_size, partner))

    def array(shape, dtype):
        return jax.ShapeDtypeStruct(shape, dtype)

    q1, q2, lonrec, record, rank0, total, zonal = pl.pallas_call(
        pack_kernel,
        out_shape=(
            array((high, LANES), BF16),
            array((high, LANES), BF16),
            array((REC, LANES), BF16),
            array((REC, reach_of(slots)), BF16),
            array((1, reach_of(slots)), I32),
            array((1, LANES), I32),
            array((depth, rows, cols), BF16),
        ),
        in_specs=[HBM, HBM, HBM, SMEM, HBM],
        out_specs=(VMEM,) * 7,
        scratch_shapes=[
            pltpu.VMEM((3, depth, 8, cols), BF16),
            pltpu.VMEM((3, 1, slots), F32),
            pltpu.VMEM((3, 1, slots), I32),
            pltpu.VMEM((1, slots), I32),
            pltpu.VMEM((tiles * 8 * stride, LANES), F32),
            pltpu.VMEM((REC, reach_of(slots)), F32),
            pltpu.VMEM((3 * up8(depth) + 8, LANES), F32),
            pltpu.SemaphoreType.DMA((2, 3)),
            pltpu.SemaphoreType.DMA((4,)),
        ],
        compiler_params=room(14),
        name="pack",
    )(*(pltpu.with_memory_space_constraint(x, pltpu.HBM) for x in (velocity, offsets, cells)), counts, pltpu.with_memory_space_constraint(moves, pltpu.HBM))

    q1r = send(q1, lambda p, r: (p, r ^ 1))

    def second(p, r):
        if r == lat_size - 1:
            return (lon_size - 1 - p, r)
        return None if r == 0 else (p, ((r + 1) ^ 1) - 1)

    q2r = send(q2, second)
    per = LANES // rows
    deep = up8(-(-depth // per))
    strips = tiles * rows + 1
    first, last, seam, table, stay, index = pl.pallas_call(
        table_kernel,
        out_shape=(
            array((planes, LANES), F32),
            array((planes, LANES), F32),
            array((planes, LANES), F32),
            array((strips * stride + 8, LANES), F32),
            array((8, slots), F32),
            array((4, slots), I32),
        ),
        in_specs=[HBM] + [VMEM] * 4,
        out_specs=(VMEM,) * 6,
        scratch_shapes=[
            pltpu.VMEM((2, depth, rows, cols), BF16),
            pltpu.VMEM((5 * deep, LANES), F32),
            pltpu.VMEM((9 * up8(per * deep), LANES), F32),
            pltpu.SemaphoreType.DMA((2,)),
        ],
        compiler_params=room(20),
        cost_estimate=pl.CostEstimate(flops=10**9, bytes_accessed=2 * velocity.size, transcendentals=0),
        name="table",
    )(pltpu.with_memory_space_constraint(velocity, pltpu.HBM), zonal, record, rank0, total)
    p1, p2 = pl.pallas_call(
        side_kernel,
        out_shape=(array((planes + REC, LANES), BF16), array((planes + REC, LANES), BF16)),
        in_specs=[VMEM] * 5,
        out_specs=(VMEM, VMEM),
        compiler_params=room(5),
        name="sides",
    )(first, last, lonrec, q1r, q2r)
    p2r = send(p2, lambda p, r: ((((p + 1) ^ 1) - 1) % lon_size, r))
    p1r = send(p1, lambda p, r: (p ^ 1, r))
    got, listed = pl.pallas_call(
        functools.partial(gather_kernel, stride),
        out_shape=(array((4, slots // LANES, 8, LANES), F32), array((slots + LANES,), I32)),
        in_specs=[VMEM, SMEM],
        out_specs=(VMEM, SMEM),
        compiler_params=room(10),
        cost_estimate=pl.CostEstimate(flops=10**9, bytes_accessed=2 * velocity.size, transcendentals=0),
        name="gather",
    )(table, index)
    return pl.pallas_call(
        functools.partial(final_kernel, rows, cols, lat_size),
        out_shape=(
            array((3, 1, slots), F32),
            array((3, 1, slots), I32),
            array((1, 1), I32),
        ),
        in_specs=[VMEM, VMEM, pl.BlockSpec(memory_space=pl.ANY)] + [VMEM] * 9,
        out_specs=(VMEM, VMEM, SMEM),
        scratch_shapes=[
            pltpu.VMEM((15 * planes + 8, LANES), F32),
            pltpu.VMEM((4, slots // LANES, 8, LANES), F32),
            pltpu.VMEM((24, LANES), F32),
            pltpu.VMEM((2, 16, LANES), I32),
            pltpu.SMEM((16, LANES), I32),
            pltpu.SMEM((16, LANES), I32),
            pltpu.VMEM((32, LANES), I32),
            pltpu.SMEM((32, LANES), I32),
            pltpu.SMEM((slots + LANES,), I32),
            pltpu.SemaphoreType.DMA((4,)),
        ],
        compiler_params=room(8),
        name="final",
    )(stay, got, listed, first, last, seam, q1, q2, q1r, q2r, p1r, p2r)


def solution(mesh):
    placed = (
        P(None, None, "lat", "lon"),
        P(None, "lat", "lon"),
        P(None, "lat", "lon"),
        P("lat", "lon"),
        P("lat", "lon"),
    )
    return jax.shard_map(
        shards,
        mesh=mesh,
        in_specs=placed,
        out_specs=(P(None, "lat", "lon"), P(None, "lat", "lon"), P("lat", "lon")),
        check_vma=False,
    )
```
